128 devices in a mesh: dp: 2 (over core), context: 2 (over y_lo), expert: 32 (over z, x, y_hi).
Axes of the slice: x: 4, y: 4 (y_hi: 2, y_lo: 2; y = y_hi * 2 + y_lo), z: 4, core: 2. Of those that a mesh axis runs over, the one named last changes fastest.
Arguments:
- tokens: bfloat16 [64, 256, 2048], P(('dp', 'expert'), 'context'), may hold values from -16 to 16
- grad_output: bfloat16 [64, 256, 2048], P(('dp', 'expert'), 'context'), may hold values from -6 to 6
- routes: int32 [64, 256, 8], P(('dp', 'expert'), 'context'), may hold values from 0 to 31, all different within a row; in each aligned block of 128 rows (0 to 127, 128 to 255, ..., all dimensions but the last counted through in order) at most 40 rows name the same one
- positions: int32 [64, 256], P(('dp', 'expert')), may hold values from 0 to 255, as said below
- attn_gain: float32 [2048], replicated, may hold values from 0.5 to 1.5
- q_gain: float32 [2048], replicated, may hold values from 0.1 to 1.9
- k_gain: float32 [2048], replicated, may hold values from 0.1 to 1.9
- ffn_gain: float32 [2048], replicated, may hold values from 0.5 to 1.5
- qkv_weight: bfloat16 [3, 2048, 2048], P(None, ('dp', 'context', 'expert')), may hold values from -0.125 to 0.125
- out_weight: bfloat16 [2048, 2048], P(('dp', 'context', 'expert')), may hold values from -1 to 1
- router_weight: bfloat16 [2048, 32], replicated, may hold values from -0.25 to 0.25
- expert_in: bfloat16 [32, 2, 2048, 1024], P('expert'), may hold values from -0.125 to 0.125
- expert_out: bfloat16 [32, 1024, 2048], P('expert'), may hold values from -0.75 to 0.75
Outputs:
- output: float32 [64, 256, 2048], P(('dp', 'expert'), 'context')
- grad_tokens: float32 [64, 256, 2048], P(('dp', 'expert'), 'context')
- grad_attn_gain: float32 [2048], replicated
- grad_q_gain: float32 [2048], replicated
- grad_k_gain: float32 [2048], replicated
- grad_ffn_gain: float32 [2048], replicated
- grad_router: float32 [2048, 32], replicated
- grad_qkv_weight: float32 [3, 2048, 2048], P(None, ('dp', 'context', 'expert'))
- grad_out_weight: float32 [2048, 2048], P(('dp', 'context', 'expert'))
- grad_expert_in: float32 [32, 2, 2048, 1024], P('expert', None, ('dp', 'context'))
- grad_expert_out: float32 [32, 1024, 2048], P('expert', None, ('dp', 'context'))
The draws below stay inside these ranges and needn't reach their ends.
Inputs may be any that keep to these rules, and one draw needn't show every extreme that they name: `routes`: each row names 8 different experts; the rows of one device name one expert at most 40 times. Each row is a permutation of the positions of one sequence.
All inputs are finite; a program needn't handle non-finite values.
Results may differ from the reference program's by a relative error of at most 0.019.
Values may be sent and summed in bfloat16 or wider, within the bound.
No kernel may reach another device: no remote copies, remote signals or barrier semaphores. Data moves between devices by JAX's collectives and lax.ppermute only.
A program may use at most 448 MiB of HBM per device.

```python
import math
import jax
import jax.numpy as jnp
import numpy as np
from jax import lax

D = 2048
HEADS = 16
HDIM = 128
HIDDEN_SIZE = 1024
TOP = 8
TOK_DEV = 128
EXPERTS = 32
SEQ = 256
SEQS = 64
CAP = 40
N_CONTEXT = 2


def draw_positions(key, part):
    base = jnp.tile(jnp.arange(SEQ, dtype=jnp.int32)[None, :], (SEQS, 1))
    return jax.random.permutation(key, base, axis=1, independent=True)


def spiked(array, rng, source, target, parts, factor):
    def block_of(position):
        return (jnp.arange(array.shape[position]) // (array.shape[position] // parts)).reshape((-1,) + (1,) * (array.ndim - 1 - position))

    near = jax.random.permutation(rng, parts)[block_of(target)]
    far = (block_of(target) + parts // 2) % parts
    return jnp.where((block_of(source) == near) | (block_of(source) == far), factor * array, array)


def level_of(stream_key, shape, shards, least, high):
    level, own = 1.0, jax.random.fold_in(stream_key, 6)
    for dim, blocks in shards:
        heights = jnp.exp(jax.random.uniform(jax.random.fold_in(own, dim), (blocks,), jnp.float32, least / len(shards), high / len(shards)))
        level = level * jnp.repeat(heights, shape[dim] // blocks).reshape([-1 if axis == dim else 1 for axis in range(len(shape))])
    return level


def assign_block(key, own, number, rows, count, top, limit, slope):
    sequence = jax.random.permutation(key, count)
    heavy_load, ordinary = shares(count, rows * top, limit, slope, True), shares(count, rows * top, limit, slope, False)
    places = jnp.arange(count)

    def named(lengths, rotation):
        used = int((lengths > 0).sum())
        fixed = max(1, used // 4)
        shifted = fixed + (places - fixed + rotation * (used - fixed)) % max(1, count - fixed)
        return jnp.zeros((count,), jnp.int32).at[sequence[jnp.where(places < fixed, places, shifted)]].set(jnp.asarray(lengths, jnp.int32))

    lengths = jnp.where(number % 4 == 0, named(heavy_load, number // 4), named(ordinary, number - number // 4 - 1))
    mixed = jax.random.permutation(jax.random.fold_in(own, 3), count)
    source_of, taker = mixed[0:count // 2 * 2:2], mixed[1:count // 2 * 2:2]
    slack = jnp.minimum(lengths[source_of] - 1, limit - lengths[taker]) // 2
    slack = jnp.where((source_of == sequence[0]) | (taker == sequence[0]) | (lengths[taker] == 0), 0, jnp.maximum(slack, 0))
    shifted = jax.random.randint(jax.random.fold_in(own, 4), (count // 2,), 0, 1 << 20) % (slack + 1)
    lengths = lengths.at[source_of].add(-shifted).at[taker].add(shifted)
    items = jnp.searchsorted(jnp.cumsum(lengths), jnp.arange(rows * top), side="right").astype(jnp.int32)
    table = items.reshape(top, rows).T
    table = table[jax.random.permutation(jax.random.fold_in(own, 1), rows)]
    rotation = jax.random.randint(jax.random.fold_in(own, 2), (rows, 1), 0, top)
    return jnp.take_along_axis(table, (jnp.arange(top)[None, :] + rotation) % top, axis=1)


def shares(amount, total, reach, skew, full):
    portions = [(1 << 20) // math.isqrt(grade ** skew) + 1 for grade in range(1, amount + 1)]
    largest = reach if full else min(reach, max(-(-total // amount), total * portions[0] // sum(portions)))
    least = 1 if total - largest >= amount - 1 else 0
    counts, spare = [largest] + [least] * (amount - 1), total - largest - least * (amount - 1)
    while spare > 0:
        movable = [i for i in range(1, amount) if counts[i] < largest] or [i for i in range(1, amount) if counts[i] < reach]
        pool, left = sum([portions[i] for i in movable]), spare
        for i in movable:
            addition = min(reach - counts[i], max(1, left * portions[i] // pool), spare)
            counts[i] = counts[i] + addition
            spare = spare - addition
    return np.array(counts)


def normal_values(own_key, extent, scale, reach, pieces=(), kind=jnp.bfloat16):
    factor_of = level_of(own_key, extent, pieces, -0.22, 0.18) if pieces else 1.0
    array = jax.random.normal(own_key, extent, jnp.float32) * scale * factor_of
    return jnp.minimum(jnp.maximum(array, -reach), reach).astype(kind)


def bell_draw_with(rng, shape, spread, bound, shards, heavy, kind=jnp.bfloat16):
    values = spread * jax.random.normal(rng, shape, jnp.float32)
    if shards:
        values = values * level_of(rng, shape, shards, -0.22, 0.18)
    return jnp.clip(spiked(values, jax.random.fold_in(rng, 3), *heavy), -bound, bound).astype(kind)


def setup_inputs(seed: int = 0) -> dict:
    streams_of = jax.random.split(jax.random.key(seed), 14)
    tokens = bell_draw_with(streams_of[0], (SEQS, SEQ, D), 1.0, 16.0, ((0, 64), (1, 2)), (0, 2, 64, 4.0))
    grad_output = normal_values(streams_of[1], (SEQS, SEQ, D), 1.0, 6.0, ((0, 64), (1, 2)))
    routes_keys = jax.random.split(jax.random.fold_in(streams_of[2], 1), SEQS * SEQ // TOK_DEV)
    routes_turns = jax.random.permutation(jax.random.fold_in(streams_of[2], 3), SEQS * SEQ // TOK_DEV)
    routes = jax.vmap(lambda own, number: assign_block(jax.random.fold_in(streams_of[2], 2), own, number, TOK_DEV, EXPERTS, TOP, CAP, 2))(routes_keys, routes_turns).reshape((SEQS, SEQ, TOP))
    positions = draw_positions(jax.random.fold_in(streams_of[13], 71), 0)
    attn_gain = jnp.clip(1.0 + 0.1 * jax.random.normal(streams_of[4], (D,), jnp.float32), 0.5, 1.5)
    q_gain = jnp.clip(1.0 + 0.18 * jax.random.normal(streams_of[5], (HEADS * HDIM,), jnp.float32), 0.1, 1.9)
    k_gain = jnp.clip(1.0 + 0.18 * jax.random.normal(streams_of[6], (HEADS * HDIM,), jnp.float32), 0.1, 1.9)
    ffn_gain = jnp.clip(1.0 + 0.1 * jax.random.normal(streams_of[7], (D,), jnp.float32), 0.5, 1.5)
    qkv_weight = normal_values(streams_of[8], (3, D, HEADS * HDIM), D ** -0.5, 0.125, ((1, 128),))
    out_weight = normal_values(streams_of[9], (D, HEADS * HDIM), (max(HEADS * HDIM // 64, 1)) ** -0.5, 1.0, ((0, 128),))
    router_weight = normal_values(streams_of[10], (D, EXPERTS), (D // 4) ** -0.5, 0.25)
    expert_in = normal_values(streams_of[11], (EXPERTS, 2, D, HIDDEN_SIZE), D ** -0.5, 0.125, ((0, 32),))
    expert_out = normal_values(streams_of[12], (EXPERTS, HIDDEN_SIZE, D), (HIDDEN_SIZE // 16) ** -0.5, 0.75, ((0, 32),))
    return {"tokens": tokens, "grad_output": grad_output, "routes": routes, "positions": positions, "attn_gain": attn_gain, "q_gain": q_gain, "k_gain": k_gain, "ffn_gain": ffn_gain, "qkv_weight": qkv_weight, "out_weight": out_weight, "router_weight": router_weight, "expert_in": expert_in, "expert_out": expert_out}


EPS = 1e-05
THETA = 10000.0

def rounded(values):
    return lax.optimization_barrier(values.astype(jnp.bfloat16))

def rope_tables(places):
    half = HDIM // 2
    freq = THETA ** (-jnp.arange(half, dtype=jnp.float32) * 2.0 / HDIM)
    angle = places.astype(jnp.float32)[:, None] * freq[None, :]
    return (jnp.cos(angle), jnp.sin(angle))

def rotate(values, cosine, sine, sign):
    half = values.shape[-1] // 2
    first = values[..., :half]
    second = values[..., half:]
    cosine = cosine[:, None, :]
    sine = sign * sine[:, None, :]
    return jnp.concatenate([first * cosine - second * sine, second * cosine + first * sine], axis=-1)

def rms_forward(values):
    factor = lax.rsqrt(lax.optimization_barrier(jnp.mean(values * values, axis=-1, keepdims=True)) + EPS)
    return (values * factor, factor)

def rms_backward(grad_out, normed, factor, gain):
    scaled = grad_out * gain
    grad_in = factor * (scaled - normed * lax.optimization_barrier(jnp.mean(scaled * normed, axis=-1, keepdims=True)))
    return (grad_in, lax.optimization_barrier(jnp.sum(grad_out * normed, axis=0)))

def slot_index(route_rows, experts, capacity):
    onehot = (route_rows[:, None] == jnp.arange(experts, dtype=jnp.int32)[None, :]).astype(jnp.int32)
    before = jnp.cumsum(onehot, axis=0) - onehot
    return route_rows * capacity + lax.optimization_barrier(jnp.sum(before * onehot, axis=1))

def reference(tokens, grad_output, routes, positions, attn_gain, q_gain, k_gain, ffn_gain, qkv_weight, out_weight, router_weight, expert_in, expert_out):
    single_precision = jnp.float32
    bf16 = jnp.bfloat16
    width = HEADS * HDIM
    scale = HDIM ** (-0.5)
    query_key_value_broad = qkv_weight.astype(single_precision)
    out_wide = out_weight.astype(single_precision)
    gate_wide = expert_in[:, 0].astype(single_precision)
    up_wide = expert_in[:, 1].astype(single_precision)
    down_wide = expert_out.astype(single_precision)

    def one_sequence(carry, items):
        x_b, dy_b, route, places = items
        x = x_b.astype(single_precision)
        normed1, factor1 = rms_forward(x)
        attention_input = rounded(normed1 * attn_gain)
        projected_output = jnp.einsum('hp,lpa->lha', attention_input.astype(single_precision), query_key_value_broad)
        q_normed, q_factor = rms_forward(projected_output[0])
        k_normed, k_factor = rms_forward(projected_output[1])
        values = rounded(projected_output[2]).reshape(SEQ, HEADS, HDIM)
        cosine, sine = rope_tables(places)
        queries = rounded(rotate((q_normed * q_gain).reshape(SEQ, HEADS, HDIM), cosine, sine, 1.0))
        keys = rounded(rotate((k_normed * k_gain).reshape(SEQ, HEADS, HDIM), cosine, sine, 1.0))
        allowed = (places[None, :] <= places[:, None])[None]
        scores = jnp.einsum('qhd,khd->hqk', queries.astype(single_precision), keys.astype(single_precision)) * scale
        scores = jnp.where(allowed, scores, -jnp.inf)
        lse = jnp.log(lax.optimization_barrier(jnp.sum(jnp.exp(scores), axis=-1, keepdims=True)))
        probs = jnp.exp(scores - lse)
        probs_b = rounded(probs)
        attended = rounded(jnp.einsum('hqk,khd->qhd', probs_b.astype(single_precision), values.astype(single_precision))).reshape(SEQ, width)
        mid = x + jnp.einsum('tq,dq->td', attended.astype(single_precision), out_wide)
        normed2, factor2 = rms_forward(mid)
        ffn_in = rounded(normed2 * ffn_gain)
        router_exp = jnp.exp(jnp.dot(ffn_in, router_weight, preferred_element_type=single_precision))
        router_probs = router_exp / lax.optimization_barrier(jnp.sum(router_exp, axis=-1, keepdims=True))
        slots = jax.vmap(lambda rows: slot_index(rows, EXPERTS, CAP))(route.reshape(N_CONTEXT, TOK_DEV * TOP))

        def dispatch(rows_by_route):
            blocks = rows_by_route.reshape(N_CONTEXT, TOK_DEV * TOP, D)
            filled = jax.vmap(lambda s, v: jnp.zeros((EXPERTS * CAP, D), bf16).at[s].set(v))(slots, blocks)
            return filled.reshape(N_CONTEXT, EXPERTS, CAP, D).transpose(1, 0, 2, 3).reshape(EXPERTS, N_CONTEXT * CAP, D)

        def collect(buffer):
            blocks = buffer.reshape(EXPERTS, N_CONTEXT, CAP, D).transpose(1, 0, 2, 3).reshape(N_CONTEXT, EXPERTS * CAP, D)
            taken = jax.vmap(lambda b, s: b[s])(blocks, slots)
            return taken.reshape(SEQ, TOP, D)
        rows = dispatch(jnp.repeat(ffn_in, TOP, axis=0)).astype(single_precision)
        gate = jnp.einsum('erd,edh->erh', rows, gate_wide)
        up = jnp.einsum('erd,edh->erh', rows, up_wide)
        sig = jax.nn.sigmoid(gate)
        hidden = rounded(gate * sig * up).astype(single_precision)
        expert_result = rounded(jnp.einsum('erh,ehd->erd', hidden, down_wide))
        route_out = collect(expert_result).astype(single_precision)
        route_weight = jnp.take_along_axis(router_probs, route, axis=1)
        output = mid + lax.optimization_barrier(jnp.sum(route_weight[:, :, None] * route_out, axis=1))
        grad = dy_b.astype(single_precision)
        route_grad_weight = lax.optimization_barrier(jnp.sum(grad[:, None, :] * route_out, axis=-1))
        route_grad = rounded(route_weight[:, :, None] * grad[:, None, :])
        grad_rows = dispatch(route_grad.reshape(SEQ * TOP, D)).astype(single_precision)
        grad_hidden = jnp.einsum('erd,ehd->erh', grad_rows, down_wide)
        grad_down = jnp.einsum('erh,erd->ehd', hidden, grad_rows)
        grad_gate = rounded(grad_hidden * up * sig * (1.0 + gate * (1.0 - sig))).astype(single_precision)
        grad_up = rounded(grad_hidden * gate * sig).astype(single_precision)
        grad_gate_w = jnp.einsum('erd,erh->edh', rows, grad_gate)
        grad_up_w = jnp.einsum('erd,erh->edh', rows, grad_up)
        route_grad_in = rounded(jnp.einsum('erh,edh->erd', grad_gate, gate_wide) + jnp.einsum('erh,edh->erd', grad_up, up_wide))
        grad_ffn_in = lax.optimization_barrier(jnp.sum(collect(route_grad_in).astype(single_precision), axis=1))
        chosen = (route[:, :, None] == jnp.arange(EXPERTS, dtype=jnp.int32)[None, None, :]).astype(single_precision)
        grad_probs = lax.optimization_barrier(jnp.sum(route_grad_weight[:, :, None] * chosen, axis=1))
        grad_logits = rounded(router_probs * (grad_probs - lax.optimization_barrier(jnp.sum(router_probs * grad_probs, axis=-1, keepdims=True))))
        grad_router = jnp.dot(ffn_in.T, grad_logits, preferred_element_type=single_precision)
        grad_ffn_in = grad_ffn_in + jnp.dot(grad_logits, router_weight.T, preferred_element_type=single_precision)
        grad_mid_norm, grad_ffn_gain = rms_backward(grad_ffn_in, normed2, factor2, ffn_gain)
        grad_mid = grad + grad_mid_norm
        grad_mid_b = rounded(grad_mid)
        grad_out_w = jnp.dot(grad_mid_b.T, attended, preferred_element_type=single_precision)
        grad_att = rounded(jnp.dot(grad_mid_b, out_weight, preferred_element_type=single_precision)).astype(single_precision).reshape(SEQ, HEADS, HDIM)
        delta = lax.optimization_barrier(jnp.sum(grad_att * attended.astype(single_precision).reshape(SEQ, HEADS, HDIM), axis=-1))
        grad_values = jnp.einsum('hqk,qhd->khd', probs_b.astype(single_precision), grad_att)
        grad_p = jnp.einsum('qhd,khd->hqk', grad_att, values.astype(single_precision))
        grad_scores = rounded(probs * (grad_p - delta.T[:, :, None])).astype(single_precision)
        grad_queries = jnp.einsum('hqk,khd->qhd', grad_scores, keys.astype(single_precision)) * scale
        grad_keys = jnp.einsum('hqk,qhd->khd', grad_scores, queries.astype(single_precision)) * scale
        grad_qn = rotate(grad_queries, cosine, sine, -1.0).reshape(SEQ, width)
        grad_kn = rotate(grad_keys, cosine, sine, -1.0).reshape(SEQ, width)
        grad_q_raw, grad_q_gain = rms_backward(grad_qn, q_normed, q_factor, q_gain)
        grad_k_raw, grad_k_gain = rms_backward(grad_kn, k_normed, k_factor, k_gain)
        projected_gradient = rounded(jnp.stack([grad_q_raw, grad_k_raw, grad_values.reshape(SEQ, width)])).astype(single_precision)
        query_key_value_gradient = jnp.einsum('gu,sgx->sux', attention_input.astype(single_precision), projected_gradient)
        attention_input_gradient = jnp.einsum('yaz,ygz->ag', projected_gradient, query_key_value_broad)
        grad_x_norm, grad_attn_gain = rms_backward(attention_input_gradient, normed1, factor1, attn_gain)
        grad_tokens = grad_mid + grad_x_norm
        terms = (grad_attn_gain, grad_q_gain, grad_k_gain, grad_ffn_gain, grad_router, query_key_value_gradient, grad_out_w, jnp.stack([grad_gate_w, grad_up_w], axis=1), grad_down)
        carry = tuple((c + t for c, t in zip(carry, terms)))
        return (carry, (output, grad_tokens))
    init = (jnp.zeros((D,), single_precision), jnp.zeros((width,), single_precision), jnp.zeros((width,), single_precision), jnp.zeros((D,), single_precision), jnp.zeros((D, EXPERTS), single_precision), jnp.zeros((3, D, width), single_precision), jnp.zeros((D, width), single_precision), jnp.zeros((EXPERTS, 2, D, HIDDEN_SIZE), single_precision), jnp.zeros((EXPERTS, HIDDEN_SIZE, D), single_precision))
    carry, (outputs, grad_tokens) = lax.scan(one_sequence, init, (tokens, grad_output, routes, positions))
    return (outputs, grad_tokens, carry[0], carry[1], carry[2], carry[3], carry[4], carry[5], carry[6], carry[7], carry[8])
```

```python
import jax
import jax.numpy as jnp
from jax import lax
from jax.sharding import PartitionSpec as P

HDIM = 128


EPS = 1e-05
THETA = 10000.0


def rope_tables(places, head_dim):
    half = head_dim // 2
    freq = THETA ** (-jnp.arange(half, dtype=jnp.float32) * 2.0 / head_dim)
    angle = places.astype(jnp.float32)[:, None] * freq[None, :]
    return (jnp.cos(angle), jnp.sin(angle))


def rotate(values, cosine, sine, sign):
    half = values.shape[-1] // 2
    first = values[..., :half]
    second = values[..., half:]
    cosine = cosine[:, None, :]
    sine = sign * sine[:, None, :]
    return jnp.concatenate(
        [first * cosine - second * sine, second * cosine + first * sine], axis=-1
    )


def rms_forward(values):
    factor = lax.rsqrt(jnp.mean(values * values, axis=-1, keepdims=True) + EPS)
    return (values * factor, factor)


def rms_backward(grad_out, normed, factor, gain):
    scaled = grad_out * gain
    grad_in = factor * (scaled - normed * jnp.mean(scaled * normed, axis=-1, keepdims=True))
    return (grad_in, jnp.sum(grad_out * normed, axis=0))


def slot_index(route_rows, experts, capacity):
    onehot = (route_rows[:, None] == jnp.arange(experts, dtype=jnp.int32)[None, :]).astype(
        jnp.int32
    )
    before = jnp.cumsum(onehot, axis=0) - onehot
    return route_rows * capacity + jnp.sum(before * onehot, axis=1)


def expert_major(received, local_experts, capacity):
    sources, _, width = received.shape
    return (
        received.reshape(sources, local_experts, capacity, width)
        .transpose(1, 0, 2, 3)
        .reshape(local_experts, sources * capacity, width)
    )


def source_major(results, sources, capacity):
    local_experts, _, width = results.shape
    return (
        results.reshape(local_experts, sources, capacity, width)
        .transpose(1, 0, 2, 3)
        .reshape(sources, local_experts * capacity, width)
    )


def body(
    tokens,
    grad_output,
    routes,
    positions,
    attn_gain,
    q_gain,
    k_gain,
    ffn_gain,
    qkv_weight,
    out_weight,
    router_weight,
    expert_in,
    expert_out,
):
    single_precision = jnp.float32
    bf16 = jnp.bfloat16
    seq_tok = tokens.shape[1]
    width = tokens.shape[2]
    top = routes.shape[2]
    heads_width = out_weight.shape[1]
    head_dim = HDIM
    heads = heads_width // head_dim
    local_experts = expert_in.shape[0]
    experts = router_weight.shape[1]
    sources = lax.axis_size("expert")
    capacity = min(seq_tok, seq_tok * top * 5 // (4 * experts))
    scale = head_dim ** (-0.5)
    x = tokens[0].astype(single_precision)
    normed1, factor1 = rms_forward(x)
    attention_input = (normed1 * attn_gain).astype(bf16)
    all_axes = ("dp", "context", "expert")
    weights_full = lax.all_gather(
        jnp.concatenate([qkv_weight, out_weight[None]], axis=0), all_axes, axis=1, tiled=True
    )
    query_key_value_complete = weights_full[:3]
    out_full = weights_full[3]
    projected_output = jnp.einsum(
        "hp,lpa->lha",
        attention_input,
        query_key_value_complete,
        preferred_element_type=single_precision,
    )
    q_normed, q_factor = rms_forward(projected_output[0])
    k_normed, k_factor = rms_forward(projected_output[1])
    values = projected_output[2].astype(bf16)
    all_places = positions[0]
    own_places = lax.dynamic_slice_in_dim(all_places, lax.axis_index("context") * seq_tok, seq_tok)
    cosine, sine = rope_tables(own_places, head_dim)
    queries = rotate(
        (q_normed * q_gain).reshape(seq_tok, heads, head_dim), cosine, sine, 1.0
    ).astype(bf16)
    own_keys = rotate(
        (k_normed * k_gain).reshape(seq_tok, heads, head_dim), cosine, sine, 1.0
    ).astype(bf16)
    keys, vals = (
        lax.all_gather(own_keys.reshape(seq_tok, heads_width), "context", axis=0, tiled=True),
        lax.all_gather(values, "context", axis=0, tiled=True),
    )
    seq_len = keys.shape[0]
    keys3 = keys.reshape(seq_len, heads, head_dim)
    vals3 = vals.reshape(seq_len, heads, head_dim)
    allowed = (all_places[None, :] <= own_places[:, None])[None]

    def masked_scores():
        scores = (
            jnp.einsum("qhd,khd->hqk", queries, keys3, preferred_element_type=single_precision)
            * scale
        )
        return jnp.where(allowed, scores, -jnp.inf)

    scores = masked_scores()
    lse = jnp.log(jnp.sum(jnp.exp(scores), axis=-1, keepdims=True))
    probs_b = jnp.exp(scores - lse).astype(bf16)
    attended = (
        jnp.einsum("hqk,khd->qhd", probs_b, vals3, preferred_element_type=single_precision)
        .astype(bf16)
        .reshape(seq_tok, heads_width)
    )
    mid = x + jnp.einsum("tq,dq->td", attended, out_full, preferred_element_type=single_precision)
    normed2, factor2 = rms_forward(mid)
    ffn_in = (normed2 * ffn_gain).astype(bf16)
    router_exp = jnp.exp(jnp.dot(ffn_in, router_weight, preferred_element_type=single_precision))
    router_probs = router_exp / jnp.sum(router_exp, axis=-1, keepdims=True)
    own_routes = routes[0]
    slots = slot_index(own_routes.reshape(-1), experts, capacity)
    send = (
        jnp.zeros((experts * capacity, width), bf16).at[slots].set(jnp.repeat(ffn_in, top, axis=0))
    )
    received = lax.all_to_all(
        send.reshape(sources, local_experts * capacity, width),
        "expert",
        split_axis=0,
        concat_axis=0,
        tiled=True,
    )
    rows = expert_major(received, local_experts, capacity)
    gate_up = jnp.einsum("lrd,lkdh->lkrh", rows, expert_in, preferred_element_type=single_precision)
    gate = gate_up[:, 0]
    up = gate_up[:, 1]
    sig = jax.nn.sigmoid(gate)
    hidden = (gate * sig * up).astype(bf16)
    results = jnp.einsum(
        "lrh,lhd->lrd", hidden, expert_out, preferred_element_type=single_precision
    ).astype(bf16)
    back = lax.all_to_all(
        source_major(results, sources, capacity), "expert", split_axis=0, concat_axis=0, tiled=True
    )
    route_out = back.reshape(experts * capacity, width)[slots].reshape(seq_tok, top, width)
    route_weight = jnp.take_along_axis(router_probs, own_routes, axis=1)
    output = mid + jnp.sum(route_weight[:, :, None] * route_out, axis=1)
    grad = grad_output[0].astype(single_precision)
    route_grad_weight = jnp.sum(grad[:, None, :] * route_out, axis=-1)
    route_grad = (
        (route_weight[:, :, None] * grad[:, None, :]).astype(bf16).reshape(seq_tok * top, width)
    )
    grad_send = jnp.zeros((experts * capacity, width), bf16).at[slots].set(route_grad)
    grad_received = lax.all_to_all(
        grad_send.reshape(sources, local_experts * capacity, width),
        "expert",
        split_axis=0,
        concat_axis=0,
        tiled=True,
    )
    grad_rows = expert_major(grad_received, local_experts, capacity)
    grad_hidden = jnp.einsum(
        "lrd,lhd->lrh", grad_rows, expert_out, preferred_element_type=single_precision
    )
    grad_down = jnp.einsum(
        "lrh,lrd->lhd", hidden, grad_rows, preferred_element_type=single_precision
    )
    grad_gate = (grad_hidden * up * sig * (1.0 + gate * (1.0 - sig))).astype(bf16)
    grad_up = (grad_hidden * gate * sig).astype(bf16)
    grad_gate_up = jnp.stack([grad_gate, grad_up], axis=1)
    grad_gate_up_w = jnp.einsum(
        "lrd,lkrh->lkdh", rows, grad_gate_up, preferred_element_type=single_precision
    )
    grad_rows_in = jnp.einsum(
        "lkrh,lkdh->lrd", grad_gate_up, expert_in, preferred_element_type=single_precision
    ).astype(bf16)
    grad_back = lax.all_to_all(
        source_major(grad_rows_in, sources, capacity),
        "expert",
        split_axis=0,
        concat_axis=0,
        tiled=True,
    )
    grad_route_in = grad_back.reshape(experts * capacity, width)[slots].reshape(seq_tok, top, width)
    grad_ffn_in = jnp.sum(grad_route_in, axis=1, dtype=single_precision)
    chosen = (own_routes[:, :, None] == jnp.arange(experts, dtype=jnp.int32)[None, None, :]).astype(
        single_precision
    )
    grad_probs = jnp.sum(route_grad_weight[:, :, None] * chosen, axis=1)
    grad_logits = (
        router_probs * (grad_probs - jnp.sum(router_probs * grad_probs, axis=-1, keepdims=True))
    ).astype(bf16)
    grad_router = jnp.einsum(
        "td,te->de", ffn_in, grad_logits, preferred_element_type=single_precision
    )
    grad_ffn_in = grad_ffn_in + jnp.einsum(
        "te,de->td", grad_logits, router_weight, preferred_element_type=single_precision
    )
    grad_mid_norm, grad_ffn_gain = rms_backward(grad_ffn_in, normed2, factor2, ffn_gain)
    grad_mid = grad + grad_mid_norm
    grad_mid_b = grad_mid.astype(bf16)
    grad_out_w = jnp.einsum(
        "td,tq->dq", grad_mid_b, attended, preferred_element_type=single_precision
    )
    grad_att = (
        jnp.einsum("td,dq->tq", grad_mid_b, out_full, preferred_element_type=single_precision)
        .astype(bf16)
        .reshape(seq_tok, heads, head_dim)
    )
    delta = jnp.sum(
        grad_att.astype(single_precision)
        * attended.reshape(seq_tok, heads, head_dim).astype(single_precision),
        axis=-1,
    )
    probs = jnp.exp(masked_scores() - lse)
    grad_vals = jnp.einsum(
        "hqk,qhd->khd", probs.astype(bf16), grad_att, preferred_element_type=single_precision
    )
    grad_p = jnp.einsum("qhd,khd->hqk", grad_att, vals3, preferred_element_type=single_precision)
    grad_scores = (probs * (grad_p - delta.T[:, :, None])).astype(bf16)
    grad_queries = (
        jnp.einsum("hqk,khd->qhd", grad_scores, keys3, preferred_element_type=single_precision)
        * scale
    )
    grad_keys_all = (
        jnp.einsum("hqk,qhd->khd", grad_scores, queries, preferred_element_type=single_precision)
        * scale
    )
    grad_keys, grad_values = (
        lax.psum_scatter(
            grad_keys_all.reshape(seq_len, heads_width).astype(jnp.bfloat16),
            "context",
            scatter_dimension=0,
            tiled=True,
        ).astype(jnp.float32),
        lax.psum_scatter(
            grad_vals.reshape(seq_len, heads_width).astype(jnp.bfloat16),
            "context",
            scatter_dimension=0,
            tiled=True,
        ).astype(jnp.float32),
    )
    grad_qn = rotate(grad_queries, cosine, sine, -1.0).reshape(seq_tok, heads_width)
    grad_kn = rotate(grad_keys.reshape(seq_tok, heads, head_dim), cosine, sine, -1.0).reshape(
        seq_tok, heads_width
    )
    grad_q_raw, grad_q_gain = rms_backward(grad_qn, q_normed, q_factor, q_gain)
    grad_k_raw, grad_k_gain = rms_backward(grad_kn, k_normed, k_factor, k_gain)
    projected_gradient = jnp.stack([grad_q_raw, grad_k_raw, grad_values]).astype(bf16)
    query_key_value_gradient = jnp.einsum(
        "gu,sgx->sux", attention_input, projected_gradient, preferred_element_type=single_precision
    )
    attention_input_gradient = jnp.einsum(
        "yaz,ygz->ag",
        projected_gradient,
        query_key_value_complete,
        preferred_element_type=single_precision,
    )
    grad_x_norm, grad_attn_gain = rms_backward(
        attention_input_gradient, normed1, factor1, attn_gain
    )
    grad_tokens = grad_mid + grad_x_norm
    def scatter_over_copies(values):
        values = lax.psum_scatter(values.astype(bf16), "dp", scatter_dimension=1, tiled=True)
        values = lax.psum_scatter(values, "context", scatter_dimension=1, tiled=True)
        return values.astype(single_precision)

    grad_in_shard = scatter_over_copies(grad_gate_up_w[0])[None]
    grad_down_shard = scatter_over_copies(grad_down[0])[None]
    small = jnp.concatenate(
        [grad_attn_gain, grad_q_gain, grad_k_gain, grad_ffn_gain, grad_router.reshape(-1)]
    )
    small_rows = -(-small.shape[0] // width)
    pad_rows = 64
    small = jnp.pad(small, (0, pad_rows * width - small.shape[0])).reshape(pad_rows, width)
    stacked = jnp.concatenate(
        [query_key_value_gradient.reshape(3 * width, heads_width), grad_out_w, small], axis=0
    )
    summed = lax.psum(stacked, all_axes)
    shard_rows = width // lax.axis_size(all_axes)
    start = lax.axis_index(all_axes) * shard_rows
    weight_sums = summed[: 4 * width].reshape(4, width, heads_width)
    weight_shard = lax.dynamic_slice_in_dim(weight_sums, start, shard_rows, axis=1)
    grad_qkv_shard = weight_shard[:3]
    grad_out_shard = weight_shard[3]
    small_sum = summed[4 * width : 4 * width + small_rows].reshape(-1)
    sizes = [width, heads_width, heads_width, width, width * experts]
    offsets = [sum(sizes[:n]) for n in range(len(sizes))]
    totals = [small_sum[o : o + n] for o, n in zip(offsets, sizes)]
    totals[4] = totals[4].reshape(width, experts)
    return (
        output[None],
        grad_tokens[None],
        totals[0],
        totals[1],
        totals[2],
        totals[3],
        totals[4],
        grad_qkv_shard,
        grad_out_shard,
        grad_in_shard,
        grad_down_shard,
    )


def solution(mesh):
    return jax.shard_map(
        body,
        mesh=mesh,
        in_specs=(
            P(("dp", "expert"), "context", None),
            P(("dp", "expert"), "context", None),
            P(("dp", "expert"), "context", None),
            P(("dp", "expert"), None),
            P(),
            P(),
            P(),
            P(),
            P(None, ("dp", "context", "expert"), None),
            P(("dp", "context", "expert"), None),
            P(),
            P("expert", None, None, None),
            P("expert", None, None),
        ),
        out_specs=(
            P(("dp", "expert"), "context", None),
            P(("dp", "expert"), "context", None),
            P(),
            P(),
            P(),
            P(),
            P(),
            P(None, ("dp", "context", "expert"), None),
            P(("dp", "context", "expert"), None),
            P("expert", None, ("dp", "context"), None),
            P("expert", None, ("dp", "context")),
        ),
        check_vma=False,
    )
```

```python
import jax
import jax.numpy as jnp
from jax import lax
from jax.sharding import PartitionSpec as P

HDIM = 128


EPS = 1e-05
THETA = 10000.0


def rope_tables(places, head_dim):
    half = head_dim // 2
    freq = THETA ** (-jnp.arange(half, dtype=jnp.float32) * 2.0 / head_dim)
    angle = places.astype(jnp.float32)[:, None] * freq[None, :]
    return (jnp.cos(angle), jnp.sin(angle))


def rotate(values, cosine, sine, sign):
    half = values.shape[-1] // 2
    first = values[..., :half]
    second = values[..., half:]
    cosine = cosine[:, None, :]
    sine = sign * sine[:, None, :]
    return jnp.concatenate(
        [first * cosine - second * sine, second * cosine + first * sine], axis=-1
    )


def rms_forward(values):
    factor = lax.rsqrt(jnp.mean(values * values, axis=-1, keepdims=True) + EPS)
    return (values * factor, factor)


def rms_backward(grad_out, normed, factor, gain):
    scaled = grad_out * gain
    grad_in = factor * (scaled - normed * jnp.mean(scaled * normed, axis=-1, keepdims=True))
    return (grad_in, jnp.sum(grad_out * normed, axis=0))


def slot_index(route_rows, experts, capacity):
    onehot = (route_rows[:, None] == jnp.arange(experts, dtype=jnp.int32)[None, :]).astype(
        jnp.int32
    )
    count = route_rows.shape[0]
    earlier = (
        jnp.arange(count, dtype=jnp.int32)[None, :] < jnp.arange(count, dtype=jnp.int32)[:, None]
    ).astype(jnp.bfloat16)
    before = jnp.dot(earlier, onehot.astype(jnp.bfloat16), preferred_element_type=jnp.float32)
    return route_rows * capacity + jnp.sum(before.astype(jnp.int32) * onehot, axis=1)


def expert_major(received, local_experts, capacity):
    sources, _, width = received.shape
    return (
        received.reshape(sources, local_experts, capacity, width)
        .transpose(1, 0, 2, 3)
        .reshape(local_experts, sources * capacity, width)
    )


def source_major(results, sources, capacity):
    local_experts, _, width = results.shape
    return (
        results.reshape(local_experts, sources, capacity, width)
        .transpose(1, 0, 2, 3)
        .reshape(sources, local_experts * capacity, width)
    )


def body(
    tokens,
    grad_output,
    routes,
    positions,
    attn_gain,
    q_gain,
    k_gain,
    ffn_gain,
    qkv_weight,
    out_weight,
    router_weight,
    expert_in,
    expert_out,
):
    single_precision = jnp.float32
    bf16 = jnp.bfloat16
    seq_tok = tokens.shape[1]
    width = tokens.shape[2]
    top = routes.shape[2]
    heads_width = out_weight.shape[1]
    head_dim = HDIM
    heads = heads_width // head_dim
    local_experts = expert_in.shape[0]
    experts = router_weight.shape[1]
    sources = lax.axis_size("expert")
    capacity = min(seq_tok, seq_tok * top * 5 // (4 * experts))
    scale = head_dim ** (-0.5)
    x = tokens[0].astype(single_precision)
    normed1, factor1 = rms_forward(x)
    attention_input = (normed1 * attn_gain).astype(bf16)
    all_axes = ("dp", "context", "expert")
    weights_full = lax.all_gather(
        jnp.concatenate([qkv_weight.transpose(1, 0, 2), out_weight[:, None, :]], axis=1),
        all_axes,
        axis=0,
        tiled=True,
    )
    out_full = weights_full[:, 3, :]
    projected_all = jnp.dot(
        attention_input,
        weights_full.reshape(width, 4 * heads_width),
        preferred_element_type=single_precision,
    ).reshape(seq_tok, 4, heads_width)
    projected_output = projected_all[:, :3].transpose(1, 0, 2)
    q_normed, q_factor = rms_forward(projected_output[0])
    k_normed, k_factor = rms_forward(projected_output[1])
    values = projected_output[2].astype(bf16)
    all_places = positions[0]
    own_places = lax.dynamic_slice_in_dim(all_places, lax.axis_index("context") * seq_tok, seq_tok)
    cosine, sine = rope_tables(own_places, head_dim)
    queries = rotate(
        (q_normed * q_gain).reshape(seq_tok, heads, head_dim), cosine, sine, 1.0
    ).astype(bf16)
    own_keys = rotate(
        (k_normed * k_gain).reshape(seq_tok, heads, head_dim), cosine, sine, 1.0
    ).astype(bf16)
    keys, vals = (
        lax.all_gather(own_keys.reshape(seq_tok, heads_width), "context", axis=0, tiled=True),
        lax.all_gather(values, "context", axis=0, tiled=True),
    )
    seq_len = keys.shape[0]
    keys3 = keys.reshape(seq_len, heads, head_dim)
    vals3 = vals.reshape(seq_len, heads, head_dim)
    allowed = (all_places[None, :] <= own_places[:, None])[None]

    def masked_scores():
        scores = (
            jnp.einsum("qhd,khd->hqk", queries, keys3, preferred_element_type=single_precision)
            * scale
        )
        return jnp.where(allowed, scores, -jnp.inf)

    scores = masked_scores()
    lse = jnp.log(jnp.sum(jnp.exp(scores), axis=-1, keepdims=True))
    probs_b = jnp.exp(scores - lse).astype(bf16)
    attended = (
        jnp.einsum("hqk,khd->qhd", probs_b, vals3, preferred_element_type=single_precision)
        .astype(bf16)
        .reshape(seq_tok, heads_width)
    )
    mid = x + jnp.einsum("tq,dq->td", attended, out_full, preferred_element_type=single_precision)
    normed2, factor2 = rms_forward(mid)
    ffn_in = (normed2 * ffn_gain).astype(bf16)
    router_exp = jnp.exp(jnp.dot(ffn_in, router_weight, preferred_element_type=single_precision))
    router_probs = router_exp / jnp.sum(router_exp, axis=-1, keepdims=True)
    own_routes = routes[0]
    slots = slot_index(own_routes.reshape(-1), experts, capacity)
    send = (
        jnp.zeros((experts * capacity, width), bf16).at[slots].set(jnp.repeat(ffn_in, top, axis=0))
    )
    received = lax.all_to_all(
        send.reshape(sources, local_experts * capacity, width),
        "expert",
        split_axis=0,
        concat_axis=0,
        tiled=True,
    )
    rows = expert_major(received, local_experts, capacity)
    gate_up = jnp.einsum("lrd,lkdh->lkrh", rows, expert_in, preferred_element_type=single_precision)
    gate = gate_up[:, 0]
    up = gate_up[:, 1]
    sig = jax.nn.sigmoid(gate)
    hidden = (gate * sig * up).astype(bf16)
    results = jnp.einsum(
        "lrh,lhd->lrd", hidden, expert_out, preferred_element_type=single_precision
    ).astype(bf16)
    back = lax.all_to_all(
        source_major(results, sources, capacity), "expert", split_axis=0, concat_axis=0, tiled=True
    )
    route_out = back.reshape(experts * capacity, width)[slots].reshape(seq_tok, top, width)
    route_weight = jnp.take_along_axis(router_probs, own_routes, axis=1)
    output = mid + jnp.sum(route_weight[:, :, None] * route_out, axis=1)
    grad = grad_output[0].astype(single_precision)
    route_grad_weight = jnp.sum(grad[:, None, :] * route_out, axis=-1)
    route_grad = (
        (route_weight[:, :, None] * grad[:, None, :]).astype(bf16).reshape(seq_tok * top, width)
    )
    grad_send = jnp.zeros((experts * capacity, width), bf16).at[slots].set(route_grad)
    grad_received = lax.all_to_all(
        grad_send.reshape(sources, local_experts * capacity, width),
        "expert",
        split_axis=0,
        concat_axis=0,
        tiled=True,
    )
    grad_rows = expert_major(grad_received, local_experts, capacity)
    grad_hidden = jnp.einsum(
        "lrd,lhd->lrh", grad_rows, expert_out, preferred_element_type=single_precision
    )
    grad_down = jnp.einsum(
        "lrh,lrd->lhd", hidden, grad_rows, preferred_element_type=single_precision
    )
    grad_gate = (grad_hidden * up * sig * (1.0 + gate * (1.0 - sig))).astype(bf16)
    grad_up = (grad_hidden * gate * sig).astype(bf16)
    grad_gate_up = jnp.stack([grad_gate, grad_up], axis=1)
    grad_gate_up_w = jnp.einsum(
        "lrd,lkrh->lkdh", rows, grad_gate_up, preferred_element_type=single_precision
    )
    grad_rows_in = jnp.einsum(
        "lkrh,lkdh->lrd", grad_gate_up, expert_in, preferred_element_type=single_precision
    ).astype(bf16)
    grad_back = lax.all_to_all(
        source_major(grad_rows_in, sources, capacity),
        "expert",
        split_axis=0,
        concat_axis=0,
        tiled=True,
    )
    grad_route_in = grad_back.reshape(experts * capacity, width)[slots].reshape(seq_tok, top, width)
    grad_ffn_in = jnp.sum(grad_route_in, axis=1, dtype=single_precision)
    chosen = (own_routes[:, :, None] == jnp.arange(experts, dtype=jnp.int32)[None, None, :]).astype(
        single_precision
    )
    grad_probs = jnp.sum(route_grad_weight[:, :, None] * chosen, axis=1)
    grad_logits = (
        router_probs * (grad_probs - jnp.sum(router_probs * grad_probs, axis=-1, keepdims=True))
    ).astype(bf16)
    grad_router = jnp.einsum(
        "td,te->de", ffn_in, grad_logits, preferred_element_type=single_precision
    )
    grad_ffn_in = grad_ffn_in + jnp.einsum(
        "te,de->td", grad_logits, router_weight, preferred_element_type=single_precision
    )
    grad_mid_norm, grad_ffn_gain = rms_backward(grad_ffn_in, normed2, factor2, ffn_gain)
    grad_mid = grad + grad_mid_norm
    grad_mid_b = grad_mid.astype(bf16)
    grad_att = (
        jnp.einsum("td,dq->tq", grad_mid_b, out_full, preferred_element_type=single_precision)
        .astype(bf16)
        .reshape(seq_tok, heads, head_dim)
    )
    delta = jnp.sum(
        grad_att.astype(single_precision)
        * attended.reshape(seq_tok, heads, head_dim).astype(single_precision),
        axis=-1,
    )
    probs = jnp.exp(masked_scores() - lse)
    grad_vals = jnp.einsum(
        "hqk,qhd->khd", probs.astype(bf16), grad_att, preferred_element_type=single_precision
    )
    grad_p = jnp.einsum("qhd,khd->hqk", grad_att, vals3, preferred_element_type=single_precision)
    grad_scores = (probs * (grad_p - delta.T[:, :, None])).astype(bf16)
    grad_queries = (
        jnp.einsum("hqk,khd->qhd", grad_scores, keys3, preferred_element_type=single_precision)
        * scale
    )
    grad_keys_all = (
        jnp.einsum("hqk,qhd->khd", grad_scores, queries, preferred_element_type=single_precision)
        * scale
    )
    grad_keys, grad_values = (
        lax.psum_scatter(
            grad_keys_all.reshape(seq_len, heads_width).astype(jnp.bfloat16),
            "context",
            scatter_dimension=0,
            tiled=True,
        ).astype(jnp.float32),
        lax.psum_scatter(
            grad_vals.reshape(seq_len, heads_width).astype(jnp.bfloat16),
            "context",
            scatter_dimension=0,
            tiled=True,
        ).astype(jnp.float32),
    )
    grad_qn = rotate(grad_queries, cosine, sine, -1.0).reshape(seq_tok, heads_width)
    grad_kn = rotate(grad_keys.reshape(seq_tok, heads, head_dim), cosine, sine, -1.0).reshape(
        seq_tok, heads_width
    )
    grad_q_raw, grad_q_gain = rms_backward(grad_qn, q_normed, q_factor, q_gain)
    grad_k_raw, grad_k_gain = rms_backward(grad_kn, k_normed, k_factor, k_gain)
    projected_gradient = jnp.stack(
        [grad_q_raw, grad_k_raw, grad_values, jnp.zeros_like(grad_values)], axis=1
    ).astype(bf16)
    attention_input_gradient = jnp.dot(
        projected_gradient.reshape(seq_tok, 4 * heads_width),
        weights_full.reshape(width, 4 * heads_width).T,
        preferred_element_type=single_precision,
    )
    grad_x_norm, grad_attn_gain = rms_backward(
        attention_input_gradient, normed1, factor1, attn_gain
    )
    grad_tokens = grad_mid + grad_x_norm
    def scatter_over_copies(values):
        values = lax.psum_scatter(values.astype(bf16), "dp", scatter_dimension=1, tiled=True)
        values = lax.psum_scatter(values, "context", scatter_dimension=1, tiled=True)
        return values.astype(single_precision)

    grad_in_shard = scatter_over_copies(grad_gate_up_w[0])[None]
    grad_down_shard = scatter_over_copies(grad_down[0])[None]
    pad_rows = 16
    left = jnp.pad(
        jnp.stack([attention_input] * 3 + [grad_mid_b]), ((0, 0), (0, 0), (0, pad_rows))
    )
    right = jnp.concatenate(
        [projected_gradient[:, :3].transpose(1, 0, 2), attended[None]], axis=0
    )
    stacked = jnp.einsum("sta,stb->sab", left, right, preferred_element_type=single_precision)
    small = jnp.concatenate(
        [grad_attn_gain, grad_q_gain, grad_k_gain, grad_ffn_gain, grad_router.reshape(-1)]
    )
    small_rows = -(-small.shape[0] // (4 * heads_width))
    small = jnp.pad(small, (0, 4 * small_rows * heads_width - small.shape[0]))
    stacked = lax.dynamic_update_slice(
        stacked, small.reshape(4, small_rows, heads_width), (0, width, 0)
    )
    summed = lax.psum(stacked, all_axes)
    shard_rows = width // lax.axis_size(all_axes)
    start = lax.axis_index(all_axes) * shard_rows
    weight_shard = lax.dynamic_slice_in_dim(summed, start, shard_rows, axis=1)
    grad_qkv_shard = weight_shard[:3]
    grad_out_shard = weight_shard[3]
    small_sum = summed[:, width : width + small_rows].reshape(-1)
    sizes = [width, heads_width, heads_width, width, width * experts]
    offsets = [sum(sizes[:n]) for n in range(len(sizes))]
    totals = [small_sum[o : o + n] for o, n in zip(offsets, sizes)]
    totals[4] = totals[4].reshape(width, experts)
    return (
        output[None],
        grad_tokens[None],
        totals[0],
        totals[1],
        totals[2],
        totals[3],
        totals[4],
        grad_qkv_shard,
        grad_out_shard,
        grad_in_shard,
        grad_down_shard,
    )


def solution(mesh):
    return jax.shard_map(
        body,
        mesh=mesh,
        in_specs=(
            P(("dp", "expert"), "context", None),
            P(("dp", "expert"), "context", None),
            P(("dp", "expert"), "context", None),
            P(("dp", "expert"), None),
            P(),
            P(),
            P(),
            P(),
            P(None, ("dp", "context", "expert"), None),
            P(("dp", "context", "expert"), None),
            P(),
            P("expert", None, None, None),
            P("expert", None, None),
        ),
        out_specs=(
            P(("dp", "expert"), "context", None),
            P(("dp", "expert"), "context", None),
            P(),
            P(),
            P(),
            P(),
            P(),
            P(None, ("dp", "context", "expert"), None),
            P(("dp", "context", "expert"), None),
            P("expert", None, ("dp", "context"), None),
            P("expert", None, ("dp", "context")),
        ),
        check_vma=False,
    )
```

```python
import jax
import jax.numpy as jnp
from jax import lax
from jax.sharding import PartitionSpec as P

HDIM = 128


EPS = 1e-05
THETA = 10000.0


def rope_tables(places, head_dim):
    half = head_dim // 2
    freq = THETA ** (-jnp.arange(half, dtype=jnp.float32) * 2.0 / head_dim)
    angle = places.astype(jnp.float32)[:, None] * freq[None, :]
    return (jnp.cos(angle), jnp.sin(angle))


def rotate(values, cosine, sine, sign):
    half = values.shape[-1] // 2
    first = values[..., :half]
    second = values[..., half:]
    cosine = cosine[:, None, :]
    sine = sign * sine[:, None, :]
    return jnp.concatenate(
        [first * cosine - second * sine, second * cosine + first * sine], axis=-1
    )


def rms_forward(values):
    factor = lax.rsqrt(jnp.mean(values * values, axis=-1, keepdims=True) + EPS)
    return (values * factor, factor)


def rms_backward(grad_out, normed, factor, gain):
    scaled = grad_out * gain
    grad_in = factor * (scaled - normed * jnp.mean(scaled * normed, axis=-1, keepdims=True))
    return (grad_in, jnp.sum(grad_out * normed, axis=0))


def slot_index(route_rows, experts, capacity):
    onehot = (route_rows[:, None] == jnp.arange(experts, dtype=jnp.int32)[None, :]).astype(
        jnp.int32
    )
    count = route_rows.shape[0]
    earlier = (
        jnp.arange(count, dtype=jnp.int32)[None, :] < jnp.arange(count, dtype=jnp.int32)[:, None]
    ).astype(jnp.bfloat16)
    before = jnp.dot(earlier, onehot.astype(jnp.bfloat16), preferred_element_type=jnp.float32)
    return route_rows * capacity + jnp.sum(before.astype(jnp.int32) * onehot, axis=1)


def expert_major(received, local_experts, capacity):
    sources, _, width = received.shape
    return (
        received.reshape(sources, local_experts, capacity, width)
        .transpose(1, 0, 2, 3)
        .reshape(local_experts, sources * capacity, width)
    )


def source_major(results, sources, capacity):
    local_experts, _, width = results.shape
    return (
        results.reshape(local_experts, sources, capacity, width)
        .transpose(1, 0, 2, 3)
        .reshape(sources, local_experts * capacity, width)
    )


def swap_context(values):
    return lax.ppermute(values, "context", [(0, 1), (1, 0)])


def gather_context(values):
    other = swap_context(values)
    first = lax.axis_index("context") == 0
    return jnp.concatenate(
        [jnp.where(first, values, other), jnp.where(first, other, values)], axis=0
    )


def sum_context_halves(values):
    half = values.shape[0] // 2
    first = lax.axis_index("context") == 0
    own = jnp.where(first, values[:half], values[half:])
    given = jnp.where(first, values[half:], values[:half]).astype(jnp.bfloat16)
    return own + swap_context(given).astype(own.dtype)


def butterfly_sum(values, axes):
    index = lax.axis_index(axes)
    count = 1
    for name in axes:
        count *= lax.axis_size(name)
    step = 1
    while step < count:
        partner = [(i, i ^ step) for i in range(count)]
        received = lax.ppermute(values, axes, partner)
        mine_first = (index & step) == 0
        values = jnp.where(mine_first, values + received, received + values)
        step *= 2
    return values


def body(
    tokens,
    grad_output,
    routes,
    positions,
    attn_gain,
    q_gain,
    k_gain,
    ffn_gain,
    qkv_weight,
    out_weight,
    router_weight,
    expert_in,
    expert_out,
):
    single_precision = jnp.float32
    bf16 = jnp.bfloat16
    seq_tok = tokens.shape[1]
    width = tokens.shape[2]
    top = routes.shape[2]
    heads_width = out_weight.shape[1]
    head_dim = HDIM
    heads = heads_width // head_dim
    local_experts = expert_in.shape[0]
    experts = router_weight.shape[1]
    sources = lax.axis_size("expert")
    capacity = min(seq_tok, seq_tok * top * 5 // (4 * experts))
    scale = head_dim ** (-0.5)
    x = tokens[0].astype(single_precision)
    normed1, factor1 = rms_forward(x)
    attention_input = (normed1 * attn_gain).astype(bf16)
    all_axes = ("dp", "context", "expert")
    weights_full = lax.all_gather(
        jnp.concatenate([qkv_weight.transpose(1, 0, 2), out_weight[:, None, :]], axis=1),
        all_axes,
        axis=0,
        tiled=True,
    )
    out_full = weights_full[:, 3, :]
    projected_all = jnp.dot(
        attention_input,
        weights_full.reshape(width, 4 * heads_width),
        preferred_element_type=single_precision,
    ).reshape(seq_tok, 4, heads_width)
    projected_output = projected_all[:, :3].transpose(1, 0, 2)
    q_normed, q_factor = rms_forward(projected_output[0])
    k_normed, k_factor = rms_forward(projected_output[1])
    values = projected_output[2].astype(bf16)
    all_places = positions[0]
    own_places = lax.dynamic_slice_in_dim(all_places, lax.axis_index("context") * seq_tok, seq_tok)
    cosine, sine = rope_tables(own_places, head_dim)
    queries = rotate(
        (q_normed * q_gain).reshape(seq_tok, heads, head_dim), cosine, sine, 1.0
    ).astype(bf16)
    own_keys = rotate(
        (k_normed * k_gain).reshape(seq_tok, heads, head_dim), cosine, sine, 1.0
    ).astype(bf16)
    keys_vals = gather_context(
        jnp.stack([own_keys.reshape(seq_tok, heads_width), values], axis=1)
    )
    keys = keys_vals[:, 0]
    vals = keys_vals[:, 1]
    seq_len = keys.shape[0]
    keys3 = keys.reshape(seq_len, heads, head_dim)
    vals3 = vals.reshape(seq_len, heads, head_dim)
    allowed = (all_places[None, :] <= own_places[:, None])[None]

    def masked_scores():
        scores = (
            jnp.einsum("qhd,khd->hqk", queries, keys3, preferred_element_type=single_precision)
            * scale
        )
        return jnp.where(allowed, scores, -jnp.inf)

    scores = masked_scores()
    lse = jnp.log(jnp.sum(jnp.exp(scores), axis=-1, keepdims=True))
    probs_b = jnp.exp(scores - lse).astype(bf16)
    attended = (
        jnp.einsum("hqk,khd->qhd", probs_b, vals3, preferred_element_type=single_precision)
        .astype(bf16)
        .reshape(seq_tok, heads_width)
    )
    mid = x + jnp.einsum("tq,dq->td", attended, out_full, preferred_element_type=single_precision)
    normed2, factor2 = rms_forward(mid)
    ffn_in = (normed2 * ffn_gain).astype(bf16)
    router_exp = jnp.exp(jnp.dot(ffn_in, router_weight, preferred_element_type=single_precision))
    router_probs = router_exp / jnp.sum(router_exp, axis=-1, keepdims=True)
    own_routes = routes[0]
    slots = slot_index(own_routes.reshape(-1), experts, capacity)
    send = (
        jnp.zeros((experts * capacity, width), bf16).at[slots].set(jnp.repeat(ffn_in, top, axis=0))
    )
    received = lax.all_to_all(
        send.reshape(sources, local_experts * capacity, width),
        "expert",
        split_axis=0,
        concat_axis=0,
        tiled=True,
    )
    rows = expert_major(received, local_experts, capacity)
    gate_up = jnp.einsum("lrd,lkdh->lkrh", rows, expert_in, preferred_element_type=single_precision)
    gate = gate_up[:, 0]
    up = gate_up[:, 1]
    sig = jax.nn.sigmoid(gate)
    hidden = (gate * sig * up).astype(bf16)
    results = jnp.einsum(
        "lrh,lhd->lrd", hidden, expert_out, preferred_element_type=single_precision
    ).astype(bf16)
    back = lax.all_to_all(
        source_major(results, sources, capacity), "expert", split_axis=0, concat_axis=0, tiled=True
    )
    route_out = back.reshape(experts * capacity, width)[slots].reshape(seq_tok, top, width)
    route_weight = jnp.take_along_axis(router_probs, own_routes, axis=1)
    output = mid + jnp.sum(route_weight[:, :, None] * route_out, axis=1)
    grad = grad_output[0].astype(single_precision)
    route_grad_weight = jnp.sum(grad[:, None, :] * route_out, axis=-1)
    route_grad = (
        (route_weight[:, :, None] * grad[:, None, :]).astype(bf16).reshape(seq_tok * top, width)
    )
    grad_send = jnp.zeros((experts * capacity, width), bf16).at[slots].set(route_grad)
    grad_received = lax.all_to_all(
        grad_send.reshape(sources, local_experts * capacity, width),
        "expert",
        split_axis=0,
        concat_axis=0,
        tiled=True,
    )
    grad_rows = expert_major(grad_received, local_experts, capacity)
    grad_hidden = jnp.einsum(
        "lrd,lhd->lrh", grad_rows, expert_out, preferred_element_type=single_precision
    )
    grad_down = jnp.einsum(
        "lrh,lrd->lhd", hidden, grad_rows, preferred_element_type=single_precision
    )
    grad_gate = (grad_hidden * up * sig * (1.0 + gate * (1.0 - sig))).astype(bf16)
    grad_up = (grad_hidden * gate * sig).astype(bf16)
    grad_gate_up = jnp.stack([grad_gate, grad_up], axis=1)
    grad_gate_up_w = jnp.einsum(
        "lrd,lkrh->lkdh", rows, grad_gate_up, preferred_element_type=single_precision
    )
    grad_rows_in = jnp.einsum(
        "lkrh,lkdh->lrd", grad_gate_up, expert_in, preferred_element_type=single_precision
    ).astype(bf16)
    grad_back = lax.all_to_all(
        source_major(grad_rows_in, sources, capacity),
        "expert",
        split_axis=0,
        concat_axis=0,
        tiled=True,
    )
    grad_route_in = grad_back.reshape(experts * capacity, width)[slots].reshape(seq_tok, top, width)
    grad_ffn_in = jnp.sum(grad_route_in, axis=1, dtype=single_precision)
    chosen = (own_routes[:, :, None] == jnp.arange(experts, dtype=jnp.int32)[None, None, :]).astype(
        single_precision
    )
    grad_probs = jnp.sum(route_grad_weight[:, :, None] * chosen, axis=1)
    grad_logits = (
        router_probs * (grad_probs - jnp.sum(router_probs * grad_probs, axis=-1, keepdims=True))
    ).astype(bf16)
    grad_router = jnp.einsum(
        "td,te->de", ffn_in, grad_logits, preferred_element_type=single_precision
    )
    grad_ffn_in = grad_ffn_in + jnp.einsum(
        "te,de->td", grad_logits, router_weight, preferred_element_type=single_precision
    )
    grad_mid_norm, grad_ffn_gain = rms_backward(grad_ffn_in, normed2, factor2, ffn_gain)
    grad_mid = grad + grad_mid_norm
    grad_mid_b = grad_mid.astype(bf16)
    grad_att = (
        jnp.einsum("td,dq->tq", grad_mid_b, out_full, preferred_element_type=single_precision)
        .astype(bf16)
        .reshape(seq_tok, heads, head_dim)
    )
    delta = jnp.sum(
        grad_att.astype(single_precision)
        * attended.reshape(seq_tok, heads, head_dim).astype(single_precision),
        axis=-1,
    )
    probs = jnp.exp(masked_scores() - lse)
    grad_vals = jnp.einsum(
        "hqk,qhd->khd", probs.astype(bf16), grad_att, preferred_element_type=single_precision
    )
    grad_p = jnp.einsum("qhd,khd->hqk", grad_att, vals3, preferred_element_type=single_precision)
    grad_scores = (probs * (grad_p - delta.T[:, :, None])).astype(bf16)
    grad_queries = (
        jnp.einsum("hqk,khd->qhd", grad_scores, keys3, preferred_element_type=single_precision)
        * scale
    )
    grad_keys_all = (
        jnp.einsum("hqk,qhd->khd", grad_scores, queries, preferred_element_type=single_precision)
        * scale
    )
    grad_keys_values = sum_context_halves(
        jnp.stack(
            [grad_keys_all.reshape(seq_len, heads_width), grad_vals.reshape(seq_len, heads_width)],
            axis=1,
        )
    )
    grad_keys = grad_keys_values[:, 0]
    grad_values = grad_keys_values[:, 1]
    grad_qn = rotate(grad_queries, cosine, sine, -1.0).reshape(seq_tok, heads_width)
    grad_kn = rotate(grad_keys.reshape(seq_tok, heads, head_dim), cosine, sine, -1.0).reshape(
        seq_tok, heads_width
    )
    grad_q_raw, grad_q_gain = rms_backward(grad_qn, q_normed, q_factor, q_gain)
    grad_k_raw, grad_k_gain = rms_backward(grad_kn, k_normed, k_factor, k_gain)
    projected_gradient = jnp.stack(
        [grad_q_raw, grad_k_raw, grad_values, jnp.zeros_like(grad_values)], axis=1
    ).astype(bf16)
    attention_input_gradient = jnp.dot(
        projected_gradient.reshape(seq_tok, 4 * heads_width),
        weights_full.reshape(width, 4 * heads_width).T,
        preferred_element_type=single_precision,
    )
    grad_x_norm, grad_attn_gain = rms_backward(
        attention_input_gradient, normed1, factor1, attn_gain
    )
    grad_tokens = grad_mid + grad_x_norm
    def scatter_over_copies(values):
        values = lax.psum_scatter(values.astype(bf16), "dp", scatter_dimension=1, tiled=True)
        values = lax.psum_scatter(values, "context", scatter_dimension=1, tiled=True)
        return values.astype(single_precision)

    grad_in_shard = scatter_over_copies(grad_gate_up_w[0])[None]
    grad_down_shard = scatter_over_copies(grad_down[0])[None]
    left = jnp.stack([attention_input] * 3 + [grad_mid_b])
    right = jnp.concatenate(
        [projected_gradient[:, :3].transpose(1, 0, 2), attended[None]], axis=0
    )
    stacked = jnp.einsum("sta,stb->sab", left, right, preferred_element_type=single_precision)
    summed = lax.psum(stacked.astype(bf16), all_axes)
    shard_rows = width // lax.axis_size(all_axes)
    start = lax.axis_index(all_axes) * shard_rows
    weight_shard = lax.dynamic_slice_in_dim(summed, start, shard_rows, axis=1).astype(
        single_precision
    )
    grad_qkv_shard = weight_shard[:3]
    grad_out_shard = weight_shard[3]
    small_sum = butterfly_sum(
        jnp.concatenate(
            [grad_attn_gain, grad_q_gain, grad_k_gain, grad_ffn_gain, grad_router.reshape(-1)]
        ),
        all_axes,
    )
    sizes = [width, heads_width, heads_width, width, width * experts]
    offsets = [sum(sizes[:n]) for n in range(len(sizes))]
    totals = [small_sum[o : o + n] for o, n in zip(offsets, sizes)]
    totals[4] = totals[4].reshape(width, experts)
    return (
        output[None],
        grad_tokens[None],
        totals[0],
        totals[1],
        totals[2],
        totals[3],
        totals[4],
        grad_qkv_shard,
        grad_out_shard,
        grad_in_shard,
        grad_down_shard,
    )


def solution(mesh):
    return jax.shard_map(
        body,
        mesh=mesh,
        in_specs=(
            P(("dp", "expert"), "context", None),
            P(("dp", "expert"), "context", None),
            P(("dp", "expert"), "context", None),
            P(("dp", "expert"), None),
            P(),
            P(),
            P(),
            P(),
            P(None, ("dp", "context", "expert"), None),
            P(("dp", "context", "expert"), None),
            P(),
            P("expert", None, None, None),
            P("expert", None, None),
        ),
        out_specs=(
            P(("dp", "expert"), "context", None),
            P(("dp", "expert"), "context", None),
            P(),
            P(),
            P(),
            P(),
            P(),
            P(None, ("dp", "context", "expert"), None),
            P(("dp", "context", "expert"), None),
            P("expert", None, ("dp", "context"), None),
            P("expert", None, ("dp", "context")),
        ),
        check_vma=False,
    )
```

```python
import functools

import jax
import jax.numpy as jnp
from jax import lax
from jax.experimental import pallas as pl
from jax.experimental.pallas import tpu as pltpu
from jax.sharding import PartitionSpec as P

HDIM = 128


EPS = 1e-05
THETA = 10000.0


def rope_tables(places, head_dim):
    half = head_dim // 2
    freq = THETA ** (-jnp.arange(half, dtype=jnp.float32) * 2.0 / head_dim)
    angle = places.astype(jnp.float32)[:, None] * freq[None, :]
    return (jnp.cos(angle), jnp.sin(angle))


def rotate(values, cosine, sine, sign):
    half = values.shape[-1] // 2
    first = values[..., :half]
    second = values[..., half:]
    cosine = cosine[:, None, :]
    sine = sign * sine[:, None, :]
    return jnp.concatenate(
        [first * cosine - second * sine, second * cosine + first * sine], axis=-1
    )


def rms_forward(values):
    factor = lax.rsqrt(jnp.mean(values * values, axis=-1, keepdims=True) + EPS)
    return (values * factor, factor)


def rms_backward(grad_out, normed, factor, gain):
    scaled = grad_out * gain
    grad_in = factor * (scaled - normed * jnp.mean(scaled * normed, axis=-1, keepdims=True))
    return (grad_in, jnp.sum(grad_out * normed, axis=0))


def slot_index(route_rows, experts, capacity):
    onehot = (route_rows[:, None] == jnp.arange(experts, dtype=jnp.int32)[None, :]).astype(
        jnp.int32
    )
    count = route_rows.shape[0]
    earlier = (
        jnp.arange(count, dtype=jnp.int32)[None, :] < jnp.arange(count, dtype=jnp.int32)[:, None]
    ).astype(jnp.bfloat16)
    before = jnp.dot(earlier, onehot.astype(jnp.bfloat16), preferred_element_type=jnp.float32)
    return route_rows * capacity + jnp.sum(before.astype(jnp.int32) * onehot, axis=1)


def expert_major(received, local_experts, capacity):
    sources, _, width = received.shape
    return (
        received.reshape(sources, local_experts, capacity, width)
        .transpose(1, 0, 2, 3)
        .reshape(local_experts, sources * capacity, width)
    )


def source_major(results, sources, capacity):
    local_experts, _, width = results.shape
    return (
        results.reshape(local_experts, sources, capacity, width)
        .transpose(1, 0, 2, 3)
        .reshape(sources, local_experts * capacity, width)
    )


def _project_kernel(inputs_ref, weights_ref, out_ref):
    out_ref[0] = jnp.dot(inputs_ref[...], weights_ref[0], preferred_element_type=jnp.float32)


def project(inputs, weights, blocks, tile=512):
    tokens, depth = inputs.shape
    columns = weights.shape[2]
    return pl.pallas_call(
        _project_kernel,
        out_shape=jax.ShapeDtypeStruct((blocks, tokens, columns), jnp.float32),
        grid=(blocks, columns // tile),
        in_specs=[
            pl.BlockSpec((tokens, depth), lambda s, j: (0, 0)),
            pl.BlockSpec((1, depth, tile), lambda s, j: (s, 0, j)),
        ],
        out_specs=pl.BlockSpec((1, tokens, tile), lambda s, j: (s, 0, j)),
        cost_estimate=pl.CostEstimate(
            flops=2 * tokens * depth * columns * blocks,
            transcendentals=0,
            bytes_accessed=2 * depth * columns * blocks + 2 * tokens * depth
            + 4 * tokens * columns * blocks,
        ),
    )(inputs, weights)


def sum_halves(values, axis, dim):
    half = values.shape[dim] // 2
    index = lax.axis_index(axis)
    own = lax.dynamic_slice_in_dim(values, index * half, half, axis=dim)
    given = lax.dynamic_slice_in_dim(values, (1 - index) * half, half, axis=dim)
    received = lax.ppermute(given.astype(jnp.bfloat16), axis, [(0, 1), (1, 0)])
    return own + received.astype(own.dtype)


def swap_context(values):
    return lax.ppermute(values, "context", [(0, 1), (1, 0)])


def gather_context(values):
    other = swap_context(values)
    first = lax.axis_index("context") == 0
    return jnp.concatenate(
        [jnp.where(first, values, other), jnp.where(first, other, values)], axis=0
    )


def sum_context_halves(values):
    half = values.shape[0] // 2
    first = lax.axis_index("context") == 0
    own = jnp.where(first, values[:half], values[half:])
    given = jnp.where(first, values[half:], values[:half]).astype(jnp.bfloat16)
    return own + swap_context(given).astype(own.dtype)


def butterfly_sum(values, axes):
    index = lax.axis_index(axes)
    count = 1
    for name in axes:
        count *= lax.axis_size(name)
    step = 1
    while step < count:
        partner = [(i, i ^ step) for i in range(count)]
        received = lax.ppermute(values, axes, partner)
        mine_first = (index & step) == 0
        values = jnp.where(mine_first, values + received, received + values)
        step *= 2
    return values


def body(
    tokens,
    grad_output,
    routes,
    positions,
    attn_gain,
    q_gain,
    k_gain,
    ffn_gain,
    qkv_weight,
    out_weight,
    router_weight,
    expert_in,
    expert_out,
):
    single_precision = jnp.float32
    bf16 = jnp.bfloat16
    seq_tok = tokens.shape[1]
    width = tokens.shape[2]
    top = routes.shape[2]
    heads_width = out_weight.shape[1]
    head_dim = HDIM
    heads = heads_width // head_dim
    local_experts = expert_in.shape[0]
    experts = router_weight.shape[1]
    sources = lax.axis_size("expert")
    capacity = min(seq_tok, seq_tok * top * 5 // (4 * experts))
    scale = head_dim ** (-0.5)
    x = tokens[0].astype(single_precision)
    normed1, factor1 = rms_forward(x)
    attention_input = (normed1 * attn_gain).astype(bf16)
    all_axes = ("dp", "context", "expert")
    weights_full = lax.all_gather(
        jnp.concatenate([qkv_weight.transpose(1, 0, 2), out_weight[:, None, :]], axis=1),
        all_axes,
        axis=0,
        tiled=True,
    )
    out_full = weights_full[:, 3, :]
    projected_output = project(attention_input, weights_full.transpose(1, 0, 2), 3)
    q_normed, q_factor = rms_forward(projected_output[0])
    k_normed, k_factor = rms_forward(projected_output[1])
    values = projected_output[2].astype(bf16)
    all_places = positions[0]
    own_places = lax.dynamic_slice_in_dim(all_places, lax.axis_index("context") * seq_tok, seq_tok)
    cosine, sine = rope_tables(own_places, head_dim)
    queries = rotate(
        (q_normed * q_gain).reshape(seq_tok, heads, head_dim), cosine, sine, 1.0
    ).astype(bf16)
    own_keys = rotate(
        (k_normed * k_gain).reshape(seq_tok, heads, head_dim), cosine, sine, 1.0
    ).astype(bf16)
    keys_vals = gather_context(
        jnp.stack([own_keys.reshape(seq_tok, heads_width), values], axis=1)
    )
    keys = keys_vals[:, 0]
    vals = keys_vals[:, 1]
    seq_len = keys.shape[0]
    keys3 = keys.reshape(seq_len, heads, head_dim)
    vals3 = vals.reshape(seq_len, heads, head_dim)
    allowed = (all_places[None, :] <= own_places[:, None])[None]

    def masked_scores():
        scores = (
            jnp.einsum("qhd,khd->hqk", queries, keys3, preferred_element_type=single_precision)
            * scale
        )
        return jnp.where(allowed, scores, -jnp.inf)

    scores = masked_scores()
    lse = jnp.log(jnp.sum(jnp.exp(scores), axis=-1, keepdims=True))
    probs_b = jnp.exp(scores - lse).astype(bf16)
    attended = (
        jnp.einsum("hqk,khd->qhd", probs_b, vals3, preferred_element_type=single_precision)
        .astype(bf16)
        .reshape(seq_tok, heads_width)
    )
    mid = x + jnp.einsum("tq,dq->td", attended, out_full, preferred_element_type=single_precision)
    normed2, factor2 = rms_forward(mid)
    ffn_in = (normed2 * ffn_gain).astype(bf16)
    router_exp = jnp.exp(jnp.dot(ffn_in, router_weight, preferred_element_type=single_precision))
    router_probs = router_exp / jnp.sum(router_exp, axis=-1, keepdims=True)
    own_routes = routes[0]
    slots = slot_index(own_routes.reshape(-1), experts, capacity)
    send = (
        jnp.zeros((experts * capacity, width), bf16).at[slots].set(jnp.repeat(ffn_in, top, axis=0))
    )
    received = lax.all_to_all(
        send.reshape(sources, local_experts * capacity, width),
        "expert",
        split_axis=0,
        concat_axis=0,
        tiled=True,
    )
    rows = expert_major(received, local_experts, capacity)
    gate_up = jnp.einsum("lrd,lkdh->lkrh", rows, expert_in, preferred_element_type=single_precision)
    gate = gate_up[:, 0]
    up = gate_up[:, 1]
    sig = jax.nn.sigmoid(gate)
    hidden = (gate * sig * up).astype(bf16)
    results = jnp.einsum(
        "lrh,lhd->lrd", hidden, expert_out, preferred_element_type=single_precision
    ).astype(bf16)
    back = lax.all_to_all(
        source_major(results, sources, capacity), "expert", split_axis=0, concat_axis=0, tiled=True
    )
    route_out = back.reshape(experts * capacity, width)[slots].reshape(seq_tok, top, width)
    route_weight = jnp.take_along_axis(router_probs, own_routes, axis=1)
    output = mid + jnp.sum(route_weight[:, :, None] * route_out, axis=1)
    grad = grad_output[0].astype(single_precision)
    route_grad_weight = jnp.sum(grad[:, None, :] * route_out, axis=-1)
    route_grad = (
        (route_weight[:, :, None] * grad[:, None, :]).astype(bf16).reshape(seq_tok * top, width)
    )
    grad_send = jnp.zeros((experts * capacity, width), bf16).at[slots].set(route_grad)
    grad_received = lax.all_to_all(
        grad_send.reshape(sources, local_experts * capacity, width),
        "expert",
        split_axis=0,
        concat_axis=0,
        tiled=True,
    )
    grad_rows = expert_major(grad_received, local_experts, capacity)
    grad_hidden = jnp.einsum(
        "lrd,lhd->lrh", grad_rows, expert_out, preferred_element_type=single_precision
    )
    grad_down = jnp.einsum(
        "lrh,lrd->lhd", hidden, grad_rows, preferred_element_type=single_precision
    )
    grad_gate = (grad_hidden * up * sig * (1.0 + gate * (1.0 - sig))).astype(bf16)
    grad_up = (grad_hidden * gate * sig).astype(bf16)
    grad_gate_up = jnp.stack([grad_gate, grad_up], axis=1)
    grad_gate_up_w = jnp.einsum(
        "lrd,lkrh->lkdh", rows, grad_gate_up, preferred_element_type=single_precision
    )
    grad_rows_in = jnp.einsum(
        "lkrh,lkdh->lrd", grad_gate_up, expert_in, preferred_element_type=single_precision
    ).astype(bf16)
    grad_back = lax.all_to_all(
        source_major(grad_rows_in, sources, capacity),
        "expert",
        split_axis=0,
        concat_axis=0,
        tiled=True,
    )
    grad_route_in = grad_back.reshape(experts * capacity, width)[slots].reshape(seq_tok, top, width)
    grad_ffn_in = jnp.sum(grad_route_in, axis=1, dtype=single_precision)
    chosen = (own_routes[:, :, None] == jnp.arange(experts, dtype=jnp.int32)[None, None, :]).astype(
        single_precision
    )
    grad_probs = jnp.sum(route_grad_weight[:, :, None] * chosen, axis=1)
    grad_logits = (
        router_probs * (grad_probs - jnp.sum(router_probs * grad_probs, axis=-1, keepdims=True))
    ).astype(bf16)
    grad_router = jnp.einsum(
        "td,te->de", ffn_in, grad_logits, preferred_element_type=single_precision
    )
    grad_ffn_in = grad_ffn_in + jnp.einsum(
        "te,de->td", grad_logits, router_weight, preferred_element_type=single_precision
    )
    grad_mid_norm, grad_ffn_gain = rms_backward(grad_ffn_in, normed2, factor2, ffn_gain)
    grad_mid = grad + grad_mid_norm
    grad_mid_b = grad_mid.astype(bf16)
    grad_att = (
        jnp.einsum("td,dq->tq", grad_mid_b, out_full, preferred_element_type=single_precision)
        .astype(bf16)
        .reshape(seq_tok, heads, head_dim)
    )
    delta = jnp.sum(
        grad_att.astype(single_precision)
        * attended.reshape(seq_tok, heads, head_dim).astype(single_precision),
        axis=-1,
    )
    probs = jnp.exp(masked_scores() - lse)
    grad_vals = jnp.einsum(
        "hqk,qhd->khd", probs.astype(bf16), grad_att, preferred_element_type=single_precision
    )
    grad_p = jnp.einsum("qhd,khd->hqk", grad_att, vals3, preferred_element_type=single_precision)
    grad_scores = (probs * (grad_p - delta.T[:, :, None])).astype(bf16)
    grad_queries = (
        jnp.einsum("hqk,khd->qhd", grad_scores, keys3, preferred_element_type=single_precision)
        * scale
    )
    grad_keys_all = (
        jnp.einsum("hqk,qhd->khd", grad_scores, queries, preferred_element_type=single_precision)
        * scale
    )
    grad_keys_values = sum_context_halves(
        jnp.stack(
            [grad_keys_all.reshape(seq_len, heads_width), grad_vals.reshape(seq_len, heads_width)],
            axis=1,
        )
    )
    grad_keys = grad_keys_values[:, 0]
    grad_values = grad_keys_values[:, 1]
    grad_qn = rotate(grad_queries, cosine, sine, -1.0).reshape(seq_tok, heads_width)
    grad_kn = rotate(grad_keys.reshape(seq_tok, heads, head_dim), cosine, sine, -1.0).reshape(
        seq_tok, heads_width
    )
    grad_q_raw, grad_q_gain = rms_backward(grad_qn, q_normed, q_factor, q_gain)
    grad_k_raw, grad_k_gain = rms_backward(grad_kn, k_normed, k_factor, k_gain)
    projected_gradient = jnp.stack(
        [grad_q_raw, grad_k_raw, grad_values, jnp.zeros_like(grad_values)], axis=1
    ).astype(bf16)
    attention_input_gradient = jnp.dot(
        projected_gradient.reshape(seq_tok, 4 * heads_width),
        weights_full.reshape(width, 4 * heads_width).T,
        preferred_element_type=single_precision,
    )
    grad_x_norm, grad_attn_gain = rms_backward(
        attention_input_gradient, normed1, factor1, attn_gain
    )
    grad_tokens = grad_mid + grad_x_norm
    def scatter_over_copies(values):
        return sum_halves(sum_halves(values, "dp", 1), "context", 1)

    grad_in_shard = scatter_over_copies(grad_gate_up_w[0])[None]
    grad_down_shard = scatter_over_copies(grad_down[0])[None]
    left = jnp.stack([attention_input] * 3 + [grad_mid_b])
    right = jnp.concatenate(
        [projected_gradient[:, :3].transpose(1, 0, 2), attended[None]], axis=0
    )
    stacked = jnp.einsum("sta,stb->sab", left, right, preferred_element_type=single_precision)
    summed = lax.psum(stacked.astype(bf16), all_axes)
    shard_rows = width // lax.axis_size(all_axes)
    start = lax.axis_index(all_axes) * shard_rows
    weight_shard = lax.dynamic_slice_in_dim(summed, start, shard_rows, axis=1).astype(
        single_precision
    )
    grad_qkv_shard = weight_shard[:3]
    grad_out_shard = weight_shard[3]
    small_sum = butterfly_sum(
        jnp.concatenate(
            [grad_attn_gain, grad_q_gain, grad_k_gain, grad_ffn_gain, grad_router.reshape(-1)]
        ),
        all_axes,
    )
    sizes = [width, heads_width, heads_width, width, width * experts]
    offsets = [sum(sizes[:n]) for n in range(len(sizes))]
    totals = [small_sum[o : o + n] for o, n in zip(offsets, sizes)]
    totals[4] = totals[4].reshape(width, experts)
    return (
        output[None],
        grad_tokens[None],
        totals[0],
        totals[1],
        totals[2],
        totals[3],
        totals[4],
        grad_qkv_shard,
        grad_out_shard,
        grad_in_shard,
        grad_down_shard,
    )


def solution(mesh):
    return jax.shard_map(
        body,
        mesh=mesh,
        in_specs=(
            P(("dp", "expert"), "context", None),
            P(("dp", "expert"), "context", None),
            P(("dp", "expert"), "context", None),
            P(("dp", "expert"), None),
            P(),
            P(),
            P(),
            P(),
            P(None, ("dp", "context", "expert"), None),
            P(("dp", "context", "expert"), None),
            P(),
            P("expert", None, None, None),
            P("expert", None, None),
        ),
        out_specs=(
            P(("dp", "expert"), "context", None),
            P(("dp", "expert"), "context", None),
            P(),
            P(),
            P(),
            P(),
            P(),
            P(None, ("dp", "context", "expert"), None),
            P(("dp", "context", "expert"), None),
            P("expert", None, ("dp", "context"), None),
            P("expert", None, ("dp", "context")),
        ),
        check_vma=False,
    )
```

```python
import functools

import jax
import jax.numpy as jnp
from jax import lax
from jax.experimental import pallas as pl
from jax.experimental.pallas import tpu as pltpu
from jax.sharding import PartitionSpec as P

HDIM = 128


EPS = 1e-05
THETA = 10000.0


def rope_tables(places, head_dim):
    half = head_dim // 2
    freq = THETA ** (-jnp.arange(half, dtype=jnp.float32) * 2.0 / head_dim)
    angle = places.astype(jnp.float32)[:, None] * freq[None, :]
    return (jnp.cos(angle), jnp.sin(angle))


def rotate(values, cosine, sine, sign):
    half = values.shape[-1] // 2
    first = values[..., :half]
    second = values[..., half:]
    cosine = cosine[:, None, :]
    sine = sign * sine[:, None, :]
    return jnp.concatenate(
        [first * cosine - second * sine, second * cosine + first * sine], axis=-1
    )


def rms_forward(values):
    factor = lax.rsqrt(jnp.mean(values * values, axis=-1, keepdims=True) + EPS)
    return (values * factor, factor)


def rms_backward(grad_out, normed, factor, gain):
    scaled = grad_out * gain
    grad_in = factor * (scaled - normed * jnp.mean(scaled * normed, axis=-1, keepdims=True))
    return (grad_in, jnp.sum(grad_out * normed, axis=0))


def slot_index(route_rows, experts, capacity):
    onehot = (route_rows[:, None] == jnp.arange(experts, dtype=jnp.int32)[None, :]).astype(
        jnp.int32
    )
    count = route_rows.shape[0]
    earlier = (
        jnp.arange(count, dtype=jnp.int32)[None, :] < jnp.arange(count, dtype=jnp.int32)[:, None]
    ).astype(jnp.bfloat16)
    before = jnp.dot(earlier, onehot.astype(jnp.bfloat16), preferred_element_type=jnp.float32)
    return route_rows * capacity + jnp.sum(before.astype(jnp.int32) * onehot, axis=1)


def expert_major(received, local_experts, capacity):
    sources, _, width = received.shape
    return (
        received.reshape(sources, local_experts, capacity, width)
        .transpose(1, 0, 2, 3)
        .reshape(local_experts, sources * capacity, width)
    )


def source_major(results, sources, capacity):
    local_experts, _, width = results.shape
    return (
        results.reshape(local_experts, sources, capacity, width)
        .transpose(1, 0, 2, 3)
        .reshape(sources, local_experts * capacity, width)
    )


def _project_kernel(inputs_ref, weights_ref, out_ref):
    out_ref[0] = jnp.dot(inputs_ref[...], weights_ref[0], preferred_element_type=jnp.float32)


def project(inputs, weights, blocks, tile=512):
    tokens, depth = inputs.shape
    columns = weights.shape[2]
    return pl.pallas_call(
        _project_kernel,
        out_shape=jax.ShapeDtypeStruct((blocks, tokens, columns), jnp.float32),
        grid=(blocks, columns // tile),
        in_specs=[
            pl.BlockSpec((tokens, depth), lambda s, j: (0, 0)),
            pl.BlockSpec((1, depth, tile), lambda s, j: (s, 0, j)),
        ],
        out_specs=pl.BlockSpec((1, tokens, tile), lambda s, j: (s, 0, j)),
        cost_estimate=pl.CostEstimate(
            flops=2 * tokens * depth * columns * blocks,
            transcendentals=0,
            bytes_accessed=2 * depth * columns * blocks + 2 * tokens * depth
            + 4 * tokens * columns * blocks,
        ),
    )(inputs, weights)


def sum_halves(values, axis, dim):
    half = values.shape[dim] // 2
    index = lax.axis_index(axis)
    own = lax.dynamic_slice_in_dim(values, index * half, half, axis=dim)
    given = lax.dynamic_slice_in_dim(values, (1 - index) * half, half, axis=dim)
    received = lax.ppermute(given.astype(jnp.bfloat16), axis, [(0, 1), (1, 0)])
    return own + received.astype(own.dtype)


def swap_context(values):
    return lax.ppermute(values, "context", [(0, 1), (1, 0)])


def gather_context(values):
    other = swap_context(values)
    first = lax.axis_index("context") == 0
    return jnp.concatenate(
        [jnp.where(first, values, other), jnp.where(first, other, values)], axis=0
    )


def sum_context_halves(values):
    half = values.shape[0] // 2
    first = lax.axis_index("context") == 0
    own = jnp.where(first, values[:half], values[half:])
    given = jnp.where(first, values[half:], values[:half]).astype(jnp.bfloat16)
    return own + swap_context(given).astype(own.dtype)


def butterfly_sum(values, axes):
    index = lax.axis_index(axes)
    count = 1
    for name in axes:
        count *= lax.axis_size(name)
    step = 1
    while step < count:
        partner = [(i, i ^ step) for i in range(count)]
        received = lax.ppermute(values, axes, partner)
        mine_first = (index & step) == 0
        values = jnp.where(mine_first, values + received, received + values)
        step *= 2
    return values


def body(
    tokens,
    grad_output,
    routes,
    positions,
    attn_gain,
    q_gain,
    k_gain,
    ffn_gain,
    qkv_weight,
    out_weight,
    router_weight,
    expert_in,
    expert_out,
):
    single_precision = jnp.float32
    bf16 = jnp.bfloat16
    seq_tok = tokens.shape[1]
    width = tokens.shape[2]
    top = routes.shape[2]
    heads_width = out_weight.shape[1]
    head_dim = HDIM
    heads = heads_width // head_dim
    local_experts = expert_in.shape[0]
    experts = router_weight.shape[1]
    sources = lax.axis_size("expert")
    capacity = min(seq_tok, seq_tok * top * 5 // (4 * experts))
    scale = head_dim ** (-0.5)
    x = tokens[0].astype(single_precision)
    normed1, factor1 = rms_forward(x)
    attention_input = (normed1 * attn_gain).astype(bf16)
    all_axes = ("dp", "context", "expert")
    weights_full = lax.all_gather(
        jnp.concatenate([qkv_weight.transpose(1, 0, 2), out_weight[:, None, :]], axis=1),
        all_axes,
        axis=0,
        tiled=True,
    )
    out_full = weights_full[:, 3, :]
    projected_output = project(attention_input, weights_full.transpose(1, 0, 2), 3)
    q_normed, q_factor = rms_forward(projected_output[0])
    k_normed, k_factor = rms_forward(projected_output[1])
    values = projected_output[2].astype(bf16)
    all_places = positions[0]
    own_places = lax.dynamic_slice_in_dim(all_places, lax.axis_index("context") * seq_tok, seq_tok)
    cosine, sine = rope_tables(own_places, head_dim)
    queries = rotate(
        (q_normed * q_gain).reshape(seq_tok, heads, head_dim), cosine, sine, 1.0
    ).astype(bf16)
    own_keys = rotate(
        (k_normed * k_gain).reshape(seq_tok, heads, head_dim), cosine, sine, 1.0
    ).astype(bf16)
    keys_vals = gather_context(
        jnp.stack([own_keys.reshape(seq_tok, heads_width), values], axis=1)
    )
    keys = keys_vals[:, 0]
    vals = keys_vals[:, 1]
    seq_len = keys.shape[0]
    keys3 = keys.reshape(seq_len, heads, head_dim)
    vals3 = vals.reshape(seq_len, heads, head_dim)
    allowed = (all_places[None, :] <= own_places[:, None])[None]

    def masked_scores():
        scores = (
            jnp.einsum("qhd,khd->hqk", queries, keys3, preferred_element_type=single_precision)
            * scale
        )
        return jnp.where(allowed, scores, -jnp.inf)

    scores = masked_scores()
    lse = jnp.log(jnp.sum(jnp.exp(scores), axis=-1, keepdims=True))
    probs_b = jnp.exp(scores - lse).astype(bf16)
    attended = (
        jnp.einsum("hqk,khd->qhd", probs_b, vals3, preferred_element_type=single_precision)
        .astype(bf16)
        .reshape(seq_tok, heads_width)
    )
    mid = x + jnp.einsum("tq,dq->td", attended, out_full, preferred_element_type=single_precision)
    normed2, factor2 = rms_forward(mid)
    ffn_in = (normed2 * ffn_gain).astype(bf16)
    router_exp = jnp.exp(jnp.dot(ffn_in, router_weight, preferred_element_type=single_precision))
    router_probs = router_exp / jnp.sum(router_exp, axis=-1, keepdims=True)
    own_routes = routes[0]
    slots = slot_index(own_routes.reshape(-1), experts, capacity)
    send = (
        jnp.zeros((experts * capacity, width), bf16).at[slots].set(jnp.repeat(ffn_in, top, axis=0))
    )
    received = lax.all_to_all(
        send.reshape(sources, local_experts * capacity, width),
        "expert",
        split_axis=0,
        concat_axis=0,
        tiled=True,
    )
    rows = expert_major(received, local_experts, capacity)
    gate_up = jnp.einsum("lrd,lkdh->lkrh", rows, expert_in, preferred_element_type=single_precision)
    gate = gate_up[:, 0]
    up = gate_up[:, 1]
    sig = jax.nn.sigmoid(gate)
    hidden = (gate * sig * up).astype(bf16)
    results = jnp.einsum(
        "lrh,lhd->lrd", hidden, expert_out, preferred_element_type=single_precision
    ).astype(bf16)
    back = lax.all_to_all(
        source_major(results, sources, capacity), "expert", split_axis=0, concat_axis=0, tiled=True
    )
    route_out = back.reshape(experts * capacity, width)[slots].reshape(seq_tok, top, width)
    route_weight = jnp.take_along_axis(router_probs, own_routes, axis=1)
    output = mid + jnp.sum(route_weight[:, :, None] * route_out, axis=1)
    grad = grad_output[0].astype(single_precision)
    route_grad_weight = jnp.sum(grad[:, None, :] * route_out, axis=-1)
    route_grad = (
        (route_weight[:, :, None] * grad[:, None, :]).astype(bf16).reshape(seq_tok * top, width)
    )
    grad_send = jnp.zeros((experts * capacity, width), bf16).at[slots].set(route_grad)
    grad_received = lax.all_to_all(
        grad_send.reshape(sources, local_experts * capacity, width),
        "expert",
        split_axis=0,
        concat_axis=0,
        tiled=True,
    )
    grad_rows = expert_major(grad_received, local_experts, capacity)
    grad_hidden = jnp.einsum(
        "lrd,lhd->lrh", grad_rows, expert_out, preferred_element_type=single_precision
    )
    grad_gate = (grad_hidden * up * sig * (1.0 + gate * (1.0 - sig))).astype(bf16)
    grad_up = (grad_hidden * gate * sig).astype(bf16)
    grad_gate_up = jnp.stack([grad_gate, grad_up], axis=1)
    grad_rows_in = jnp.einsum(
        "lkrh,lkdh->lrd", grad_gate_up, expert_in, preferred_element_type=single_precision
    ).astype(bf16)
    grad_back = lax.all_to_all(
        source_major(grad_rows_in, sources, capacity),
        "expert",
        split_axis=0,
        concat_axis=0,
        tiled=True,
    )
    grad_route_in = grad_back.reshape(experts * capacity, width)[slots].reshape(seq_tok, top, width)
    grad_ffn_in = jnp.sum(grad_route_in, axis=1, dtype=single_precision)
    chosen = (own_routes[:, :, None] == jnp.arange(experts, dtype=jnp.int32)[None, None, :]).astype(
        single_precision
    )
    grad_probs = jnp.sum(route_grad_weight[:, :, None] * chosen, axis=1)
    grad_logits = (
        router_probs * (grad_probs - jnp.sum(router_probs * grad_probs, axis=-1, keepdims=True))
    ).astype(bf16)
    grad_router = jnp.einsum(
        "td,te->de", ffn_in, grad_logits, preferred_element_type=single_precision
    )
    grad_ffn_in = grad_ffn_in + jnp.einsum(
        "te,de->td", grad_logits, router_weight, preferred_element_type=single_precision
    )
    grad_mid_norm, grad_ffn_gain = rms_backward(grad_ffn_in, normed2, factor2, ffn_gain)
    grad_mid = grad + grad_mid_norm
    grad_mid_b = grad_mid.astype(bf16)
    all_axes_size = lax.axis_size(all_axes)
    shard_rows = width // all_axes_size
    start = lax.axis_index(all_axes) * shard_rows
    out_weight_sum = lax.psum(
        jnp.einsum("td,tq->dq", grad_mid_b, attended, preferred_element_type=single_precision).astype(
            bf16
        ),
        all_axes,
    )
    grad_att = (
        jnp.einsum("td,dq->tq", grad_mid_b, out_full, preferred_element_type=single_precision)
        .astype(bf16)
        .reshape(seq_tok, heads, head_dim)
    )
    delta = jnp.sum(
        grad_att.astype(single_precision)
        * attended.reshape(seq_tok, heads, head_dim).astype(single_precision),
        axis=-1,
    )
    probs = jnp.exp(masked_scores() - lse)
    grad_vals = jnp.einsum(
        "hqk,qhd->khd", probs.astype(bf16), grad_att, preferred_element_type=single_precision
    )
    grad_p = jnp.einsum("qhd,khd->hqk", grad_att, vals3, preferred_element_type=single_precision)
    grad_scores = (probs * (grad_p - delta.T[:, :, None])).astype(bf16)
    grad_queries = (
        jnp.einsum("hqk,khd->qhd", grad_scores, keys3, preferred_element_type=single_precision)
        * scale
    )
    grad_keys_all = (
        jnp.einsum("hqk,qhd->khd", grad_scores, queries, preferred_element_type=single_precision)
        * scale
    )
    grad_keys_values = sum_context_halves(
        jnp.stack(
            [grad_keys_all.reshape(seq_len, heads_width), grad_vals.reshape(seq_len, heads_width)],
            axis=1,
        )
    )
    grad_keys = grad_keys_values[:, 0]
    grad_values = grad_keys_values[:, 1]
    grad_qn = rotate(grad_queries, cosine, sine, -1.0).reshape(seq_tok, heads_width)
    grad_kn = rotate(grad_keys.reshape(seq_tok, heads, head_dim), cosine, sine, -1.0).reshape(
        seq_tok, heads_width
    )
    grad_q_raw, grad_q_gain = rms_backward(grad_qn, q_normed, q_factor, q_gain)
    grad_k_raw, grad_k_gain = rms_backward(grad_kn, k_normed, k_factor, k_gain)
    projected_gradient = jnp.stack(
        [grad_q_raw, grad_k_raw, grad_values, jnp.zeros_like(grad_values)], axis=1
    ).astype(bf16)
    attention_input_gradient = jnp.dot(
        projected_gradient.reshape(seq_tok, 4 * heads_width),
        weights_full.reshape(width, 4 * heads_width).T,
        preferred_element_type=single_precision,
    )
    grad_x_norm, grad_attn_gain = rms_backward(
        attention_input_gradient, normed1, factor1, attn_gain
    )
    grad_tokens = grad_mid + grad_x_norm
    stacked = jnp.einsum(
        "ta,stb->sab",
        attention_input,
        projected_gradient[:, :3].transpose(1, 0, 2),
        preferred_element_type=single_precision,
    ).astype(bf16)
    stacked, out_weight_sum, rows, grad_gate_up, hidden, grad_rows = lax.optimization_barrier(
        (stacked, out_weight_sum, rows, grad_gate_up, hidden, grad_rows)
    )
    summed = lax.psum(stacked, all_axes)
    grad_out_shard = lax.dynamic_slice_in_dim(out_weight_sum, start, shard_rows, axis=0).astype(
        single_precision
    )
    grad_qkv_shard = lax.dynamic_slice_in_dim(summed, start, shard_rows, axis=1).astype(
        single_precision
    )
    grad_gate_up_w = jnp.einsum(
        "lrd,lkrh->lkdh", rows, grad_gate_up, preferred_element_type=single_precision
    )
    grad_down = jnp.einsum(
        "lrh,lrd->lhd", hidden, grad_rows, preferred_element_type=single_precision
    )

    def scatter_over_copies(values):
        return sum_halves(sum_halves(values, "dp", 1), "context", 1)

    grad_in_shard = scatter_over_copies(grad_gate_up_w[0])[None]
    grad_down_shard = scatter_over_copies(grad_down[0])[None]
    small_sum = butterfly_sum(
        jnp.concatenate(
            [grad_attn_gain, grad_q_gain, grad_k_gain, grad_ffn_gain, grad_router.reshape(-1)]
        ),
        all_axes,
    )
    sizes = [width, heads_width, heads_width, width, width * experts]
    offsets = [sum(sizes[:n]) for n in range(len(sizes))]
    totals = [small_sum[o : o + n] for o, n in zip(offsets, sizes)]
    totals[4] = totals[4].reshape(width, experts)
    return (
        output[None],
        grad_tokens[None],
        totals[0],
        totals[1],
        totals[2],
        totals[3],
        totals[4],
        grad_qkv_shard,
        grad_out_shard,
        grad_in_shard,
        grad_down_shard,
    )


def solution(mesh):
    return jax.shard_map(
        body,
        mesh=mesh,
        in_specs=(
            P(("dp", "expert"), "context", None),
            P(("dp", "expert"), "context", None),
            P(("dp", "expert"), "context", None),
            P(("dp", "expert"), None),
            P(),
            P(),
            P(),
            P(),
            P(None, ("dp", "context", "expert"), None),
            P(("dp", "context", "expert"), None),
            P(),
            P("expert", None, None, None),
            P("expert", None, None),
        ),
        out_specs=(
            P(("dp", "expert"), "context", None),
            P(("dp", "expert"), "context", None),
            P(),
            P(),
            P(),
            P(),
            P(),
            P(None, ("dp", "context", "expert"), None),
            P(("dp", "context", "expert"), None),
            P("expert", None, ("dp", "context"), None),
            P("expert", None, ("dp", "context")),
        ),
        check_vma=False,
    )
```

```python
import functools

import jax
import jax.numpy as jnp
from jax import lax
from jax.experimental import pallas as pl
from jax.experimental.pallas import tpu as pltpu
from jax.sharding import PartitionSpec as P

HDIM = 128


EPS = 1e-05
THETA = 10000.0


def rope_tables(places, head_dim):
    half = head_dim // 2
    freq = THETA ** (-jnp.arange(half, dtype=jnp.float32) * 2.0 / head_dim)
    angle = places.astype(jnp.float32)[:, None] * freq[None, :]
    return (jnp.cos(angle), jnp.sin(angle))


def rotate(values, cosine, sine, sign):
    half = values.shape[-1] // 2
    first = values[..., :half]
    second = values[..., half:]
    cosine = cosine[:, None, :]
    sine = sign * sine[:, None, :]
    return jnp.concatenate(
        [first * cosine - second * sine, second * cosine + first * sine], axis=-1
    )


def rms_forward(values):
    factor = lax.rsqrt(jnp.mean(values * values, axis=-1, keepdims=True) + EPS)
    return (values * factor, factor)


def rms_backward(grad_out, normed, factor, gain):
    scaled = grad_out * gain
    grad_in = factor * (scaled - normed * jnp.mean(scaled * normed, axis=-1, keepdims=True))
    return (grad_in, jnp.sum(grad_out * normed, axis=0))


def slot_index(route_rows, experts, capacity):
    onehot = (route_rows[:, None] == jnp.arange(experts, dtype=jnp.int32)[None, :]).astype(
        jnp.int32
    )
    count = route_rows.shape[0]
    earlier = (
        jnp.arange(count, dtype=jnp.int32)[None, :] < jnp.arange(count, dtype=jnp.int32)[:, None]
    ).astype(jnp.bfloat16)
    before = jnp.dot(earlier, onehot.astype(jnp.bfloat16), preferred_element_type=jnp.float32)
    return route_rows * capacity + jnp.sum(before.astype(jnp.int32) * onehot, axis=1)


def expert_major(received, local_experts, capacity):
    sources, _, width = received.shape
    return (
        received.reshape(sources, local_experts, capacity, width)
        .transpose(1, 0, 2, 3)
        .reshape(local_experts, sources * capacity, width)
    )


def source_major(results, sources, capacity):
    local_experts, _, width = results.shape
    return (
        results.reshape(local_experts, sources, capacity, width)
        .transpose(1, 0, 2, 3)
        .reshape(sources, local_experts * capacity, width)
    )


def _project_kernel(inputs_ref, weights_ref, out_ref):
    out_ref[0] = jnp.dot(inputs_ref[...], weights_ref[0], preferred_element_type=jnp.float32)


def project(inputs, weights, blocks, tile=512):
    tokens, depth = inputs.shape
    columns = weights.shape[2]
    return pl.pallas_call(
        _project_kernel,
        out_shape=jax.ShapeDtypeStruct((blocks, tokens, columns), jnp.float32),
        grid=(blocks, columns // tile),
        in_specs=[
            pl.BlockSpec((tokens, depth), lambda s, j: (0, 0)),
            pl.BlockSpec((1, depth, tile), lambda s, j: (s, 0, j)),
        ],
        out_specs=pl.BlockSpec((1, tokens, tile), lambda s, j: (s, 0, j)),
        cost_estimate=pl.CostEstimate(
            flops=2 * tokens * depth * columns * blocks,
            transcendentals=0,
            bytes_accessed=2 * depth * columns * blocks + 2 * tokens * depth
            + 4 * tokens * columns * blocks,
        ),
    )(inputs, weights)


def sum_halves(values, axis, dim):
    half = values.shape[dim] // 2
    index = lax.axis_index(axis)
    own = lax.dynamic_slice_in_dim(values, index * half, half, axis=dim)
    given = lax.dynamic_slice_in_dim(values, (1 - index) * half, half, axis=dim)
    received = lax.ppermute(given.astype(jnp.bfloat16), axis, [(0, 1), (1, 0)])
    return own + received.astype(own.dtype)


def swap_context(values):
    return lax.ppermute(values, "context", [(0, 1), (1, 0)])


def gather_context(values):
    other = swap_context(values)
    first = lax.axis_index("context") == 0
    return jnp.concatenate(
        [jnp.where(first, values, other), jnp.where(first, other, values)], axis=0
    )


def sum_context_halves(values):
    half = values.shape[0] // 2
    first = lax.axis_index("context") == 0
    own = jnp.where(first, values[:half], values[half:])
    given = jnp.where(first, values[half:], values[:half]).astype(jnp.bfloat16)
    return own + swap_context(given).astype(own.dtype)


def butterfly_sum(values, axes):
    index = lax.axis_index(axes)
    count = 1
    for name in axes:
        count *= lax.axis_size(name)
    step = 1
    while step < count:
        partner = [(i, i ^ step) for i in range(count)]
        received = lax.ppermute(values, axes, partner)
        mine_first = (index & step) == 0
        values = jnp.where(mine_first, values + received, received + values)
        step *= 2
    return values


def body(
    tokens,
    grad_output,
    routes,
    positions,
    attn_gain,
    q_gain,
    k_gain,
    ffn_gain,
    qkv_weight,
    out_weight,
    router_weight,
    expert_in,
    expert_out,
):
    single_precision = jnp.float32
    bf16 = jnp.bfloat16
    seq_tok = tokens.shape[1]
    width = tokens.shape[2]
    top = routes.shape[2]
    heads_width = out_weight.shape[1]
    head_dim = HDIM
    heads = heads_width // head_dim
    local_experts = expert_in.shape[0]
    experts = router_weight.shape[1]
    sources = lax.axis_size("expert")
    capacity = min(seq_tok, seq_tok * top * 5 // (4 * experts))
    scale = head_dim ** (-0.5)
    x = tokens[0].astype(single_precision)
    normed1, factor1 = rms_forward(x)
    attention_input = (normed1 * attn_gain).astype(bf16)
    all_axes = ("dp", "context", "expert")
    weights_full = lax.all_gather(
        jnp.concatenate([qkv_weight.transpose(1, 0, 2), out_weight[:, None, :]], axis=1),
        all_axes,
        axis=0,
        tiled=True,
    )
    out_full = weights_full[:, 3, :]
    projected_output = project(attention_input, weights_full.transpose(1, 0, 2), 3)
    q_normed, q_factor = rms_forward(projected_output[0])
    k_normed, k_factor = rms_forward(projected_output[1])
    values = projected_output[2].astype(bf16)
    all_places = positions[0]
    own_places = lax.dynamic_slice_in_dim(all_places, lax.axis_index("context") * seq_tok, seq_tok)
    cosine, sine = rope_tables(own_places, head_dim)
    queries = rotate(
        (q_normed * q_gain).reshape(seq_tok, heads, head_dim), cosine, sine, 1.0
    ).astype(bf16)
    own_keys = rotate(
        (k_normed * k_gain).reshape(seq_tok, heads, head_dim), cosine, sine, 1.0
    ).astype(bf16)
    keys_vals = gather_context(
        jnp.stack([own_keys.reshape(seq_tok, heads_width), values], axis=1)
    )
    keys = keys_vals[:, 0]
    vals = keys_vals[:, 1]
    seq_len = keys.shape[0]
    keys3 = keys.reshape(seq_len, heads, head_dim)
    vals3 = vals.reshape(seq_len, heads, head_dim)
    allowed = (all_places[None, :] <= own_places[:, None])[None]

    def masked_scores():
        scores = (
            jnp.einsum("qhd,khd->hqk", queries, keys3, preferred_element_type=single_precision)
            * scale
        )
        return jnp.where(allowed, scores, -jnp.inf)

    scores = masked_scores()
    lse = jnp.log(jnp.sum(jnp.exp(scores), axis=-1, keepdims=True))
    probs_b = jnp.exp(scores - lse).astype(bf16)
    attended = (
        jnp.einsum("hqk,khd->qhd", probs_b, vals3, preferred_element_type=single_precision)
        .astype(bf16)
        .reshape(seq_tok, heads_width)
    )
    mid = x + jnp.einsum("tq,dq->td", attended, out_full, preferred_element_type=single_precision)
    normed2, factor2 = rms_forward(mid)
    ffn_in = (normed2 * ffn_gain).astype(bf16)
    router_exp = jnp.exp(jnp.dot(ffn_in, router_weight, preferred_element_type=single_precision))
    router_probs = router_exp / jnp.sum(router_exp, axis=-1, keepdims=True)
    own_routes = routes[0]
    slots = slot_index(own_routes.reshape(-1), experts, capacity)
    route_weight = jnp.take_along_axis(router_probs, own_routes, axis=1)
    grad = grad_output[0].astype(single_precision)
    route_grad = (
        (route_weight[:, :, None] * grad[:, None, :]).astype(bf16).reshape(seq_tok * top, width)
    )
    send = jnp.stack(
        [
            jnp.zeros((experts * capacity, width), bf16).at[slots].set(jnp.repeat(ffn_in, top, axis=0)),
            jnp.zeros((experts * capacity, width), bf16).at[slots].set(route_grad),
        ]
    ).reshape(2, sources, local_experts * capacity, width)
    received = lax.all_to_all(
        send.transpose(1, 0, 2, 3), "expert", split_axis=0, concat_axis=0, tiled=True
    )
    rows = expert_major(received[:, 0], local_experts, capacity)
    grad_rows = expert_major(received[:, 1], local_experts, capacity)
    gate_up = jnp.einsum("lrd,lkdh->lkrh", rows, expert_in, preferred_element_type=single_precision)
    gate = gate_up[:, 0]
    up = gate_up[:, 1]
    sig = jax.nn.sigmoid(gate)
    hidden = (gate * sig * up).astype(bf16)
    results = jnp.einsum(
        "lrh,lhd->lrd", hidden, expert_out, preferred_element_type=single_precision
    ).astype(bf16)
    grad_hidden = jnp.einsum(
        "lrd,lhd->lrh", grad_rows, expert_out, preferred_element_type=single_precision
    )
    grad_gate = (grad_hidden * up * sig * (1.0 + gate * (1.0 - sig))).astype(bf16)
    grad_up = (grad_hidden * gate * sig).astype(bf16)
    grad_gate_up = jnp.stack([grad_gate, grad_up], axis=1)
    grad_rows_in = jnp.einsum(
        "lkrh,lkdh->lrd", grad_gate_up, expert_in, preferred_element_type=single_precision
    ).astype(bf16)
    grad_down = jnp.einsum(
        "lrh,lrd->lhd", hidden, grad_rows, preferred_element_type=single_precision
    )
    grad_gate_up_w = jnp.einsum(
        "lrd,lkrh->lkdh", rows, grad_gate_up, preferred_element_type=single_precision
    )
    back_both = lax.all_to_all(
        jnp.stack(
            [source_major(results, sources, capacity), source_major(grad_rows_in, sources, capacity)],
            axis=1,
        ),
        "expert",
        split_axis=0,
        concat_axis=0,
        tiled=True,
    )
    back = back_both[:, 0]
    grad_back = back_both[:, 1]
    route_out = back.reshape(experts * capacity, width)[slots].reshape(seq_tok, top, width)
    output = mid + jnp.sum(route_weight[:, :, None] * route_out, axis=1)
    route_grad_weight = jnp.sum(grad[:, None, :] * route_out, axis=-1)
    grad_route_in = grad_back.reshape(experts * capacity, width)[slots].reshape(seq_tok, top, width)
    grad_ffn_in = jnp.sum(grad_route_in, axis=1, dtype=single_precision)
    chosen = (own_routes[:, :, None] == jnp.arange(experts, dtype=jnp.int32)[None, None, :]).astype(
        single_precision
    )
    grad_probs = jnp.sum(route_grad_weight[:, :, None] * chosen, axis=1)
    grad_logits = (
        router_probs * (grad_probs - jnp.sum(router_probs * grad_probs, axis=-1, keepdims=True))
    ).astype(bf16)
    grad_router = jnp.einsum(
        "td,te->de", ffn_in, grad_logits, preferred_element_type=single_precision
    )
    grad_ffn_in = grad_ffn_in + jnp.einsum(
        "te,de->td", grad_logits, router_weight, preferred_element_type=single_precision
    )
    grad_mid_norm, grad_ffn_gain = rms_backward(grad_ffn_in, normed2, factor2, ffn_gain)
    grad_mid = grad + grad_mid_norm
    grad_mid_b = grad_mid.astype(bf16)
    grad_att = (
        jnp.einsum("td,dq->tq", grad_mid_b, out_full, preferred_element_type=single_precision)
        .astype(bf16)
        .reshape(seq_tok, heads, head_dim)
    )
    delta = jnp.sum(
        grad_att.astype(single_precision)
        * attended.reshape(seq_tok, heads, head_dim).astype(single_precision),
        axis=-1,
    )
    probs = jnp.exp(masked_scores() - lse)
    grad_vals = jnp.einsum(
        "hqk,qhd->khd", probs.astype(bf16), grad_att, preferred_element_type=single_precision
    )
    grad_p = jnp.einsum("qhd,khd->hqk", grad_att, vals3, preferred_element_type=single_precision)
    grad_scores = (probs * (grad_p - delta.T[:, :, None])).astype(bf16)
    grad_queries = (
        jnp.einsum("hqk,khd->qhd", grad_scores, keys3, preferred_element_type=single_precision)
        * scale
    )
    grad_keys_all = (
        jnp.einsum("hqk,qhd->khd", grad_scores, queries, preferred_element_type=single_precision)
        * scale
    )
    grad_keys_values = sum_context_halves(
        jnp.stack(
            [grad_keys_all.reshape(seq_len, heads_width), grad_vals.reshape(seq_len, heads_width)],
            axis=1,
        )
    )
    grad_keys = grad_keys_values[:, 0]
    grad_values = grad_keys_values[:, 1]
    grad_qn = rotate(grad_queries, cosine, sine, -1.0).reshape(seq_tok, heads_width)
    grad_kn = rotate(grad_keys.reshape(seq_tok, heads, head_dim), cosine, sine, -1.0).reshape(
        seq_tok, heads_width
    )
    grad_q_raw, grad_q_gain = rms_backward(grad_qn, q_normed, q_factor, q_gain)
    grad_k_raw, grad_k_gain = rms_backward(grad_kn, k_normed, k_factor, k_gain)
    projected_gradient = jnp.stack(
        [grad_q_raw, grad_k_raw, grad_values, jnp.zeros_like(grad_values)], axis=1
    ).astype(bf16)
    attention_input_gradient = jnp.dot(
        projected_gradient.reshape(seq_tok, 4 * heads_width),
        weights_full.reshape(width, 4 * heads_width).T,
        preferred_element_type=single_precision,
    )
    grad_x_norm, grad_attn_gain = rms_backward(
        attention_input_gradient, normed1, factor1, attn_gain
    )
    grad_tokens = grad_mid + grad_x_norm
    def scatter_over_copies(values):
        return sum_halves(sum_halves(values, "dp", 1), "context", 1)

    grad_in_shard = scatter_over_copies(grad_gate_up_w[0])[None]
    grad_down_shard = scatter_over_copies(grad_down[0])[None]
    left = jnp.stack([attention_input] * 3 + [grad_mid_b])
    right = jnp.concatenate(
        [projected_gradient[:, :3].transpose(1, 0, 2), attended[None]], axis=0
    )
    stacked = jnp.einsum("sta,stb->sab", left, right, preferred_element_type=single_precision)
    summed = lax.psum(stacked.astype(bf16), all_axes)
    shard_rows = width // lax.axis_size(all_axes)
    start = lax.axis_index(all_axes) * shard_rows
    weight_shard = lax.dynamic_slice_in_dim(summed, start, shard_rows, axis=1).astype(
        single_precision
    )
    grad_qkv_shard = weight_shard[:3]
    grad_out_shard = weight_shard[3]
    small_sum = butterfly_sum(
        jnp.concatenate(
            [grad_attn_gain, grad_q_gain, grad_k_gain, grad_ffn_gain, grad_router.reshape(-1)]
        ),
        all_axes,
    )
    sizes = [width, heads_width, heads_width, width, width * experts]
    offsets = [sum(sizes[:n]) for n in range(len(sizes))]
    totals = [small_sum[o : o + n] for o, n in zip(offsets, sizes)]
    totals[4] = totals[4].reshape(width, experts)
    return (
        output[None],
        grad_tokens[None],
        totals[0],
        totals[1],
        totals[2],
        totals[3],
        totals[4],
        grad_qkv_shard,
        grad_out_shard,
        grad_in_shard,
        grad_down_shard,
    )


def solution(mesh):
    return jax.shard_map(
        body,
        mesh=mesh,
        in_specs=(
            P(("dp", "expert"), "context", None),
            P(("dp", "expert"), "context", None),
            P(("dp", "expert"), "context", None),
            P(("dp", "expert"), None),
            P(),
            P(),
            P(),
            P(),
            P(None, ("dp", "context", "expert"), None),
            P(("dp", "context", "expert"), None),
            P(),
            P("expert", None, None, None),
            P("expert", None, None),
        ),
        out_specs=(
            P(("dp", "expert"), "context", None),
            P(("dp", "expert"), "context", None),
            P(),
            P(),
            P(),
            P(),
            P(),
            P(None, ("dp", "context", "expert"), None),
            P(("dp", "context", "expert"), None),
            P("expert", None, ("dp", "context"), None),
            P("expert", None, ("dp", "context")),
        ),
        check_vma=False,
    )
```

```python
import functools

import jax
import jax.numpy as jnp
from jax import lax
from jax.experimental import pallas as pl
from jax.experimental.pallas import tpu as pltpu
from jax.sharding import PartitionSpec as P

HDIM = 128


EPS = 1e-05
THETA = 10000.0


def rope_tables(places, head_dim):
    half = head_dim // 2
    freq = THETA ** (-jnp.arange(half, dtype=jnp.float32) * 2.0 / head_dim)
    angle = places.astype(jnp.float32)[:, None] * freq[None, :]
    return (jnp.cos(angle), jnp.sin(angle))


def rotate(values, cosine, sine, sign):
    half = values.shape[-1] // 2
    first = values[..., :half]
    second = values[..., half:]
    cosine = cosine[:, None, :]
    sine = sign * sine[:, None, :]
    return jnp.concatenate(
        [first * cosine - second * sine, second * cosine + first * sine], axis=-1
    )


def rms_forward(values):
    factor = lax.rsqrt(jnp.mean(values * values, axis=-1, keepdims=True) + EPS)
    return (values * factor, factor)


def rms_backward(grad_out, normed, factor, gain):
    scaled = grad_out * gain
    grad_in = factor * (scaled - normed * jnp.mean(scaled * normed, axis=-1, keepdims=True))
    return (grad_in, jnp.sum(grad_out * normed, axis=0))


def slot_index(route_rows, experts, capacity):
    onehot = (route_rows[:, None] == jnp.arange(experts, dtype=jnp.int32)[None, :]).astype(
        jnp.int32
    )
    count = route_rows.shape[0]
    earlier = (
        jnp.arange(count, dtype=jnp.int32)[None, :] < jnp.arange(count, dtype=jnp.int32)[:, None]
    ).astype(jnp.bfloat16)
    before = jnp.dot(earlier, onehot.astype(jnp.bfloat16), preferred_element_type=jnp.float32)
    return route_rows * capacity + jnp.sum(before.astype(jnp.int32) * onehot, axis=1)


def expert_major(received, local_experts, capacity):
    sources, _, width = received.shape
    return (
        received.reshape(sources, local_experts, capacity, width)
        .transpose(1, 0, 2, 3)
        .reshape(local_experts, sources * capacity, width)
    )


def source_major(results, sources, capacity):
    local_experts, _, width = results.shape
    return (
        results.reshape(local_experts, sources, capacity, width)
        .transpose(1, 0, 2, 3)
        .reshape(sources, local_experts * capacity, width)
    )


def _project_kernel(inputs_ref, weights_ref, out_ref):
    out_ref[0] = jnp.dot(inputs_ref[...], weights_ref[0], preferred_element_type=jnp.float32)


def project(inputs, weights, blocks, tile=512):
    tokens, depth = inputs.shape
    columns = weights.shape[2]
    return pl.pallas_call(
        _project_kernel,
        out_shape=jax.ShapeDtypeStruct((blocks, tokens, columns), jnp.float32),
        grid=(blocks, columns // tile),
        in_specs=[
            pl.BlockSpec((tokens, depth), lambda s, j: (0, 0)),
            pl.BlockSpec((1, depth, tile), lambda s, j: (s, 0, j)),
        ],
        out_specs=pl.BlockSpec((1, tokens, tile), lambda s, j: (s, 0, j)),
        cost_estimate=pl.CostEstimate(
            flops=2 * tokens * depth * columns * blocks,
            transcendentals=0,
            bytes_accessed=2 * depth * columns * blocks + 2 * tokens * depth
            + 4 * tokens * columns * blocks,
        ),
    )(inputs, weights)


def _dispatch_kernel(token_ref, weight_ref, rows_ref, grad_ref, send_ref, grad_send_ref):
    tile = token_ref.shape[0]
    tokens = rows_ref.shape[0]
    pick = (
        token_ref[...] == lax.broadcasted_iota(jnp.int32, (tile, tokens), 1)
    ).astype(jnp.bfloat16)
    send_ref[...] = jnp.dot(pick, rows_ref[...], preferred_element_type=jnp.float32).astype(
        send_ref.dtype
    )
    picked_grad = jnp.dot(pick, grad_ref[...], preferred_element_type=jnp.float32)
    grad_send_ref[...] = (weight_ref[...] * picked_grad).astype(grad_send_ref.dtype)


def dispatch(slot_token, slot_weight, rows, grad, tile=256):
    slots = slot_token.shape[0]
    tokens, width = rows.shape
    out = jax.ShapeDtypeStruct((slots, width), jnp.bfloat16)
    return pl.pallas_call(
        _dispatch_kernel,
        out_shape=(out, out),
        grid=(slots // tile,),
        in_specs=[
            pl.BlockSpec((tile, 1), lambda i: (i, 0)),
            pl.BlockSpec((tile, 1), lambda i: (i, 0)),
            pl.BlockSpec((tokens, width), lambda i: (0, 0)),
            pl.BlockSpec((tokens, width), lambda i: (0, 0)),
        ],
        out_specs=(
            pl.BlockSpec((tile, width), lambda i: (i, 0)),
            pl.BlockSpec((tile, width), lambda i: (i, 0)),
        ),
        cost_estimate=pl.CostEstimate(
            flops=4 * slots * tokens * width,
            transcendentals=0,
            bytes_accessed=4 * slots * width + 4 * tokens * width + 8 * slots,
        ),
    )(slot_token, slot_weight, rows, grad)


def _combine_kernel(with_dots, slot_ref, weight_ref, table_ref, base_ref, other_ref, out_ref, dots_ref):
    tokens, top = slot_ref.shape
    count = table_ref.shape[0]
    total = base_ref[...]
    for k in range(top):
        pick = (
            slot_ref[:, k : k + 1] == lax.broadcasted_iota(jnp.int32, (tokens, count), 1)
        ).astype(jnp.bfloat16)
        row = jnp.dot(pick, table_ref[...], preferred_element_type=jnp.float32)
        total = total + weight_ref[:, k : k + 1] * row
        if with_dots:
            dots_ref[:, k : k + 1] = jnp.sum(
                other_ref[...].astype(jnp.float32) * row, axis=1, keepdims=True
            )
    out_ref[...] = total
    if not with_dots:
        dots_ref[...] = jnp.zeros_like(dots_ref)


def combine(slots, weights, table, base, other, with_dots):
    tokens, top = slots.shape
    count, width = table.shape
    return pl.pallas_call(
        functools.partial(_combine_kernel, with_dots),
        out_shape=(
            jax.ShapeDtypeStruct((tokens, width), jnp.float32),
            jax.ShapeDtypeStruct((tokens, top), jnp.float32),
        ),
        in_specs=[pl.BlockSpec(memory_space=pltpu.VMEM)] * 5,
        out_specs=(pl.BlockSpec(memory_space=pltpu.VMEM), pl.BlockSpec(memory_space=pltpu.VMEM)),
        cost_estimate=pl.CostEstimate(
            flops=2 * tokens * count * width * top,
            transcendentals=0,
            bytes_accessed=2 * count * width + 10 * tokens * width,
        ),
    )(slots, weights, table, base, other)


def sum_halves(values, axis, dim):
    half = values.shape[dim] // 2
    index = lax.axis_index(axis)
    own = lax.dynamic_slice_in_dim(values, index * half, half, axis=dim)
    given = lax.dynamic_slice_in_dim(values, (1 - index) * half, half, axis=dim)
    received = lax.ppermute(given.astype(jnp.bfloat16), axis, [(0, 1), (1, 0)])
    return own + received.astype(own.dtype)


def swap_context(values):
    return lax.ppermute(values, "context", [(0, 1), (1, 0)])


def gather_context(values):
    other = swap_context(values)
    first = lax.axis_index("context") == 0
    return jnp.concatenate(
        [jnp.where(first, values, other), jnp.where(first, other, values)], axis=0
    )


def sum_context_halves(values):
    half = values.shape[0] // 2
    first = lax.axis_index("context") == 0
    own = jnp.where(first, values[:half], values[half:])
    given = jnp.where(first, values[half:], values[:half]).astype(jnp.bfloat16)
    return own + swap_context(given).astype(own.dtype)


def butterfly_sum(values, axes):
    index = lax.axis_index(axes)
    count = 1
    for name in axes:
        count *= lax.axis_size(name)
    step = 1
    while step < count:
        partner = [(i, i ^ step) for i in range(count)]
        received = lax.ppermute(values, axes, partner)
        mine_first = (index & step) == 0
        values = jnp.where(mine_first, values + received, received + values)
        step *= 2
    return values


def body(
    tokens,
    grad_output,
    routes,
    positions,
    attn_gain,
    q_gain,
    k_gain,
    ffn_gain,
    qkv_weight,
    out_weight,
    router_weight,
    expert_in,
    expert_out,
):
    single_precision = jnp.float32
    bf16 = jnp.bfloat16
    seq_tok = tokens.shape[1]
    width = tokens.shape[2]
    top = routes.shape[2]
    heads_width = out_weight.shape[1]
    head_dim = HDIM
    heads = heads_width // head_dim
    local_experts = expert_in.shape[0]
    experts = router_weight.shape[1]
    sources = lax.axis_size("expert")
    capacity = min(seq_tok, seq_tok * top * 5 // (4 * experts))
    scale = head_dim ** (-0.5)
    x = tokens[0].astype(single_precision)
    normed1, factor1 = rms_forward(x)
    attention_input = (normed1 * attn_gain).astype(bf16)
    all_axes = ("dp", "context", "expert")
    weights_full = lax.all_gather(
        jnp.concatenate([qkv_weight.transpose(1, 0, 2), out_weight[:, None, :]], axis=1),
        all_axes,
        axis=0,
        tiled=True,
    )
    out_full = weights_full[:, 3, :]
    projected_output = project(attention_input, weights_full.transpose(1, 0, 2), 3)
    q_normed, q_factor = rms_forward(projected_output[0])
    k_normed, k_factor = rms_forward(projected_output[1])
    values = projected_output[2].astype(bf16)
    all_places = positions[0]
    own_places = lax.dynamic_slice_in_dim(all_places, lax.axis_index("context") * seq_tok, seq_tok)
    cosine, sine = rope_tables(own_places, head_dim)
    queries = rotate(
        (q_normed * q_gain).reshape(seq_tok, heads, head_dim), cosine, sine, 1.0
    ).astype(bf16)
    own_keys = rotate(
        (k_normed * k_gain).reshape(seq_tok, heads, head_dim), cosine, sine, 1.0
    ).astype(bf16)
    keys_vals = gather_context(
        jnp.stack([own_keys.reshape(seq_tok, heads_width), values], axis=1)
    )
    keys = keys_vals[:, 0]
    vals = keys_vals[:, 1]
    seq_len = keys.shape[0]
    keys3 = keys.reshape(seq_len, heads, head_dim)
    vals3 = vals.reshape(seq_len, heads, head_dim)
    allowed = (all_places[None, :] <= own_places[:, None])[None]

    def masked_scores():
        scores = (
            jnp.einsum("qhd,khd->hqk", queries, keys3, preferred_element_type=single_precision)
            * scale
        )
        return jnp.where(allowed, scores, -jnp.inf)

    scores = masked_scores()
    lse = jnp.log(jnp.sum(jnp.exp(scores), axis=-1, keepdims=True))
    probs_b = jnp.exp(scores - lse).astype(bf16)
    attended = (
        jnp.einsum("hqk,khd->qhd", probs_b, vals3, preferred_element_type=single_precision)
        .astype(bf16)
        .reshape(seq_tok, heads_width)
    )
    mid = x + jnp.einsum("tq,dq->td", attended, out_full, preferred_element_type=single_precision)
    normed2, factor2 = rms_forward(mid)
    ffn_in = (normed2 * ffn_gain).astype(bf16)
    router_exp = jnp.exp(jnp.dot(ffn_in, router_weight, preferred_element_type=single_precision))
    router_probs = router_exp / jnp.sum(router_exp, axis=-1, keepdims=True)
    own_routes = routes[0]
    slots = slot_index(own_routes.reshape(-1), experts, capacity)
    route_weight = jnp.take_along_axis(router_probs, own_routes, axis=1)
    route_index = jnp.arange(seq_tok * top, dtype=jnp.int32)
    slot_token = jnp.full((experts * capacity,), -1, jnp.int32).at[slots].set(route_index // top)
    slot_weight = jnp.zeros((experts * capacity,), single_precision).at[slots].set(
        route_weight.reshape(-1)
    )
    send, grad_send = dispatch(slot_token[:, None], slot_weight[:, None], ffn_in, grad_output[0])
    received = lax.all_to_all(
        send.reshape(sources, local_experts * capacity, width),
        "expert",
        split_axis=0,
        concat_axis=0,
        tiled=True,
    )
    rows = expert_major(received, local_experts, capacity)
    gate_up = jnp.einsum("lrd,lkdh->lkrh", rows, expert_in, preferred_element_type=single_precision)
    gate = gate_up[:, 0]
    up = gate_up[:, 1]
    sig = jax.nn.sigmoid(gate)
    hidden = (gate * sig * up).astype(bf16)
    results = jnp.einsum(
        "lrh,lhd->lrd", hidden, expert_out, preferred_element_type=single_precision
    ).astype(bf16)
    back = lax.all_to_all(
        source_major(results, sources, capacity), "expert", split_axis=0, concat_axis=0, tiled=True
    )
    route_slots = slots.reshape(seq_tok, top)
    output, route_grad_weight = combine(
        route_slots,
        route_weight,
        back.reshape(experts * capacity, width),
        mid,
        grad_output[0],
        True,
    )
    grad = grad_output[0].astype(single_precision)
    grad_received = lax.all_to_all(
        grad_send.reshape(sources, local_experts * capacity, width),
        "expert",
        split_axis=0,
        concat_axis=0,
        tiled=True,
    )
    grad_rows = expert_major(grad_received, local_experts, capacity)
    grad_hidden = jnp.einsum(
        "lrd,lhd->lrh", grad_rows, expert_out, preferred_element_type=single_precision
    )
    grad_down = jnp.einsum(
        "lrh,lrd->lhd", hidden, grad_rows, preferred_element_type=single_precision
    )
    grad_gate = (grad_hidden * up * sig * (1.0 + gate * (1.0 - sig))).astype(bf16)
    grad_up = (grad_hidden * gate * sig).astype(bf16)
    grad_gate_up = jnp.stack([grad_gate, grad_up], axis=1)
    grad_gate_up_w = jnp.einsum(
        "lrd,lkrh->lkdh", rows, grad_gate_up, preferred_element_type=single_precision
    )
    grad_rows_in = jnp.einsum(
        "lkrh,lkdh->lrd", grad_gate_up, expert_in, preferred_element_type=single_precision
    ).astype(bf16)
    grad_back = lax.all_to_all(
        source_major(grad_rows_in, sources, capacity),
        "expert",
        split_axis=0,
        concat_axis=0,
        tiled=True,
    )
    chosen = (own_routes[:, :, None] == jnp.arange(experts, dtype=jnp.int32)[None, None, :]).astype(
        single_precision
    )
    grad_probs = jnp.sum(route_grad_weight[:, :, None] * chosen, axis=1)
    grad_logits = (
        router_probs * (grad_probs - jnp.sum(router_probs * grad_probs, axis=-1, keepdims=True))
    ).astype(bf16)
    grad_router = jnp.einsum(
        "td,te->de", ffn_in, grad_logits, preferred_element_type=single_precision
    )
    grad_ffn_in, _ = combine(
        route_slots,
        jnp.ones((seq_tok, top), single_precision),
        grad_back.reshape(experts * capacity, width),
        jnp.einsum("te,de->td", grad_logits, router_weight, preferred_element_type=single_precision),
        grad_output[0],
        False,
    )
    grad_mid_norm, grad_ffn_gain = rms_backward(grad_ffn_in, normed2, factor2, ffn_gain)
    grad_mid = grad + grad_mid_norm
    grad_mid_b = grad_mid.astype(bf16)
    grad_att = (
        jnp.einsum("td,dq->tq", grad_mid_b, out_full, preferred_element_type=single_precision)
        .astype(bf16)
        .reshape(seq_tok, heads, head_dim)
    )
    delta = jnp.sum(
        grad_att.astype(single_precision)
        * attended.reshape(seq_tok, heads, head_dim).astype(single_precision),
        axis=-1,
    )
    probs = jnp.exp(masked_scores() - lse)
    grad_vals = jnp.einsum(
        "hqk,qhd->khd", probs.astype(bf16), grad_att, preferred_element_type=single_precision
    )
    grad_p = jnp.einsum("qhd,khd->hqk", grad_att, vals3, preferred_element_type=single_precision)
    grad_scores = (probs * (grad_p - delta.T[:, :, None])).astype(bf16)
    grad_queries = (
        jnp.einsum("hqk,khd->qhd", grad_scores, keys3, preferred_element_type=single_precision)
        * scale
    )
    grad_keys_all = (
        jnp.einsum("hqk,qhd->khd", grad_scores, queries, preferred_element_type=single_precision)
        * scale
    )
    grad_keys_values = sum_context_halves(
        jnp.stack(
            [grad_keys_all.reshape(seq_len, heads_width), grad_vals.reshape(seq_len, heads_width)],
            axis=1,
        )
    )
    grad_keys = grad_keys_values[:, 0]
    grad_values = grad_keys_values[:, 1]
    grad_qn = rotate(grad_queries, cosine, sine, -1.0).reshape(seq_tok, heads_width)
    grad_kn = rotate(grad_keys.reshape(seq_tok, heads, head_dim), cosine, sine, -1.0).reshape(
        seq_tok, heads_width
    )
    grad_q_raw, grad_q_gain = rms_backward(grad_qn, q_normed, q_factor, q_gain)
    grad_k_raw, grad_k_gain = rms_backward(grad_kn, k_normed, k_factor, k_gain)
    projected_gradient = jnp.stack(
        [grad_q_raw, grad_k_raw, grad_values, jnp.zeros_like(grad_values)], axis=1
    ).astype(bf16)
    attention_input_gradient = jnp.dot(
        projected_gradient.reshape(seq_tok, 4 * heads_width),
        weights_full.reshape(width, 4 * heads_width).T,
        preferred_element_type=single_precision,
    )
    grad_x_norm, grad_attn_gain = rms_backward(
        attention_input_gradient, normed1, factor1, attn_gain
    )
    grad_tokens = grad_mid + grad_x_norm
    def scatter_over_copies(values):
        return sum_halves(sum_halves(values, "dp", 1), "context", 1)

    grad_in_shard = scatter_over_copies(grad_gate_up_w[0])[None]
    grad_down_shard = scatter_over_copies(grad_down[0])[None]
    left = jnp.stack([attention_input] * 3 + [grad_mid_b])
    right = jnp.concatenate(
        [projected_gradient[:, :3].transpose(1, 0, 2), attended[None]], axis=0
    )
    stacked = jnp.einsum("sta,stb->sab", left, right, preferred_element_type=single_precision)
    summed = lax.psum(stacked.astype(bf16), all_axes)
    shard_rows = width // lax.axis_size(all_axes)
    start = lax.axis_index(all_axes) * shard_rows
    weight_shard = lax.dynamic_slice_in_dim(summed, start, shard_rows, axis=1).astype(
        single_precision
    )
    grad_qkv_shard = weight_shard[:3]
    grad_out_shard = weight_shard[3]
    small_sum = butterfly_sum(
        jnp.concatenate(
            [grad_attn_gain, grad_q_gain, grad_k_gain, grad_ffn_gain, grad_router.reshape(-1)]
        ),
        all_axes,
    )
    sizes = [width, heads_width, heads_width, width, width * experts]
    offsets = [sum(sizes[:n]) for n in range(len(sizes))]
    totals = [small_sum[o : o + n] for o, n in zip(offsets, sizes)]
    totals[4] = totals[4].reshape(width, experts)
    return (
        output[None],
        grad_tokens[None],
        totals[0],
        totals[1],
        totals[2],
        totals[3],
        totals[4],
        grad_qkv_shard,
        grad_out_shard,
        grad_in_shard,
        grad_down_shard,
    )


def solution(mesh):
    return jax.shard_map(
        body,
        mesh=mesh,
        in_specs=(
            P(("dp", "expert"), "context", None),
            P(("dp", "expert"), "context", None),
            P(("dp", "expert"), "context", None),
            P(("dp", "expert"), None),
            P(),
            P(),
            P(),
            P(),
            P(None, ("dp", "context", "expert"), None),
            P(("dp", "context", "expert"), None),
            P(),
            P("expert", None, None, None),
            P("expert", None, None),
        ),
        out_specs=(
            P(("dp", "expert"), "context", None),
            P(("dp", "expert"), "context", None),
            P(),
            P(),
            P(),
            P(),
            P(),
            P(None, ("dp", "context", "expert"), None),
            P(("dp", "context", "expert"), None),
            P("expert", None, ("dp", "context"), None),
            P("expert", None, ("dp", "context")),
        ),
        check_vma=False,
    )
```

```python
import functools

import jax
import jax.numpy as jnp
from jax import lax
from jax.experimental import pallas as pl
from jax.experimental.pallas import tpu as pltpu
from jax.sharding import PartitionSpec as P

HDIM = 128


EPS = 1e-05
THETA = 10000.0


def rope_tables(places, head_dim):
    half = head_dim // 2
    freq = THETA ** (-jnp.arange(half, dtype=jnp.float32) * 2.0 / head_dim)
    angle = places.astype(jnp.float32)[:, None] * freq[None, :]
    return (jnp.cos(angle), jnp.sin(angle))


def rotate(values, cosine, sine, sign):
    half = values.shape[-1] // 2
    first = values[..., :half]
    second = values[..., half:]
    cosine = cosine[:, None, :]
    sine = sign * sine[:, None, :]
    return jnp.concatenate(
        [first * cosine - second * sine, second * cosine + first * sine], axis=-1
    )


def rms_forward(values):
    factor = lax.rsqrt(jnp.mean(values * values, axis=-1, keepdims=True) + EPS)
    return (values * factor, factor)


def rms_backward(grad_out, normed, factor, gain):
    scaled = grad_out * gain
    grad_in = factor * (scaled - normed * jnp.mean(scaled * normed, axis=-1, keepdims=True))
    return (grad_in, jnp.sum(grad_out * normed, axis=0))


def slot_index(route_rows, experts, capacity):
    onehot = (route_rows[:, None] == jnp.arange(experts, dtype=jnp.int32)[None, :]).astype(
        jnp.int32
    )
    count = route_rows.shape[0]
    earlier = (
        jnp.arange(count, dtype=jnp.int32)[None, :] < jnp.arange(count, dtype=jnp.int32)[:, None]
    ).astype(jnp.bfloat16)
    before = jnp.dot(earlier, onehot.astype(jnp.bfloat16), preferred_element_type=jnp.float32)
    return route_rows * capacity + jnp.sum(before.astype(jnp.int32) * onehot, axis=1)


def expert_major(received, local_experts, capacity):
    sources, _, width = received.shape
    return (
        received.reshape(sources, local_experts, capacity, width)
        .transpose(1, 0, 2, 3)
        .reshape(local_experts, sources * capacity, width)
    )


def source_major(results, sources, capacity):
    local_experts, _, width = results.shape
    return (
        results.reshape(local_experts, sources, capacity, width)
        .transpose(1, 0, 2, 3)
        .reshape(sources, local_experts * capacity, width)
    )


def _project_kernel(inputs_ref, weights_ref, out_ref):
    out_ref[0] = jnp.dot(inputs_ref[...], weights_ref[0], preferred_element_type=jnp.float32)


def project(inputs, weights, blocks, tile=512):
    tokens, depth = inputs.shape
    columns = weights.shape[2]
    return pl.pallas_call(
        _project_kernel,
        out_shape=jax.ShapeDtypeStruct((blocks, tokens, columns), jnp.float32),
        grid=(blocks, columns // tile),
        in_specs=[
            pl.BlockSpec((tokens, depth), lambda s, j: (0, 0)),
            pl.BlockSpec((1, depth, tile), lambda s, j: (s, 0, j)),
        ],
        out_specs=pl.BlockSpec((1, tokens, tile), lambda s, j: (s, 0, j)),
        cost_estimate=pl.CostEstimate(
            flops=2 * tokens * depth * columns * blocks,
            transcendentals=0,
            bytes_accessed=2 * depth * columns * blocks + 2 * tokens * depth
            + 4 * tokens * columns * blocks,
        ),
    )(inputs, weights)


def _dispatch_kernel(slot_ref, weight_ref, rows_ref, grad_ref, send_ref, grad_send_ref):
    tile = send_ref.shape[0]
    top, tokens = slot_ref.shape
    slot = pl.program_id(0) * tile + lax.broadcasted_iota(jnp.int32, (tile, tokens), 0)
    hit = slot == slot_ref[0:1, :]
    weight = jnp.where(hit, weight_ref[0:1, :], 0.0)
    for k in range(1, top):
        match = slot == slot_ref[k : k + 1, :]
        hit = hit | match
        weight = weight + jnp.where(match, weight_ref[k : k + 1, :], 0.0)
    pick = hit.astype(jnp.bfloat16)
    send_ref[...] = jnp.dot(pick, rows_ref[...], preferred_element_type=jnp.float32).astype(
        send_ref.dtype
    )
    picked_grad = jnp.dot(pick, grad_ref[...], preferred_element_type=jnp.float32)
    slot_weight = jnp.sum(weight, axis=1, keepdims=True)
    grad_send_ref[...] = (slot_weight * picked_grad).astype(grad_send_ref.dtype)


def dispatch(route_slots, route_weights, rows, grad, slots, tile=256):
    top, tokens = route_slots.shape
    width = rows.shape[1]
    out = jax.ShapeDtypeStruct((slots, width), jnp.bfloat16)
    return pl.pallas_call(
        _dispatch_kernel,
        out_shape=(out, out),
        grid=(slots // tile,),
        in_specs=[
            pl.BlockSpec((top, tokens), lambda i: (0, 0)),
            pl.BlockSpec((top, tokens), lambda i: (0, 0)),
            pl.BlockSpec((tokens, width), lambda i: (0, 0)),
            pl.BlockSpec((tokens, width), lambda i: (0, 0)),
        ],
        out_specs=(
            pl.BlockSpec((tile, width), lambda i: (i, 0)),
            pl.BlockSpec((tile, width), lambda i: (i, 0)),
        ),
        cost_estimate=pl.CostEstimate(
            flops=4 * slots * tokens * width,
            transcendentals=0,
            bytes_accessed=4 * slots * width + 4 * tokens * width + 8 * top * tokens,
        ),
    )(route_slots, route_weights, rows, grad)


def _combine_kernel(with_dots, slot_ref, weight_ref, table_ref, base_ref, other_ref, out_ref, dots_ref):
    tokens, top = slot_ref.shape
    count = table_ref.shape[0]
    total = base_ref[...]
    for k in range(top):
        pick = (
            slot_ref[:, k : k + 1] == lax.broadcasted_iota(jnp.int32, (tokens, count), 1)
        ).astype(jnp.bfloat16)
        row = jnp.dot(pick, table_ref[...], preferred_element_type=jnp.float32)
        total = total + weight_ref[:, k : k + 1] * row
        if with_dots:
            dots_ref[:, k : k + 1] = jnp.sum(
                other_ref[...].astype(jnp.float32) * row, axis=1, keepdims=True
            )
    out_ref[...] = total
    if not with_dots:
        dots_ref[...] = jnp.zeros_like(dots_ref)


def combine(slots, weights, table, base, other, with_dots):
    tokens, top = slots.shape
    count, width = table.shape
    return pl.pallas_call(
        functools.partial(_combine_kernel, with_dots),
        out_shape=(
            jax.ShapeDtypeStruct((tokens, width), jnp.float32),
            jax.ShapeDtypeStruct((tokens, top), jnp.float32),
        ),
        in_specs=[pl.BlockSpec(memory_space=pltpu.VMEM)] * 5,
        out_specs=(pl.BlockSpec(memory_space=pltpu.VMEM), pl.BlockSpec(memory_space=pltpu.VMEM)),
        cost_estimate=pl.CostEstimate(
            flops=2 * tokens * count * width * top,
            transcendentals=0,
            bytes_accessed=2 * count * width + 10 * tokens * width,
        ),
    )(slots, weights, table, base, other)


def sum_halves(values, axis, dim):
    half = values.shape[dim] // 2
    index = lax.axis_index(axis)
    own = lax.dynamic_slice_in_dim(values, index * half, half, axis=dim)
    given = lax.dynamic_slice_in_dim(values, (1 - index) * half, half, axis=dim)
    received = lax.ppermute(given.astype(jnp.bfloat16), axis, [(0, 1), (1, 0)])
    return own + received.astype(own.dtype)


def swap_context(values):
    return lax.ppermute(values, "context", [(0, 1), (1, 0)])


def gather_context(values):
    other = swap_context(values)
    first = lax.axis_index("context") == 0
    return jnp.concatenate(
        [jnp.where(first, values, other), jnp.where(first, other, values)], axis=0
    )


def sum_context_halves(values):
    half = values.shape[0] // 2
    first = lax.axis_index("context") == 0
    own = jnp.where(first, values[:half], values[half:])
    given = jnp.where(first, values[half:], values[:half]).astype(jnp.bfloat16)
    return own + swap_context(given).astype(own.dtype)


def butterfly_sum(values, axes):
    index = lax.axis_index(axes)
    count = 1
    for name in axes:
        count *= lax.axis_size(name)
    step = 1
    while step < count:
        partner = [(i, i ^ step) for i in range(count)]
        received = lax.ppermute(values, axes, partner)
        mine_first = (index & step) == 0
        values = jnp.where(mine_first, values + received, received + values)
        step *= 2
    return values


def body(
    tokens,
    grad_output,
    routes,
    positions,
    attn_gain,
    q_gain,
    k_gain,
    ffn_gain,
    qkv_weight,
    out_weight,
    router_weight,
    expert_in,
    expert_out,
):
    single_precision = jnp.float32
    bf16 = jnp.bfloat16
    seq_tok = tokens.shape[1]
    width = tokens.shape[2]
    top = routes.shape[2]
    heads_width = out_weight.shape[1]
    head_dim = HDIM
    heads = heads_width // head_dim
    local_experts = expert_in.shape[0]
    experts = router_weight.shape[1]
    sources = lax.axis_size("expert")
    capacity = min(seq_tok, seq_tok * top * 5 // (4 * experts))
    scale = head_dim ** (-0.5)
    x = tokens[0].astype(single_precision)
    normed1, factor1 = rms_forward(x)
    attention_input = (normed1 * attn_gain).astype(bf16)
    all_axes = ("dp", "context", "expert")
    weights_full = lax.all_gather(
        jnp.concatenate([qkv_weight.transpose(1, 0, 2), out_weight[:, None, :]], axis=1),
        all_axes,
        axis=0,
        tiled=True,
    )
    out_full = weights_full[:, 3, :]
    projected_output = project(attention_input, weights_full.transpose(1, 0, 2), 3)
    q_normed, q_factor = rms_forward(projected_output[0])
    k_normed, k_factor = rms_forward(projected_output[1])
    values = projected_output[2].astype(bf16)
    all_places = positions[0]
    own_places = lax.dynamic_slice_in_dim(all_places, lax.axis_index("context") * seq_tok, seq_tok)
    cosine, sine = rope_tables(own_places, head_dim)
    queries = rotate(
        (q_normed * q_gain).reshape(seq_tok, heads, head_dim), cosine, sine, 1.0
    ).astype(bf16)
    own_keys = rotate(
        (k_normed * k_gain).reshape(seq_tok, heads, head_dim), cosine, sine, 1.0
    ).astype(bf16)
    keys_vals = gather_context(
        jnp.stack([own_keys.reshape(seq_tok, heads_width), values], axis=1)
    )
    keys = keys_vals[:, 0]
    vals = keys_vals[:, 1]
    seq_len = keys.shape[0]
    keys3 = keys.reshape(seq_len, heads, head_dim)
    vals3 = vals.reshape(seq_len, heads, head_dim)
    allowed = (all_places[None, :] <= own_places[:, None])[None]

    def masked_scores():
        scores = (
            jnp.einsum("qhd,khd->hqk", queries, keys3, preferred_element_type=single_precision)
            * scale
        )
        return jnp.where(allowed, scores, -jnp.inf)

    scores = masked_scores()
    lse = jnp.log(jnp.sum(jnp.exp(scores), axis=-1, keepdims=True))
    probs_b = jnp.exp(scores - lse).astype(bf16)
    attended = (
        jnp.einsum("hqk,khd->qhd", probs_b, vals3, preferred_element_type=single_precision)
        .astype(bf16)
        .reshape(seq_tok, heads_width)
    )
    mid = x + jnp.einsum("tq,dq->td", attended, out_full, preferred_element_type=single_precision)
    normed2, factor2 = rms_forward(mid)
    ffn_in = (normed2 * ffn_gain).astype(bf16)
    router_exp = jnp.exp(jnp.dot(ffn_in, router_weight, preferred_element_type=single_precision))
    router_probs = router_exp / jnp.sum(router_exp, axis=-1, keepdims=True)
    own_routes = routes[0]
    slots = slot_index(own_routes.reshape(-1), experts, capacity)
    expert_ids = jnp.arange(experts, dtype=jnp.int32)
    route_weight = jnp.sum(
        jnp.where(own_routes[:, :, None] == expert_ids, router_probs[:, None, :], 0.0), axis=2
    )
    route_slots = slots.reshape(seq_tok, top)
    send, grad_send = dispatch(
        route_slots.T, route_weight.T, ffn_in, grad_output[0], experts * capacity
    )
    received = lax.all_to_all(
        send.reshape(sources, local_experts * capacity, width),
        "expert",
        split_axis=0,
        concat_axis=0,
        tiled=True,
    )
    rows = expert_major(received, local_experts, capacity)
    gate_up = jnp.einsum("lrd,lkdh->lkrh", rows, expert_in, preferred_element_type=single_precision)
    gate = gate_up[:, 0]
    up = gate_up[:, 1]
    sig = jax.nn.sigmoid(gate)
    hidden = (gate * sig * up).astype(bf16)
    results = jnp.einsum(
        "lrh,lhd->lrd", hidden, expert_out, preferred_element_type=single_precision
    ).astype(bf16)
    back = lax.all_to_all(
        source_major(results, sources, capacity), "expert", split_axis=0, concat_axis=0, tiled=True
    )
    output, route_grad_weight = combine(
        route_slots,
        route_weight,
        back.reshape(experts * capacity, width),
        mid,
        grad_output[0],
        True,
    )
    grad = grad_output[0].astype(single_precision)
    grad_received = lax.all_to_all(
        grad_send.reshape(sources, local_experts * capacity, width),
        "expert",
        split_axis=0,
        concat_axis=0,
        tiled=True,
    )
    grad_rows = expert_major(grad_received, local_experts, capacity)
    grad_hidden = jnp.einsum(
        "lrd,lhd->lrh", grad_rows, expert_out, preferred_element_type=single_precision
    )
    grad_down = jnp.einsum(
        "lrh,lrd->lhd", hidden, grad_rows, preferred_element_type=single_precision
    )
    grad_gate = (grad_hidden * up * sig * (1.0 + gate * (1.0 - sig))).astype(bf16)
    grad_up = (grad_hidden * gate * sig).astype(bf16)
    grad_gate_up = jnp.stack([grad_gate, grad_up], axis=1)
    grad_gate_up_w = jnp.einsum(
        "lrd,lkrh->lkdh", rows, grad_gate_up, preferred_element_type=single_precision
    )
    grad_rows_in = jnp.einsum(
        "lkrh,lkdh->lrd", grad_gate_up, expert_in, preferred_element_type=single_precision
    ).astype(bf16)
    grad_back = lax.all_to_all(
        source_major(grad_rows_in, sources, capacity),
        "expert",
        split_axis=0,
        concat_axis=0,
        tiled=True,
    )
    chosen = (own_routes[:, :, None] == jnp.arange(experts, dtype=jnp.int32)[None, None, :]).astype(
        single_precision
    )
    grad_probs = jnp.sum(route_grad_weight[:, :, None] * chosen, axis=1)
    grad_logits = (
        router_probs * (grad_probs - jnp.sum(router_probs * grad_probs, axis=-1, keepdims=True))
    ).astype(bf16)
    grad_router = jnp.einsum(
        "td,te->de", ffn_in, grad_logits, preferred_element_type=single_precision
    )
    grad_ffn_in, _ = combine(
        route_slots,
        jnp.ones((seq_tok, top), single_precision),
        grad_back.reshape(experts * capacity, width),
        jnp.einsum("te,de->td", grad_logits, router_weight, preferred_element_type=single_precision),
        grad_output[0],
        False,
    )
    grad_mid_norm, grad_ffn_gain = rms_backward(grad_ffn_in, normed2, factor2, ffn_gain)
    grad_mid = grad + grad_mid_norm
    grad_mid_b = grad_mid.astype(bf16)
    grad_att = (
        jnp.einsum("td,dq->tq", grad_mid_b, out_full, preferred_element_type=single_precision)
        .astype(bf16)
        .reshape(seq_tok, heads, head_dim)
    )
    delta = jnp.sum(
        grad_att.astype(single_precision)
        * attended.reshape(seq_tok, heads, head_dim).astype(single_precision),
        axis=-1,
    )
    probs = jnp.exp(masked_scores() - lse)
    grad_vals = jnp.einsum(
        "hqk,qhd->khd", probs.astype(bf16), grad_att, preferred_element_type=single_precision
    )
    grad_p = jnp.einsum("qhd,khd->hqk", grad_att, vals3, preferred_element_type=single_precision)
    grad_scores = (probs * (grad_p - delta.T[:, :, None])).astype(bf16)
    grad_queries = (
        jnp.einsum("hqk,khd->qhd", grad_scores, keys3, preferred_element_type=single_precision)
        * scale
    )
    grad_keys_all = (
        jnp.einsum("hqk,qhd->khd", grad_scores, queries, preferred_element_type=single_precision)
        * scale
    )
    grad_keys_values = sum_context_halves(
        jnp.stack(
            [grad_keys_all.reshape(seq_len, heads_width), grad_vals.reshape(seq_len, heads_width)],
            axis=1,
        )
    )
    grad_keys = grad_keys_values[:, 0]
    grad_values = grad_keys_values[:, 1]
    grad_qn = rotate(grad_queries, cosine, sine, -1.0).reshape(seq_tok, heads_width)
    grad_kn = rotate(grad_keys.reshape(seq_tok, heads, head_dim), cosine, sine, -1.0).reshape(
        seq_tok, heads_width
    )
    grad_q_raw, grad_q_gain = rms_backward(grad_qn, q_normed, q_factor, q_gain)
    grad_k_raw, grad_k_gain = rms_backward(grad_kn, k_normed, k_factor, k_gain)
    projected_gradient = jnp.stack(
        [grad_q_raw, grad_k_raw, grad_values, jnp.zeros_like(grad_values)], axis=1
    ).astype(bf16)
    attention_input_gradient = jnp.dot(
        projected_gradient.reshape(seq_tok, 4 * heads_width),
        weights_full.reshape(width, 4 * heads_width).T,
        preferred_element_type=single_precision,
    )
    grad_x_norm, grad_attn_gain = rms_backward(
        attention_input_gradient, normed1, factor1, attn_gain
    )
    grad_tokens = grad_mid + grad_x_norm
    def scatter_over_copies(values):
        return sum_halves(sum_halves(values, "dp", 1), "context", 1)

    grad_in_shard = scatter_over_copies(grad_gate_up_w[0])[None]
    grad_down_shard = scatter_over_copies(grad_down[0])[None]
    left = jnp.stack([attention_input] * 3 + [grad_mid_b])
    right = jnp.concatenate(
        [projected_gradient[:, :3].transpose(1, 0, 2), attended[None]], axis=0
    )
    stacked = jnp.einsum("sta,stb->sab", left, right, preferred_element_type=single_precision)
    summed = lax.psum(stacked.astype(bf16), all_axes)
    shard_rows = width // lax.axis_size(all_axes)
    start = lax.axis_index(all_axes) * shard_rows
    weight_shard = lax.dynamic_slice_in_dim(summed, start, shard_rows, axis=1).astype(
        single_precision
    )
    grad_qkv_shard = weight_shard[:3]
    grad_out_shard = weight_shard[3]
    small_sum = butterfly_sum(
        jnp.concatenate(
            [grad_attn_gain, grad_q_gain, grad_k_gain, grad_ffn_gain, grad_router.reshape(-1)]
        ),
        all_axes,
    )
    sizes = [width, heads_width, heads_width, width, width * experts]
    offsets = [sum(sizes[:n]) for n in range(len(sizes))]
    totals = [small_sum[o : o + n] for o, n in zip(offsets, sizes)]
    totals[4] = totals[4].reshape(width, experts)
    return (
        output[None],
        grad_tokens[None],
        totals[0],
        totals[1],
        totals[2],
        totals[3],
        totals[4],
        grad_qkv_shard,
        grad_out_shard,
        grad_in_shard,
        grad_down_shard,
    )


def solution(mesh):
    return jax.shard_map(
        body,
        mesh=mesh,
        in_specs=(
            P(("dp", "expert"), "context", None),
            P(("dp", "expert"), "context", None),
            P(("dp", "expert"), "context", None),
            P(("dp", "expert"), None),
            P(),
            P(),
            P(),
            P(),
            P(None, ("dp", "context", "expert"), None),
            P(("dp", "context", "expert"), None),
            P(),
            P("expert", None, None, None),
            P("expert", None, None),
        ),
        out_specs=(
            P(("dp", "expert"), "context", None),
            P(("dp", "expert"), "context", None),
            P(),
            P(),
            P(),
            P(),
            P(),
            P(None, ("dp", "context", "expert"), None),
            P(("dp", "context", "expert"), None),
            P("expert", None, ("dp", "context"), None),
            P("expert", None, ("dp", "context")),
        ),
        check_vma=False,
    )
```

```python
import functools

import jax
import jax.numpy as jnp
from jax import lax
from jax.experimental import pallas as pl
from jax.experimental.pallas import tpu as pltpu
from jax.sharding import PartitionSpec as P

HDIM = 128


EPS = 1e-05
THETA = 10000.0


def rope_tables(places, head_dim):
    half = head_dim // 2
    freq = THETA ** (-jnp.arange(half, dtype=jnp.float32) * 2.0 / head_dim)
    angle = places.astype(jnp.float32)[:, None] * freq[None, :]
    return (jnp.cos(angle), jnp.sin(angle))


def rotate(values, cosine, sine, sign):
    half = values.shape[-1] // 2
    first = values[..., :half]
    second = values[..., half:]
    cosine = cosine[:, None, :]
    sine = sign * sine[:, None, :]
    return jnp.concatenate(
        [first * cosine - second * sine, second * cosine + first * sine], axis=-1
    )


def rms_forward(values):
    factor = lax.rsqrt(jnp.mean(values * values, axis=-1, keepdims=True) + EPS)
    return (values * factor, factor)


def rms_backward(grad_out, normed, factor, gain):
    scaled = grad_out * gain
    grad_in = factor * (scaled - normed * jnp.mean(scaled * normed, axis=-1, keepdims=True))
    return (grad_in, jnp.sum(grad_out * normed, axis=0))


def slot_index(route_rows, experts, capacity):
    onehot = (route_rows[:, None] == jnp.arange(experts, dtype=jnp.int32)[None, :]).astype(
        jnp.int32
    )
    count = route_rows.shape[0]
    earlier = (
        jnp.arange(count, dtype=jnp.int32)[None, :] < jnp.arange(count, dtype=jnp.int32)[:, None]
    ).astype(jnp.bfloat16)
    before = jnp.dot(earlier, onehot.astype(jnp.bfloat16), preferred_element_type=jnp.float32)
    return route_rows * capacity + jnp.sum(before.astype(jnp.int32) * onehot, axis=1)


def expert_major(received, local_experts, capacity):
    sources, _, width = received.shape
    return (
        received.reshape(sources, local_experts, capacity, width)
        .transpose(1, 0, 2, 3)
        .reshape(local_experts, sources * capacity, width)
    )


def source_major(results, sources, capacity):
    local_experts, _, width = results.shape
    return (
        results.reshape(local_experts, sources, capacity, width)
        .transpose(1, 0, 2, 3)
        .reshape(sources, local_experts * capacity, width)
    )


def _project_kernel(inputs_ref, weights_ref, out_ref):
    out_ref[0] = jnp.dot(inputs_ref[...], weights_ref[0], preferred_element_type=jnp.float32)


def project(inputs, weights, blocks, tile=512):
    tokens, depth = inputs.shape
    columns = weights.shape[2]
    return pl.pallas_call(
        _project_kernel,
        out_shape=jax.ShapeDtypeStruct((blocks, tokens, columns), jnp.float32),
        grid=(blocks, columns // tile),
        in_specs=[
            pl.BlockSpec((tokens, depth), lambda s, j: (0, 0)),
            pl.BlockSpec((1, depth, tile), lambda s, j: (s, 0, j)),
        ],
        out_specs=pl.BlockSpec((1, tokens, tile), lambda s, j: (s, 0, j)),
        cost_estimate=pl.CostEstimate(
            flops=2 * tokens * depth * columns * blocks,
            transcendentals=0,
            bytes_accessed=2 * depth * columns * blocks + 2 * tokens * depth
            + 4 * tokens * columns * blocks,
        ),
    )(inputs, weights)


def _dispatch_kernel(scaled, slot_ref, weight_ref, rows_ref, send_ref):
    tile = send_ref.shape[0]
    top, tokens = slot_ref.shape
    slot = pl.program_id(0) * tile + lax.broadcasted_iota(jnp.int32, (tile, tokens), 0)
    hit = slot == slot_ref[0:1, :]
    weight = jnp.where(hit, weight_ref[0:1, :], 0.0)
    for k in range(1, top):
        match = slot == slot_ref[k : k + 1, :]
        hit = hit | match
        weight = weight + jnp.where(match, weight_ref[k : k + 1, :], 0.0)
    picked = jnp.dot(hit.astype(jnp.bfloat16), rows_ref[...], preferred_element_type=jnp.float32)
    if scaled:
        picked = jnp.sum(weight, axis=1, keepdims=True) * picked
    send_ref[...] = picked.astype(send_ref.dtype)


def dispatch(route_slots, route_weights, rows, slots, scaled, tile=256):
    top, tokens = route_slots.shape
    width = rows.shape[1]
    return pl.pallas_call(
        functools.partial(_dispatch_kernel, scaled),
        out_shape=jax.ShapeDtypeStruct((slots, width), jnp.bfloat16),
        grid=(slots // tile,),
        in_specs=[
            pl.BlockSpec((top, tokens), lambda i: (0, 0)),
            pl.BlockSpec((top, tokens), lambda i: (0, 0)),
            pl.BlockSpec((tokens, width), lambda i: (0, 0)),
        ],
        out_specs=pl.BlockSpec((tile, width), lambda i: (i, 0)),
        cost_estimate=pl.CostEstimate(
            flops=2 * slots * tokens * width,
            transcendentals=0,
            bytes_accessed=2 * slots * width + 2 * tokens * width + 8 * top * tokens,
        ),
    )(route_slots, route_weights, rows)


def _combine_kernel(with_dots, slot_ref, weight_ref, table_ref, base_ref, other_ref, out_ref, dots_ref):
    tokens, top = slot_ref.shape
    count = table_ref.shape[0]
    total = base_ref[...]
    for k in range(top):
        pick = (
            slot_ref[:, k : k + 1] == lax.broadcasted_iota(jnp.int32, (tokens, count), 1)
        ).astype(jnp.bfloat16)
        row = jnp.dot(pick, table_ref[...], preferred_element_type=jnp.float32)
        total = total + weight_ref[:, k : k + 1] * row
        if with_dots:
            dots_ref[:, k : k + 1] = jnp.sum(
                other_ref[...].astype(jnp.float32) * row, axis=1, keepdims=True
            )
    out_ref[...] = total
    if not with_dots:
        dots_ref[...] = jnp.zeros_like(dots_ref)


def combine(slots, weights, table, base, other, with_dots):
    tokens, top = slots.shape
    count, width = table.shape
    return pl.pallas_call(
        functools.partial(_combine_kernel, with_dots),
        out_shape=(
            jax.ShapeDtypeStruct((tokens, width), jnp.float32),
            jax.ShapeDtypeStruct((tokens, top), jnp.float32),
        ),
        in_specs=[pl.BlockSpec(memory_space=pltpu.VMEM)] * 5,
        out_specs=(pl.BlockSpec(memory_space=pltpu.VMEM), pl.BlockSpec(memory_space=pltpu.VMEM)),
        cost_estimate=pl.CostEstimate(
            flops=2 * tokens * count * width * top,
            transcendentals=0,
            bytes_accessed=2 * count * width + 10 * tokens * width,
        ),
    )(slots, weights, table, base, other)


def sum_halves(values, axis, dim):
    half = values.shape[dim] // 2
    index = lax.axis_index(axis)
    own = lax.dynamic_slice_in_dim(values, index * half, half, axis=dim)
    given = lax.dynamic_slice_in_dim(values, (1 - index) * half, half, axis=dim)
    received = lax.ppermute(given.astype(jnp.bfloat16), axis, [(0, 1), (1, 0)])
    return own + received.astype(own.dtype)


def swap_context(values):
    return lax.ppermute(values, "context", [(0, 1), (1, 0)])


def gather_context(values):
    other = swap_context(values)
    first = lax.axis_index("context") == 0
    return jnp.concatenate(
        [jnp.where(first, values, other), jnp.where(first, other, values)], axis=0
    )


def sum_context_halves(values):
    half = values.shape[0] // 2
    first = lax.axis_index("context") == 0
    own = jnp.where(first, values[:half], values[half:])
    given = jnp.where(first, values[half:], values[:half]).astype(jnp.bfloat16)
    return own + swap_context(given).astype(own.dtype)


def butterfly_sum(values, axes):
    index = lax.axis_index(axes)
    count = 1
    for name in axes:
        count *= lax.axis_size(name)
    step = 1
    while step < count:
        partner = [(i, i ^ step) for i in range(count)]
        received = lax.ppermute(values, axes, partner)
        mine_first = (index & step) == 0
        values = jnp.where(mine_first, values + received, received + values)
        step *= 2
    return values


def body(
    tokens,
    grad_output,
    routes,
    positions,
    attn_gain,
    q_gain,
    k_gain,
    ffn_gain,
    qkv_weight,
    out_weight,
    router_weight,
    expert_in,
    expert_out,
):
    single_precision = jnp.float32
    bf16 = jnp.bfloat16
    seq_tok = tokens.shape[1]
    width = tokens.shape[2]
    top = routes.shape[2]
    heads_width = out_weight.shape[1]
    head_dim = HDIM
    heads = heads_width // head_dim
    local_experts = expert_in.shape[0]
    experts = router_weight.shape[1]
    sources = lax.axis_size("expert")
    capacity = min(seq_tok, seq_tok * top * 5 // (4 * experts))
    scale = head_dim ** (-0.5)
    x = tokens[0].astype(single_precision)
    normed1, factor1 = rms_forward(x)
    attention_input = (normed1 * attn_gain).astype(bf16)
    all_axes = ("dp", "context", "expert")
    weights_full = lax.all_gather(
        jnp.concatenate([qkv_weight.transpose(1, 0, 2), out_weight[:, None, :]], axis=1),
        all_axes,
        axis=0,
        tiled=True,
    )
    out_full = weights_full[:, 3, :]
    projected_output = project(attention_input, weights_full.transpose(1, 0, 2), 3)
    q_normed, q_factor = rms_forward(projected_output[0])
    k_normed, k_factor = rms_forward(projected_output[1])
    values = projected_output[2].astype(bf16)
    all_places = positions[0]
    own_places = lax.dynamic_slice_in_dim(all_places, lax.axis_index("context") * seq_tok, seq_tok)
    cosine, sine = rope_tables(own_places, head_dim)
    queries = rotate(
        (q_normed * q_gain).reshape(seq_tok, heads, head_dim), cosine, sine, 1.0
    ).astype(bf16)
    own_keys = rotate(
        (k_normed * k_gain).reshape(seq_tok, heads, head_dim), cosine, sine, 1.0
    ).astype(bf16)
    keys_vals = gather_context(
        jnp.stack([own_keys.reshape(seq_tok, heads_width), values], axis=1)
    )
    keys = keys_vals[:, 0]
    vals = keys_vals[:, 1]
    seq_len = keys.shape[0]
    keys3 = keys.reshape(seq_len, heads, head_dim)
    vals3 = vals.reshape(seq_len, heads, head_dim)
    allowed = (all_places[None, :] <= own_places[:, None])[None]

    def masked_scores():
        scores = (
            jnp.einsum("qhd,khd->hqk", queries, keys3, preferred_element_type=single_precision)
            * scale
        )
        return jnp.where(allowed, scores, -jnp.inf)

    scores = masked_scores()
    lse = jnp.log(jnp.sum(jnp.exp(scores), axis=-1, keepdims=True))
    probs_b = jnp.exp(scores - lse).astype(bf16)
    attended = (
        jnp.einsum("hqk,khd->qhd", probs_b, vals3, preferred_element_type=single_precision)
        .astype(bf16)
        .reshape(seq_tok, heads_width)
    )
    mid = x + jnp.einsum("tq,dq->td", attended, out_full, preferred_element_type=single_precision)
    normed2, factor2 = rms_forward(mid)
    ffn_in = (normed2 * ffn_gain).astype(bf16)
    router_exp = jnp.exp(jnp.dot(ffn_in, router_weight, preferred_element_type=single_precision))
    router_probs = router_exp / jnp.sum(router_exp, axis=-1, keepdims=True)
    own_routes = routes[0]
    slots = slot_index(own_routes.reshape(-1), experts, capacity)
    expert_ids = jnp.arange(experts, dtype=jnp.int32)
    route_weight = jnp.sum(
        jnp.where(own_routes[:, :, None] == expert_ids, router_probs[:, None, :], 0.0), axis=2
    )
    route_slots = slots.reshape(seq_tok, top)
    send = dispatch(route_slots.T, route_weight.T, ffn_in, experts * capacity, False)
    grad_send = dispatch(route_slots.T, route_weight.T, grad_output[0], experts * capacity, True)
    received = lax.all_to_all(
        send.reshape(sources, local_experts * capacity, width),
        "expert",
        split_axis=0,
        concat_axis=0,
        tiled=True,
    )
    rows = expert_major(received, local_experts, capacity)
    gate_up = jnp.einsum("lrd,lkdh->lkrh", rows, expert_in, preferred_element_type=single_precision)
    gate = gate_up[:, 0]
    up = gate_up[:, 1]
    sig = jax.nn.sigmoid(gate)
    hidden = (gate * sig * up).astype(bf16)
    results = jnp.einsum(
        "lrh,lhd->lrd", hidden, expert_out, preferred_element_type=single_precision
    ).astype(bf16)
    back = lax.all_to_all(
        source_major(results, sources, capacity), "expert", split_axis=0, concat_axis=0, tiled=True
    )
    output, route_grad_weight = combine(
        route_slots,
        route_weight,
        back.reshape(experts * capacity, width),
        mid,
        grad_output[0],
        True,
    )
    grad = grad_output[0].astype(single_precision)
    grad_received = lax.all_to_all(
        grad_send.reshape(sources, local_experts * capacity, width),
        "expert",
        split_axis=0,
        concat_axis=0,
        tiled=True,
    )
    grad_rows = expert_major(grad_received, local_experts, capacity)
    grad_hidden = jnp.einsum(
        "lrd,lhd->lrh", grad_rows, expert_out, preferred_element_type=single_precision
    )
    grad_down = jnp.einsum(
        "lrh,lrd->lhd", hidden, grad_rows, preferred_element_type=single_precision
    )
    grad_gate = (grad_hidden * up * sig * (1.0 + gate * (1.0 - sig))).astype(bf16)
    grad_up = (grad_hidden * gate * sig).astype(bf16)
    grad_gate_up = jnp.stack([grad_gate, grad_up], axis=1)
    grad_gate_up_w = jnp.einsum(
        "lrd,lkrh->lkdh", rows, grad_gate_up, preferred_element_type=single_precision
    )
    grad_rows_in = jnp.einsum(
        "lkrh,lkdh->lrd", grad_gate_up, expert_in, preferred_element_type=single_precision
    ).astype(bf16)
    grad_back = lax.all_to_all(
        source_major(grad_rows_in, sources, capacity),
        "expert",
        split_axis=0,
        concat_axis=0,
        tiled=True,
    )
    chosen = (own_routes[:, :, None] == jnp.arange(experts, dtype=jnp.int32)[None, None, :]).astype(
        single_precision
    )
    grad_probs = jnp.sum(route_grad_weight[:, :, None] * chosen, axis=1)
    grad_logits = (
        router_probs * (grad_probs - jnp.sum(router_probs * grad_probs, axis=-1, keepdims=True))
    ).astype(bf16)
    grad_router = jnp.einsum(
        "td,te->de", ffn_in, grad_logits, preferred_element_type=single_precision
    )
    grad_ffn_in, _ = combine(
        route_slots,
        jnp.ones((seq_tok, top), single_precision),
        grad_back.reshape(experts * capacity, width),
        jnp.einsum("te,de->td", grad_logits, router_weight, preferred_element_type=single_precision),
        grad_output[0],
        False,
    )
    grad_mid_norm, grad_ffn_gain = rms_backward(grad_ffn_in, normed2, factor2, ffn_gain)
    grad_mid = grad + grad_mid_norm
    grad_mid_b = grad_mid.astype(bf16)
    grad_att = (
        jnp.einsum("td,dq->tq", grad_mid_b, out_full, preferred_element_type=single_precision)
        .astype(bf16)
        .reshape(seq_tok, heads, head_dim)
    )
    delta = jnp.sum(
        grad_att.astype(single_precision)
        * attended.reshape(seq_tok, heads, head_dim).astype(single_precision),
        axis=-1,
    )
    probs = jnp.exp(masked_scores() - lse)
    grad_vals = jnp.einsum(
        "hqk,qhd->khd", probs.astype(bf16), grad_att, preferred_element_type=single_precision
    )
    grad_p = jnp.einsum("qhd,khd->hqk", grad_att, vals3, preferred_element_type=single_precision)
    grad_scores = (probs * (grad_p - delta.T[:, :, None])).astype(bf16)
    grad_queries = (
        jnp.einsum("hqk,khd->qhd", grad_scores, keys3, preferred_element_type=single_precision)
        * scale
    )
    grad_keys_all = (
        jnp.einsum("hqk,qhd->khd", grad_scores, queries, preferred_element_type=single_precision)
        * scale
    )
    grad_keys_values = sum_context_halves(
        jnp.stack(
            [grad_keys_all.reshape(seq_len, heads_width), grad_vals.reshape(seq_len, heads_width)],
            axis=1,
        )
    )
    grad_keys = grad_keys_values[:, 0]
    grad_values = grad_keys_values[:, 1]
    grad_qn = rotate(grad_queries, cosine, sine, -1.0).reshape(seq_tok, heads_width)
    grad_kn = rotate(grad_keys.reshape(seq_tok, heads, head_dim), cosine, sine, -1.0).reshape(
        seq_tok, heads_width
    )
    grad_q_raw, grad_q_gain = rms_backward(grad_qn, q_normed, q_factor, q_gain)
    grad_k_raw, grad_k_gain = rms_backward(grad_kn, k_normed, k_factor, k_gain)
    projected_gradient = jnp.stack(
        [grad_q_raw, grad_k_raw, grad_values, jnp.zeros_like(grad_values)], axis=1
    ).astype(bf16)
    attention_input_gradient = jnp.dot(
        projected_gradient.reshape(seq_tok, 4 * heads_width),
        weights_full.reshape(width, 4 * heads_width).T,
        preferred_element_type=single_precision,
    )
    grad_x_norm, grad_attn_gain = rms_backward(
        attention_input_gradient, normed1, factor1, attn_gain
    )
    grad_tokens = grad_mid + grad_x_norm
    def scatter_over_copies(values):
        return sum_halves(sum_halves(values, "dp", 1), "context", 1)

    grad_in_shard = scatter_over_copies(grad_gate_up_w[0])[None]
    grad_down_shard = scatter_over_copies(grad_down[0])[None]
    left = jnp.stack([attention_input] * 3 + [grad_mid_b])
    right = jnp.concatenate(
        [projected_gradient[:, :3].transpose(1, 0, 2), attended[None]], axis=0
    )
    stacked = jnp.einsum("sta,stb->sab", left, right, preferred_element_type=single_precision)
    summed = lax.psum(stacked.astype(bf16), all_axes)
    shard_rows = width // lax.axis_size(all_axes)
    start = lax.axis_index(all_axes) * shard_rows
    weight_shard = lax.dynamic_slice_in_dim(summed, start, shard_rows, axis=1).astype(
        single_precision
    )
    grad_qkv_shard = weight_shard[:3]
    grad_out_shard = weight_shard[3]
    small_sum = butterfly_sum(
        jnp.concatenate(
            [grad_attn_gain, grad_q_gain, grad_k_gain, grad_ffn_gain, grad_router.reshape(-1)]
        ),
        all_axes,
    )
    sizes = [width, heads_width, heads_width, width, width * experts]
    offsets = [sum(sizes[:n]) for n in range(len(sizes))]
    totals = [small_sum[o : o + n] for o, n in zip(offsets, sizes)]
    totals[4] = totals[4].reshape(width, experts)
    return (
        output[None],
        grad_tokens[None],
        totals[0],
        totals[1],
        totals[2],
        totals[3],
        totals[4],
        grad_qkv_shard,
        grad_out_shard,
        grad_in_shard,
        grad_down_shard,
    )


def solution(mesh):
    return jax.shard_map(
        body,
        mesh=mesh,
        in_specs=(
            P(("dp", "expert"), "context", None),
            P(("dp", "expert"), "context", None),
            P(("dp", "expert"), "context", None),
            P(("dp", "expert"), None),
            P(),
            P(),
            P(),
            P(),
            P(None, ("dp", "context", "expert"), None),
            P(("dp", "context", "expert"), None),
            P(),
            P("expert", None, None, None),
            P("expert", None, None),
        ),
        out_specs=(
            P(("dp", "expert"), "context", None),
            P(("dp", "expert"), "context", None),
            P(),
            P(),
            P(),
            P(),
            P(),
            P(None, ("dp", "context", "expert"), None),
            P(("dp", "context", "expert"), None),
            P("expert", None, ("dp", "context"), None),
            P("expert", None, ("dp", "context")),
        ),
        check_vma=False,
    )
```

```python
import functools

import jax
import jax.numpy as jnp
from jax import lax
from jax.experimental import pallas as pl
from jax.experimental.pallas import tpu as pltpu
from jax.sharding import PartitionSpec as P

HDIM = 128


EPS = 1e-05
THETA = 10000.0


def rope_tables(places, head_dim):
    half = head_dim // 2
    freq = THETA ** (-jnp.arange(half, dtype=jnp.float32) * 2.0 / head_dim)
    angle = places.astype(jnp.float32)[:, None] * freq[None, :]
    return (jnp.cos(angle), jnp.sin(angle))


def rotate(values, cosine, sine, sign):
    half = values.shape[-1] // 2
    first = values[..., :half]
    second = values[..., half:]
    cosine = cosine[:, None, :]
    sine = sign * sine[:, None, :]
    return jnp.concatenate(
        [first * cosine - second * sine, second * cosine + first * sine], axis=-1
    )


def rms_forward(values):
    factor = lax.rsqrt(jnp.mean(values * values, axis=-1, keepdims=True) + EPS)
    return (values * factor, factor)


def rms_backward(grad_out, normed, factor, gain):
    scaled = grad_out * gain
    grad_in = factor * (scaled - normed * jnp.mean(scaled * normed, axis=-1, keepdims=True))
    return (grad_in, jnp.sum(grad_out * normed, axis=0))


def slot_index(route_rows, experts, capacity):
    onehot = (route_rows[:, None] == jnp.arange(experts, dtype=jnp.int32)[None, :]).astype(
        jnp.int32
    )
    count = route_rows.shape[0]
    earlier = (
        jnp.arange(count, dtype=jnp.int32)[None, :] < jnp.arange(count, dtype=jnp.int32)[:, None]
    ).astype(jnp.bfloat16)
    before = jnp.dot(earlier, onehot.astype(jnp.bfloat16), preferred_element_type=jnp.float32)
    return route_rows * capacity + jnp.sum(before.astype(jnp.int32) * onehot, axis=1)


def expert_major(received, local_experts, capacity):
    sources, _, width = received.shape
    return (
        received.reshape(sources, local_experts, capacity, width)
        .transpose(1, 0, 2, 3)
        .reshape(local_experts, sources * capacity, width)
    )


def source_major(results, sources, capacity):
    local_experts, _, width = results.shape
    return (
        results.reshape(local_experts, sources, capacity, width)
        .transpose(1, 0, 2, 3)
        .reshape(sources, local_experts * capacity, width)
    )


def _project_kernel(inputs_ref, weights_ref, out_ref):
    out_ref[0] = jnp.dot(inputs_ref[...], weights_ref[0], preferred_element_type=jnp.float32)


def project(inputs, weights, blocks, tile=512):
    tokens, depth = inputs.shape
    columns = weights.shape[2]
    return pl.pallas_call(
        _project_kernel,
        out_shape=jax.ShapeDtypeStruct((blocks, tokens, columns), jnp.float32),
        grid=(blocks, columns // tile),
        in_specs=[
            pl.BlockSpec((tokens, depth), lambda s, j: (0, 0)),
            pl.BlockSpec((1, depth, tile), lambda s, j: (s, 0, j)),
        ],
        out_specs=pl.BlockSpec((1, tokens, tile), lambda s, j: (s, 0, j)),
        cost_estimate=pl.CostEstimate(
            flops=2 * tokens * depth * columns * blocks,
            transcendentals=0,
            bytes_accessed=2 * depth * columns * blocks + 2 * tokens * depth
            + 4 * tokens * columns * blocks,
        ),
    )(inputs, weights)


def _dispatch_kernel(slot_ref, weight_ref, rows_ref, grad_ref, send_ref, grad_send_ref):
    tile = send_ref.shape[0]
    top, tokens = slot_ref.shape
    slot = pl.program_id(0) * tile + lax.broadcasted_iota(jnp.int32, (tile, tokens), 0)
    hit = slot == slot_ref[0:1, :]
    weight = jnp.where(hit, weight_ref[0:1, :], 0.0)
    for k in range(1, top):
        match = slot == slot_ref[k : k + 1, :]
        hit = hit | match
        weight = weight + jnp.where(match, weight_ref[k : k + 1, :], 0.0)
    pick = hit.astype(jnp.bfloat16)
    send_ref[...] = jnp.dot(pick, rows_ref[...], preferred_element_type=jnp.float32).astype(
        send_ref.dtype
    )
    picked_grad = jnp.dot(pick, grad_ref[...], preferred_element_type=jnp.float32)
    slot_weight = jnp.sum(weight, axis=1, keepdims=True)
    grad_send_ref[...] = (slot_weight * picked_grad).astype(grad_send_ref.dtype)


def dispatch(route_slots, route_weights, rows, grad, slots, tile=256):
    top, tokens = route_slots.shape
    width = rows.shape[1]
    out = jax.ShapeDtypeStruct((slots, width), jnp.bfloat16)
    return pl.pallas_call(
        _dispatch_kernel,
        out_shape=(out, out),
        grid=(slots // tile,),
        in_specs=[
            pl.BlockSpec((top, tokens), lambda i: (0, 0)),
            pl.BlockSpec((top, tokens), lambda i: (0, 0)),
            pl.BlockSpec((tokens, width), lambda i: (0, 0)),
            pl.BlockSpec((tokens, width), lambda i: (0, 0)),
        ],
        out_specs=(
            pl.BlockSpec((tile, width), lambda i: (i, 0)),
            pl.BlockSpec((tile, width), lambda i: (i, 0)),
        ),
        cost_estimate=pl.CostEstimate(
            flops=4 * slots * tokens * width,
            transcendentals=0,
            bytes_accessed=4 * slots * width + 4 * tokens * width + 8 * top * tokens,
        ),
    )(route_slots, route_weights, rows, grad)


def _combine_kernel(with_dots, slot_ref, weight_ref, table_ref, base_ref, other_ref, out_ref, dots_ref):
    tokens, top = slot_ref.shape
    count = table_ref.shape[0]
    total = base_ref[...]
    for k in range(top):
        pick = (
            slot_ref[:, k : k + 1] == lax.broadcasted_iota(jnp.int32, (tokens, count), 1)
        ).astype(jnp.bfloat16)
        row = jnp.dot(pick, table_ref[...], preferred_element_type=jnp.float32)
        total = total + weight_ref[:, k : k + 1] * row
        if with_dots:
            dots_ref[:, k : k + 1] = jnp.sum(
                other_ref[...].astype(jnp.float32) * row, axis=1, keepdims=True
            )
    out_ref[...] = total
    if not with_dots:
        dots_ref[...] = jnp.zeros_like(dots_ref)


def combine(slots, weights, table, base, other, with_dots):
    tokens, top = slots.shape
    count, width = table.shape
    return pl.pallas_call(
        functools.partial(_combine_kernel, with_dots),
        out_shape=(
            jax.ShapeDtypeStruct((tokens, width), jnp.float32),
            jax.ShapeDtypeStruct((tokens, top), jnp.float32),
        ),
        in_specs=[pl.BlockSpec(memory_space=pltpu.VMEM)] * 5,
        out_specs=(pl.BlockSpec(memory_space=pltpu.VMEM), pl.BlockSpec(memory_space=pltpu.VMEM)),
        cost_estimate=pl.CostEstimate(
            flops=2 * tokens * count * width * top,
            transcendentals=0,
            bytes_accessed=2 * count * width + 10 * tokens * width,
        ),
    )(slots, weights, table, base, other)


def sum_halves(values, axis, dim):
    half = values.shape[dim] // 2
    index = lax.axis_index(axis)
    own = lax.dynamic_slice_in_dim(values, index * half, half, axis=dim)
    given = lax.dynamic_slice_in_dim(values, (1 - index) * half, half, axis=dim)
    received = lax.ppermute(given.astype(jnp.bfloat16), axis, [(0, 1), (1, 0)])
    return own + received.astype(own.dtype)


def swap_context(values):
    return lax.ppermute(values, "context", [(0, 1), (1, 0)])


def gather_context(values):
    other = swap_context(values)
    first = lax.axis_index("context") == 0
    return jnp.concatenate(
        [jnp.where(first, values, other), jnp.where(first, other, values)], axis=0
    )


def sum_context_halves(values):
    half = values.shape[0] // 2
    first = lax.axis_index("context") == 0
    own = jnp.where(first, values[:half], values[half:])
    given = jnp.where(first, values[half:], values[:half]).astype(jnp.bfloat16)
    return own + swap_context(given).astype(own.dtype)


def butterfly_sum(values, axes):
    index = lax.axis_index(axes)
    count = 1
    for name in axes:
        count *= lax.axis_size(name)
    step = 1
    while step < count:
        partner = [(i, i ^ step) for i in range(count)]
        received = lax.ppermute(values, axes, partner)
        mine_first = (index & step) == 0
        values = jnp.where(mine_first, values + received, received + values)
        step *= 2
    return values


def body(
    tokens,
    grad_output,
    routes,
    positions,
    attn_gain,
    q_gain,
    k_gain,
    ffn_gain,
    qkv_weight,
    out_weight,
    router_weight,
    expert_in,
    expert_out,
):
    single_precision = jnp.float32
    bf16 = jnp.bfloat16
    seq_tok = tokens.shape[1]
    width = tokens.shape[2]
    top = routes.shape[2]
    heads_width = out_weight.shape[1]
    head_dim = HDIM
    heads = heads_width // head_dim
    local_experts = expert_in.shape[0]
    experts = router_weight.shape[1]
    sources = lax.axis_size("expert")
    capacity = min(seq_tok, seq_tok * top * 5 // (4 * experts))
    scale = head_dim ** (-0.5)
    x = tokens[0].astype(single_precision)
    normed1, factor1 = rms_forward(x)
    attention_input = (normed1 * attn_gain).astype(bf16)
    all_axes = ("dp", "context", "expert")
    weights_full = lax.all_gather(
        jnp.concatenate([qkv_weight.transpose(1, 0, 2), out_weight[:, None, :]], axis=1),
        all_axes,
        axis=0,
        tiled=True,
    )
    out_full = weights_full[:, 3, :]
    both_inputs = gather_context(attention_input)
    projected_both = project(both_inputs, weights_full.transpose(1, 0, 2), 3)
    own_start = lax.axis_index("context") * seq_tok
    projected_output = lax.dynamic_slice_in_dim(projected_both, own_start, seq_tok, axis=1)
    q_normed, q_factor = rms_forward(projected_output[0])
    k_normed, k_factor = rms_forward(projected_output[1])
    all_places = positions[0]
    own_places = lax.dynamic_slice_in_dim(all_places, own_start, seq_tok)
    cosine, sine = rope_tables(own_places, head_dim)
    all_cosine, all_sine = rope_tables(all_places, head_dim)
    queries = rotate(
        (q_normed * q_gain).reshape(seq_tok, heads, head_dim), cosine, sine, 1.0
    ).astype(bf16)
    seq_len = both_inputs.shape[0]
    keys_normed, _ = rms_forward(projected_both[1])
    keys = rotate(
        (keys_normed * k_gain).reshape(seq_len, heads, head_dim), all_cosine, all_sine, 1.0
    ).astype(bf16)
    vals = projected_both[2].astype(bf16)
    keys3 = keys.reshape(seq_len, heads, head_dim)
    vals3 = vals.reshape(seq_len, heads, head_dim)
    allowed = (all_places[None, :] <= own_places[:, None])[None]

    def masked_scores():
        scores = (
            jnp.einsum("qhd,khd->hqk", queries, keys3, preferred_element_type=single_precision)
            * scale
        )
        return jnp.where(allowed, scores, -jnp.inf)

    scores = masked_scores()
    lse = jnp.log(jnp.sum(jnp.exp(scores), axis=-1, keepdims=True))
    probs_b = jnp.exp(scores - lse).astype(bf16)
    attended = (
        jnp.einsum("hqk,khd->qhd", probs_b, vals3, preferred_element_type=single_precision)
        .astype(bf16)
        .reshape(seq_tok, heads_width)
    )
    mid = x + jnp.einsum("tq,dq->td", attended, out_full, preferred_element_type=single_precision)
    normed2, factor2 = rms_forward(mid)
    ffn_in = (normed2 * ffn_gain).astype(bf16)
    router_exp = jnp.exp(jnp.dot(ffn_in, router_weight, preferred_element_type=single_precision))
    router_probs = router_exp / jnp.sum(router_exp, axis=-1, keepdims=True)
    own_routes = routes[0]
    slots = slot_index(own_routes.reshape(-1), experts, capacity)
    expert_ids = jnp.arange(experts, dtype=jnp.int32)
    route_weight = jnp.sum(
        jnp.where(own_routes[:, :, None] == expert_ids, router_probs[:, None, :], 0.0), axis=2
    )
    route_slots = slots.reshape(seq_tok, top)
    send, grad_send = dispatch(
        route_slots.T, route_weight.T, ffn_in, grad_output[0], experts * capacity
    )
    received = lax.all_to_all(
        send.reshape(sources, local_experts * capacity, width),
        "expert",
        split_axis=0,
        concat_axis=0,
        tiled=True,
    )
    rows = expert_major(received, local_experts, capacity)
    gate_up = jnp.einsum("lrd,lkdh->lkrh", rows, expert_in, preferred_element_type=single_precision)
    gate = gate_up[:, 0]
    up = gate_up[:, 1]
    sig = jax.nn.sigmoid(gate)
    hidden = (gate * sig * up).astype(bf16)
    results = jnp.einsum(
        "lrh,lhd->lrd", hidden, expert_out, preferred_element_type=single_precision
    ).astype(bf16)
    back = lax.all_to_all(
        source_major(results, sources, capacity), "expert", split_axis=0, concat_axis=0, tiled=True
    )
    output, route_grad_weight = combine(
        route_slots,
        route_weight,
        back.reshape(experts * capacity, width),
        mid,
        grad_output[0],
        True,
    )
    grad = grad_output[0].astype(single_precision)
    grad_received = lax.all_to_all(
        grad_send.reshape(sources, local_experts * capacity, width),
        "expert",
        split_axis=0,
        concat_axis=0,
        tiled=True,
    )
    grad_rows = expert_major(grad_received, local_experts, capacity)
    grad_hidden = jnp.einsum(
        "lrd,lhd->lrh", grad_rows, expert_out, preferred_element_type=single_precision
    )
    grad_down = jnp.einsum(
        "lrh,lrd->lhd", hidden, grad_rows, preferred_element_type=single_precision
    )
    grad_gate = (grad_hidden * up * sig * (1.0 + gate * (1.0 - sig))).astype(bf16)
    grad_up = (grad_hidden * gate * sig).astype(bf16)
    grad_gate_up = jnp.stack([grad_gate, grad_up], axis=1)
    grad_gate_up_w = jnp.einsum(
        "lrd,lkrh->lkdh", rows, grad_gate_up, preferred_element_type=single_precision
    )
    grad_rows_in = jnp.einsum(
        "lkrh,lkdh->lrd", grad_gate_up, expert_in, preferred_element_type=single_precision
    ).astype(bf16)
    grad_back = lax.all_to_all(
        source_major(grad_rows_in, sources, capacity),
        "expert",
        split_axis=0,
        concat_axis=0,
        tiled=True,
    )
    chosen = (own_routes[:, :, None] == jnp.arange(experts, dtype=jnp.int32)[None, None, :]).astype(
        single_precision
    )
    grad_probs = jnp.sum(route_grad_weight[:, :, None] * chosen, axis=1)
    grad_logits = (
        router_probs * (grad_probs - jnp.sum(router_probs * grad_probs, axis=-1, keepdims=True))
    ).astype(bf16)
    grad_router = jnp.einsum(
        "td,te->de", ffn_in, grad_logits, preferred_element_type=single_precision
    )
    grad_ffn_in, _ = combine(
        route_slots,
        jnp.ones((seq_tok, top), single_precision),
        grad_back.reshape(experts * capacity, width),
        jnp.einsum("te,de->td", grad_logits, router_weight, preferred_element_type=single_precision),
        grad_output[0],
        False,
    )
    grad_mid_norm, grad_ffn_gain = rms_backward(grad_ffn_in, normed2, factor2, ffn_gain)
    grad_mid = grad + grad_mid_norm
    grad_mid_b = grad_mid.astype(bf16)
    grad_att = (
        jnp.einsum("td,dq->tq", grad_mid_b, out_full, preferred_element_type=single_precision)
        .astype(bf16)
        .reshape(seq_tok, heads, head_dim)
    )
    delta = jnp.sum(
        grad_att.astype(single_precision)
        * attended.reshape(seq_tok, heads, head_dim).astype(single_precision),
        axis=-1,
    )
    probs = jnp.exp(masked_scores() - lse)
    grad_vals = jnp.einsum(
        "hqk,qhd->khd", probs.astype(bf16), grad_att, preferred_element_type=single_precision
    )
    grad_p = jnp.einsum("qhd,khd->hqk", grad_att, vals3, preferred_element_type=single_precision)
    grad_scores = (probs * (grad_p - delta.T[:, :, None])).astype(bf16)
    grad_queries = (
        jnp.einsum("hqk,khd->qhd", grad_scores, keys3, preferred_element_type=single_precision)
        * scale
    )
    grad_keys_all = (
        jnp.einsum("hqk,qhd->khd", grad_scores, queries, preferred_element_type=single_precision)
        * scale
    )
    grad_keys_values = sum_context_halves(
        jnp.stack(
            [grad_keys_all.reshape(seq_len, heads_width), grad_vals.reshape(seq_len, heads_width)],
            axis=1,
        )
    )
    grad_keys = grad_keys_values[:, 0]
    grad_values = grad_keys_values[:, 1]
    grad_qn = rotate(grad_queries, cosine, sine, -1.0).reshape(seq_tok, heads_width)
    grad_kn = rotate(grad_keys.reshape(seq_tok, heads, head_dim), cosine, sine, -1.0).reshape(
        seq_tok, heads_width
    )
    grad_q_raw, grad_q_gain = rms_backward(grad_qn, q_normed, q_factor, q_gain)
    grad_k_raw, grad_k_gain = rms_backward(grad_kn, k_normed, k_factor, k_gain)
    projected_gradient = jnp.stack(
        [grad_q_raw, grad_k_raw, grad_values, jnp.zeros_like(grad_values)], axis=1
    ).astype(bf16)
    attention_input_gradient = jnp.dot(
        projected_gradient.reshape(seq_tok, 4 * heads_width),
        weights_full.reshape(width, 4 * heads_width).T,
        preferred_element_type=single_precision,
    )
    grad_x_norm, grad_attn_gain = rms_backward(
        attention_input_gradient, normed1, factor1, attn_gain
    )
    grad_tokens = grad_mid + grad_x_norm
    def scatter_over_copies(values):
        return sum_halves(sum_halves(values, "dp", 1), "context", 1)

    grad_in_shard = scatter_over_copies(grad_gate_up_w[0])[None]
    grad_down_shard = scatter_over_copies(grad_down[0])[None]
    left = jnp.stack([attention_input] * 3 + [grad_mid_b])
    right = jnp.concatenate(
        [projected_gradient[:, :3].transpose(1, 0, 2), attended[None]], axis=0
    )
    stacked = jnp.einsum("sta,stb->sab", left, right, preferred_element_type=single_precision)
    summed = lax.psum(stacked.astype(bf16), all_axes)
    shard_rows = width // lax.axis_size(all_axes)
    start = lax.axis_index(all_axes) * shard_rows
    weight_shard = lax.dynamic_slice_in_dim(summed, start, shard_rows, axis=1).astype(
        single_precision
    )
    grad_qkv_shard = weight_shard[:3]
    grad_out_shard = weight_shard[3]
    small_sum = butterfly_sum(
        jnp.concatenate(
            [grad_attn_gain, grad_q_gain, grad_k_gain, grad_ffn_gain, grad_router.reshape(-1)]
        ),
        all_axes,
    )
    sizes = [width, heads_width, heads_width, width, width * experts]
    offsets = [sum(sizes[:n]) for n in range(len(sizes))]
    totals = [small_sum[o : o + n] for o, n in zip(offsets, sizes)]
    totals[4] = totals[4].reshape(width, experts)
    return (
        output[None],
        grad_tokens[None],
        totals[0],
        totals[1],
        totals[2],
        totals[3],
        totals[4],
        grad_qkv_shard,
        grad_out_shard,
        grad_in_shard,
        grad_down_shard,
    )


def solution(mesh):
    return jax.shard_map(
        body,
        mesh=mesh,
        in_specs=(
            P(("dp", "expert"), "context", None),
            P(("dp", "expert"), "context", None),
            P(("dp", "expert"), "context", None),
            P(("dp", "expert"), None),
            P(),
            P(),
            P(),
            P(),
            P(None, ("dp", "context", "expert"), None),
            P(("dp", "context", "expert"), None),
            P(),
            P("expert", None, None, None),
            P("expert", None, None),
        ),
        out_specs=(
            P(("dp", "expert"), "context", None),
            P(("dp", "expert"), "context", None),
            P(),
            P(),
            P(),
            P(),
            P(),
            P(None, ("dp", "context", "expert"), None),
            P(("dp", "context", "expert"), None),
            P("expert", None, ("dp", "context"), None),
            P("expert", None, ("dp", "context")),
        ),
        check_vma=False,
    )
```

```python
import functools

import jax
import jax.numpy as jnp
from jax import lax
from jax.experimental import pallas as pl
from jax.experimental.pallas import tpu as pltpu
from jax.sharding import PartitionSpec as P

HDIM = 128


EPS = 1e-05
THETA = 10000.0


def rope_tables(places, head_dim):
    half = head_dim // 2
    freq = THETA ** (-jnp.arange(half, dtype=jnp.float32) * 2.0 / head_dim)
    angle = places.astype(jnp.float32)[:, None] * freq[None, :]
    return (jnp.cos(angle), jnp.sin(angle))


def rotate(values, cosine, sine, sign):
    half = values.shape[-1] // 2
    first = values[..., :half]
    second = values[..., half:]
    cosine = cosine[:, None, :]
    sine = sign * sine[:, None, :]
    return jnp.concatenate(
        [first * cosine - second * sine, second * cosine + first * sine], axis=-1
    )


def rms_forward(values):
    factor = lax.rsqrt(jnp.mean(values * values, axis=-1, keepdims=True) + EPS)
    return (values * factor, factor)


def rms_backward(grad_out, normed, factor, gain):
    scaled = grad_out * gain
    grad_in = factor * (scaled - normed * jnp.mean(scaled * normed, axis=-1, keepdims=True))
    return (grad_in, jnp.sum(grad_out * normed, axis=0))


def slot_index(route_rows, experts, capacity):
    onehot = (route_rows[:, None] == jnp.arange(experts, dtype=jnp.int32)[None, :]).astype(
        jnp.int32
    )
    count = route_rows.shape[0]
    earlier = (
        jnp.arange(count, dtype=jnp.int32)[None, :] < jnp.arange(count, dtype=jnp.int32)[:, None]
    ).astype(jnp.bfloat16)
    before = jnp.dot(earlier, onehot.astype(jnp.bfloat16), preferred_element_type=jnp.float32)
    return route_rows * capacity + jnp.sum(before.astype(jnp.int32) * onehot, axis=1)


def expert_major(received, local_experts, capacity):
    sources, _, width = received.shape
    return (
        received.reshape(sources, local_experts, capacity, width)
        .transpose(1, 0, 2, 3)
        .reshape(local_experts, sources * capacity, width)
    )


def source_major(results, sources, capacity):
    local_experts, _, width = results.shape
    return (
        results.reshape(local_experts, sources, capacity, width)
        .transpose(1, 0, 2, 3)
        .reshape(sources, local_experts * capacity, width)
    )


def _project_kernel(inputs_ref, weights_ref, out_ref):
    out_ref[0] = jnp.dot(inputs_ref[...], weights_ref[0], preferred_element_type=jnp.float32)


def project(inputs, weights, blocks, tile=512):
    tokens, depth = inputs.shape
    columns = weights.shape[2]
    return pl.pallas_call(
        _project_kernel,
        out_shape=jax.ShapeDtypeStruct((blocks, tokens, columns), jnp.float32),
        grid=(blocks, columns // tile),
        in_specs=[
            pl.BlockSpec((tokens, depth), lambda s, j: (0, 0)),
            pl.BlockSpec((1, depth, tile), lambda s, j: (s, 0, j)),
        ],
        out_specs=pl.BlockSpec((1, tokens, tile), lambda s, j: (s, 0, j)),
        cost_estimate=pl.CostEstimate(
            flops=2 * tokens * depth * columns * blocks,
            transcendentals=0,
            bytes_accessed=2 * depth * columns * blocks + 2 * tokens * depth
            + 4 * tokens * columns * blocks,
        ),
    )(inputs, weights)


def _dispatch_kernel(slot_ref, weight_ref, rows_ref, grad_ref, send_ref, grad_send_ref):
    tile = send_ref.shape[0]
    top, tokens = slot_ref.shape
    slot = pl.program_id(0) * tile + lax.broadcasted_iota(jnp.int32, (tile, tokens), 0)
    hit = slot == slot_ref[0:1, :]
    weight = jnp.where(hit, weight_ref[0:1, :], 0.0)
    for k in range(1, top):
        match = slot == slot_ref[k : k + 1, :]
        hit = hit | match
        weight = weight + jnp.where(match, weight_ref[k : k + 1, :], 0.0)
    pick = hit.astype(jnp.bfloat16)
    send_ref[...] = jnp.dot(pick, rows_ref[...], preferred_element_type=jnp.float32).astype(
        send_ref.dtype
    )
    picked_grad = jnp.dot(pick, grad_ref[...], preferred_element_type=jnp.float32)
    slot_weight = jnp.sum(weight, axis=1, keepdims=True)
    grad_send_ref[...] = (slot_weight * picked_grad).astype(grad_send_ref.dtype)


def dispatch(route_slots, route_weights, rows, grad, slots, tile=256):
    top, tokens = route_slots.shape
    width = rows.shape[1]
    out = jax.ShapeDtypeStruct((slots, width), jnp.bfloat16)
    return pl.pallas_call(
        _dispatch_kernel,
        out_shape=(out, out),
        grid=(slots // tile,),
        in_specs=[
            pl.BlockSpec((top, tokens), lambda i: (0, 0)),
            pl.BlockSpec((top, tokens), lambda i: (0, 0)),
            pl.BlockSpec((tokens, width), lambda i: (0, 0)),
            pl.BlockSpec((tokens, width), lambda i: (0, 0)),
        ],
        out_specs=(
            pl.BlockSpec((tile, width), lambda i: (i, 0)),
            pl.BlockSpec((tile, width), lambda i: (i, 0)),
        ),
        cost_estimate=pl.CostEstimate(
            flops=4 * slots * tokens * width,
            transcendentals=0,
            bytes_accessed=4 * slots * width + 4 * tokens * width + 8 * top * tokens,
        ),
    )(route_slots, route_weights, rows, grad)


def _combine_kernel(with_dots, slot_ref, weight_ref, table_ref, base_ref, other_ref, out_ref, dots_ref):
    tokens, top = slot_ref.shape
    count = table_ref.shape[0]
    total = base_ref[...]
    for k in range(top):
        pick = (
            slot_ref[:, k : k + 1] == lax.broadcasted_iota(jnp.int32, (tokens, count), 1)
        ).astype(jnp.bfloat16)
        row = jnp.dot(pick, table_ref[...], preferred_element_type=jnp.float32)
        total = total + weight_ref[:, k : k + 1] * row
        if with_dots:
            dots_ref[:, k : k + 1] = jnp.sum(
                other_ref[...].astype(jnp.float32) * row, axis=1, keepdims=True
            )
    out_ref[...] = total
    if not with_dots:
        dots_ref[...] = jnp.zeros_like(dots_ref)


def combine(slots, weights, table, base, other, with_dots):
    tokens, top = slots.shape
    count, width = table.shape
    return pl.pallas_call(
        functools.partial(_combine_kernel, with_dots),
        out_shape=(
            jax.ShapeDtypeStruct((tokens, width), jnp.float32),
            jax.ShapeDtypeStruct((tokens, top), jnp.float32),
        ),
        in_specs=[pl.BlockSpec(memory_space=pltpu.VMEM)] * 5,
        out_specs=(pl.BlockSpec(memory_space=pltpu.VMEM), pl.BlockSpec(memory_space=pltpu.VMEM)),
        cost_estimate=pl.CostEstimate(
            flops=2 * tokens * count * width * top,
            transcendentals=0,
            bytes_accessed=2 * count * width + 10 * tokens * width,
        ),
    )(slots, weights, table, base, other)


def sum_halves(values, axis, dim):
    half = values.shape[dim] // 2
    index = lax.axis_index(axis)
    own = lax.dynamic_slice_in_dim(values, index * half, half, axis=dim)
    given = lax.dynamic_slice_in_dim(values, (1 - index) * half, half, axis=dim)
    received = lax.ppermute(given.astype(jnp.bfloat16), axis, [(0, 1), (1, 0)])
    return own + received.astype(own.dtype)


def swap_context(values):
    return lax.ppermute(values, "context", [(0, 1), (1, 0)])


def gather_context(values):
    other = swap_context(values)
    first = lax.axis_index("context") == 0
    return jnp.concatenate(
        [jnp.where(first, values, other), jnp.where(first, other, values)], axis=0
    )


def sum_context_halves(values):
    half = values.shape[0] // 2
    first = lax.axis_index("context") == 0
    own = jnp.where(first, values[:half], values[half:])
    given = jnp.where(first, values[half:], values[:half]).astype(jnp.bfloat16)
    return own + swap_context(given).astype(own.dtype)


def butterfly_sum(values, axes):
    index = lax.axis_index(axes)
    count = 1
    for name in axes:
        count *= lax.axis_size(name)
    step = 1
    while step < count:
        partner = [(i, i ^ step) for i in range(count)]
        received = lax.ppermute(values, axes, partner)
        mine_first = (index & step) == 0
        values = jnp.where(mine_first, values + received, received + values)
        step *= 2
    return values


def body(
    tokens,
    grad_output,
    routes,
    positions,
    attn_gain,
    q_gain,
    k_gain,
    ffn_gain,
    qkv_weight,
    out_weight,
    router_weight,
    expert_in,
    expert_out,
):
    single_precision = jnp.float32
    bf16 = jnp.bfloat16
    seq_tok = tokens.shape[1]
    width = tokens.shape[2]
    top = routes.shape[2]
    heads_width = out_weight.shape[1]
    head_dim = HDIM
    heads = heads_width // head_dim
    local_experts = expert_in.shape[0]
    experts = router_weight.shape[1]
    sources = lax.axis_size("expert")
    capacity = min(seq_tok, seq_tok * top * 5 // (4 * experts))
    scale = head_dim ** (-0.5)
    x = tokens[0].astype(single_precision)
    normed1, factor1 = rms_forward(x)
    attention_input = (normed1 * attn_gain).astype(bf16)
    all_axes = ("dp", "context", "expert")
    weights_full = lax.all_gather(
        jnp.concatenate([qkv_weight.transpose(1, 0, 2), out_weight[:, None, :]], axis=1),
        all_axes,
        axis=0,
        tiled=True,
    )
    out_full = weights_full[:, 3, :]
    both_inputs = gather_context(attention_input)
    projected_both = project(both_inputs, weights_full.transpose(1, 0, 2), 3)
    own_start = lax.axis_index("context") * seq_tok
    projected_output = lax.dynamic_slice_in_dim(projected_both, own_start, seq_tok, axis=1)
    q_normed, q_factor = rms_forward(projected_output[0])
    k_normed, k_factor = rms_forward(projected_output[1])
    all_places = positions[0]
    own_places = lax.dynamic_slice_in_dim(all_places, own_start, seq_tok)
    cosine, sine = rope_tables(own_places, head_dim)
    all_cosine, all_sine = rope_tables(all_places, head_dim)
    queries = rotate(
        (q_normed * q_gain).reshape(seq_tok, heads, head_dim), cosine, sine, 1.0
    ).astype(bf16)
    seq_len = both_inputs.shape[0]
    keys_normed, _ = rms_forward(projected_both[1])
    keys = rotate(
        (keys_normed * k_gain).reshape(seq_len, heads, head_dim), all_cosine, all_sine, 1.0
    ).astype(bf16)
    vals = projected_both[2].astype(bf16)
    keys3 = keys.reshape(seq_len, heads, head_dim)
    vals3 = vals.reshape(seq_len, heads, head_dim)
    allowed = (all_places[None, :] <= own_places[:, None])[None]

    def masked_scores():
        scores = (
            jnp.einsum("qhd,khd->hqk", queries, keys3, preferred_element_type=single_precision)
            * scale
        )
        return jnp.where(allowed, scores, -jnp.inf)

    scores = masked_scores()
    lse = jnp.log(jnp.sum(jnp.exp(scores), axis=-1, keepdims=True))
    probs_b = jnp.exp(scores - lse).astype(bf16)
    attended = (
        jnp.einsum("hqk,khd->qhd", probs_b, vals3, preferred_element_type=single_precision)
        .astype(bf16)
        .reshape(seq_tok, heads_width)
    )
    mid = x + jnp.einsum("tq,dq->td", attended, out_full, preferred_element_type=single_precision)
    normed2, factor2 = rms_forward(mid)
    ffn_in = (normed2 * ffn_gain).astype(bf16)
    router_exp = jnp.exp(jnp.dot(ffn_in, router_weight, preferred_element_type=single_precision))
    router_probs = router_exp / jnp.sum(router_exp, axis=-1, keepdims=True)
    own_routes = routes[0]
    slots = slot_index(own_routes.reshape(-1), experts, capacity)
    expert_ids = jnp.arange(experts, dtype=jnp.int32)
    route_weight = jnp.sum(
        jnp.where(own_routes[:, :, None] == expert_ids, router_probs[:, None, :], 0.0), axis=2
    )
    route_slots = slots.reshape(seq_tok, top)
    send, grad_send = dispatch(
        route_slots.T, route_weight.T, ffn_in, grad_output[0], experts * capacity
    )
    received = lax.all_to_all(
        send.reshape(sources, local_experts * capacity, width),
        "expert",
        split_axis=0,
        concat_axis=0,
        tiled=True,
    )
    rows = expert_major(received, local_experts, capacity)
    gate_up = jnp.einsum("lrd,lkdh->lkrh", rows, expert_in, preferred_element_type=single_precision)
    gate = gate_up[:, 0]
    up = gate_up[:, 1]
    sig = jax.nn.sigmoid(gate)
    hidden = (gate * sig * up).astype(bf16)
    results = jnp.einsum(
        "lrh,lhd->lrd", hidden, expert_out, preferred_element_type=single_precision
    ).astype(bf16)
    back = lax.all_to_all(
        source_major(results, sources, capacity), "expert", split_axis=0, concat_axis=0, tiled=True
    )
    output, route_grad_weight = combine(
        route_slots,
        route_weight,
        back.reshape(experts * capacity, width),
        mid,
        grad_output[0],
        True,
    )
    grad = grad_output[0].astype(single_precision)
    grad_received = lax.all_to_all(
        grad_send.reshape(sources, local_experts * capacity, width),
        "expert",
        split_axis=0,
        concat_axis=0,
        tiled=True,
    )
    grad_rows = expert_major(grad_received, local_experts, capacity)
    grad_hidden = jnp.einsum(
        "lrd,lhd->lrh", grad_rows, expert_out, preferred_element_type=single_precision
    )
    grad_down = jnp.einsum(
        "lrh,lrd->lhd", hidden, grad_rows, preferred_element_type=single_precision
    )
    grad_gate = (grad_hidden * up * sig * (1.0 + gate * (1.0 - sig))).astype(bf16)
    grad_up = (grad_hidden * gate * sig).astype(bf16)
    grad_gate_up = jnp.stack([grad_gate, grad_up], axis=1)
    grad_gate_up_w = jnp.einsum(
        "lrd,lkrh->lkdh", rows, grad_gate_up, preferred_element_type=single_precision
    )
    grad_rows_in = jnp.einsum(
        "lkrh,lkdh->lrd", grad_gate_up, expert_in, preferred_element_type=single_precision
    ).astype(bf16)
    grad_back = lax.all_to_all(
        source_major(grad_rows_in, sources, capacity),
        "expert",
        split_axis=0,
        concat_axis=0,
        tiled=True,
    )
    chosen = (own_routes[:, :, None] == jnp.arange(experts, dtype=jnp.int32)[None, None, :]).astype(
        single_precision
    )
    grad_probs = jnp.sum(route_grad_weight[:, :, None] * chosen, axis=1)
    grad_logits = (
        router_probs * (grad_probs - jnp.sum(router_probs * grad_probs, axis=-1, keepdims=True))
    ).astype(bf16)
    grad_router = jnp.einsum(
        "td,te->de", ffn_in, grad_logits, preferred_element_type=single_precision
    )
    grad_ffn_in, _ = combine(
        route_slots,
        jnp.ones((seq_tok, top), single_precision),
        grad_back.reshape(experts * capacity, width),
        jnp.einsum("te,de->td", grad_logits, router_weight, preferred_element_type=single_precision),
        grad_output[0],
        False,
    )
    grad_mid_norm, grad_ffn_gain = rms_backward(grad_ffn_in, normed2, factor2, ffn_gain)
    grad_mid = grad + grad_mid_norm
    grad_mid_b = grad_mid.astype(bf16)
    grad_att = (
        jnp.einsum("td,dq->tq", grad_mid_b, out_full, preferred_element_type=single_precision)
        .astype(bf16)
        .reshape(seq_tok, heads, head_dim)
    )
    delta = jnp.sum(
        grad_att.astype(single_precision)
        * attended.reshape(seq_tok, heads, head_dim).astype(single_precision),
        axis=-1,
    )
    probs = jnp.exp(masked_scores() - lse)
    grad_vals = jnp.einsum(
        "hqk,qhd->khd", probs.astype(bf16), grad_att, preferred_element_type=single_precision
    )
    grad_p = jnp.einsum("qhd,khd->hqk", grad_att, vals3, preferred_element_type=single_precision)
    grad_scores = (probs * (grad_p - delta.T[:, :, None])).astype(bf16)
    grad_queries = (
        jnp.einsum("hqk,khd->qhd", grad_scores, keys3, preferred_element_type=single_precision)
        * scale
    )
    grad_keys_all = (
        jnp.einsum("hqk,qhd->khd", grad_scores, queries, preferred_element_type=single_precision)
        * scale
    )
    grad_values = sum_context_halves(grad_vals.reshape(seq_len, heads_width))
    grad_keys = sum_context_halves(grad_keys_all.reshape(seq_len, heads_width))
    grad_qn = rotate(grad_queries, cosine, sine, -1.0).reshape(seq_tok, heads_width)
    grad_kn = rotate(grad_keys.reshape(seq_tok, heads, head_dim), cosine, sine, -1.0).reshape(
        seq_tok, heads_width
    )
    grad_q_raw, grad_q_gain = rms_backward(grad_qn, q_normed, q_factor, q_gain)
    grad_k_raw, grad_k_gain = rms_backward(grad_kn, k_normed, k_factor, k_gain)
    projected_gradient = jnp.stack(
        [grad_q_raw, grad_k_raw, grad_values, jnp.zeros_like(grad_values)], axis=1
    ).astype(bf16)
    attention_input_gradient = jnp.dot(
        projected_gradient.reshape(seq_tok, 4 * heads_width),
        weights_full.reshape(width, 4 * heads_width).T,
        preferred_element_type=single_precision,
    )
    grad_x_norm, grad_attn_gain = rms_backward(
        attention_input_gradient, normed1, factor1, attn_gain
    )
    grad_tokens = grad_mid + grad_x_norm
    def scatter_over_copies(values):
        return sum_halves(sum_halves(values, "dp", 1), "context", 1)

    grad_in_shard = scatter_over_copies(grad_gate_up_w[0])[None]
    grad_down_shard = scatter_over_copies(grad_down[0])[None]
    left = jnp.stack([attention_input] * 3 + [grad_mid_b])
    right = jnp.concatenate(
        [projected_gradient[:, :3].transpose(1, 0, 2), attended[None]], axis=0
    )
    stacked = jnp.einsum("sta,stb->sab", left, right, preferred_element_type=single_precision)
    summed = lax.psum(stacked.astype(bf16), all_axes)
    shard_rows = width // lax.axis_size(all_axes)
    start = lax.axis_index(all_axes) * shard_rows
    weight_shard = lax.dynamic_slice_in_dim(summed, start, shard_rows, axis=1).astype(
        single_precision
    )
    grad_qkv_shard = weight_shard[:3]
    grad_out_shard = weight_shard[3]
    small_sum = butterfly_sum(
        jnp.concatenate(
            [grad_attn_gain, grad_q_gain, grad_k_gain, grad_ffn_gain, grad_router.reshape(-1)]
        ),
        all_axes,
    )
    sizes = [width, heads_width, heads_width, width, width * experts]
    offsets = [sum(sizes[:n]) for n in range(len(sizes))]
    totals = [small_sum[o : o + n] for o, n in zip(offsets, sizes)]
    totals[4] = totals[4].reshape(width, experts)
    return (
        output[None],
        grad_tokens[None],
        totals[0],
        totals[1],
        totals[2],
        totals[3],
        totals[4],
        grad_qkv_shard,
        grad_out_shard,
        grad_in_shard,
        grad_down_shard,
    )


def solution(mesh):
    return jax.shard_map(
        body,
        mesh=mesh,
        in_specs=(
            P(("dp", "expert"), "context", None),
            P(("dp", "expert"), "context", None),
            P(("dp", "expert"), "context", None),
            P(("dp", "expert"), None),
            P(),
            P(),
            P(),
            P(),
            P(None, ("dp", "context", "expert"), None),
            P(("dp", "context", "expert"), None),
            P(),
            P("expert", None, None, None),
            P("expert", None, None),
        ),
        out_specs=(
            P(("dp", "expert"), "context", None),
            P(("dp", "expert"), "context", None),
            P(),
            P(),
            P(),
            P(),
            P(),
            P(None, ("dp", "context", "expert"), None),
            P(("dp", "context", "expert"), None),
            P("expert", None, ("dp", "context"), None),
            P("expert", None, ("dp", "context")),
        ),
        check_vma=False,
    )
```

```python
import functools

import jax
import jax.numpy as jnp
from jax import lax
from jax.experimental import pallas as pl
from jax.experimental.pallas import tpu as pltpu
from jax.sharding import PartitionSpec as P

HDIM = 128


EPS = 1e-05
THETA = 10000.0


def rope_tables(places, head_dim):
    half = head_dim // 2
    freq = THETA ** (-jnp.arange(half, dtype=jnp.float32) * 2.0 / head_dim)
    angle = places.astype(jnp.float32)[:, None] * freq[None, :]
    return (jnp.cos(angle), jnp.sin(angle))


def rotate(values, cosine, sine, sign):
    half = values.shape[-1] // 2
    first = values[..., :half]
    second = values[..., half:]
    cosine = cosine[:, None, :]
    sine = sign * sine[:, None, :]
    return jnp.concatenate(
        [first * cosine - second * sine, second * cosine + first * sine], axis=-1
    )


def rms_forward(values):
    factor = lax.rsqrt(jnp.mean(values * values, axis=-1, keepdims=True) + EPS)
    return (values * factor, factor)


def rms_backward(grad_out, normed, factor, gain):
    scaled = grad_out * gain
    grad_in = factor * (scaled - normed * jnp.mean(scaled * normed, axis=-1, keepdims=True))
    return (grad_in, jnp.sum(grad_out * normed, axis=0))


def slot_index(route_rows, experts, capacity):
    onehot = (route_rows[:, None] == jnp.arange(experts, dtype=jnp.int32)[None, :]).astype(
        jnp.int32
    )
    count = route_rows.shape[0]
    earlier = (
        jnp.arange(count, dtype=jnp.int32)[None, :] < jnp.arange(count, dtype=jnp.int32)[:, None]
    ).astype(jnp.bfloat16)
    before = jnp.dot(earlier, onehot.astype(jnp.bfloat16), preferred_element_type=jnp.float32)
    return route_rows * capacity + jnp.sum(before.astype(jnp.int32) * onehot, axis=1)


def expert_major(received, local_experts, capacity):
    sources, _, width = received.shape
    return (
        received.reshape(sources, local_experts, capacity, width)
        .transpose(1, 0, 2, 3)
        .reshape(local_experts, sources * capacity, width)
    )


def source_major(results, sources, capacity):
    local_experts, _, width = results.shape
    return (
        results.reshape(local_experts, sources, capacity, width)
        .transpose(1, 0, 2, 3)
        .reshape(sources, local_experts * capacity, width)
    )


def _project_kernel(inputs_ref, weights_ref, out_ref):
    out_ref[0] = jnp.dot(inputs_ref[...], weights_ref[0], preferred_element_type=jnp.float32)


def project(inputs, weights, blocks, tile=1024):
    tokens, depth = inputs.shape
    columns = weights.shape[2]
    return pl.pallas_call(
        _project_kernel,
        out_shape=jax.ShapeDtypeStruct((blocks, tokens, columns), jnp.float32),
        grid=(blocks, columns // tile),
        in_specs=[
            pl.BlockSpec((tokens, depth), lambda s, j: (0, 0)),
            pl.BlockSpec((1, depth, tile), lambda s, j: (s, 0, j)),
        ],
        out_specs=pl.BlockSpec((1, tokens, tile), lambda s, j: (s, 0, j)),
        cost_estimate=pl.CostEstimate(
            flops=2 * tokens * depth * columns * blocks,
            transcendentals=0,
            bytes_accessed=2 * depth * columns * blocks + 2 * tokens * depth
            + 4 * tokens * columns * blocks,
        ),
    )(inputs, weights)


def _dispatch_kernel(slot_ref, weight_ref, rows_ref, grad_ref, send_ref, grad_send_ref):
    tile = send_ref.shape[0]
    top, tokens = slot_ref.shape
    slot = pl.program_id(0) * tile + lax.broadcasted_iota(jnp.int32, (tile, tokens), 0)
    hit = slot == slot_ref[0:1, :]
    weight = jnp.where(hit, weight_ref[0:1, :], 0.0)
    for k in range(1, top):
        match = slot == slot_ref[k : k + 1, :]
        hit = hit | match
        weight = weight + jnp.where(match, weight_ref[k : k + 1, :], 0.0)
    pick = hit.astype(jnp.bfloat16)
    send_ref[...] = jnp.dot(pick, rows_ref[...], preferred_element_type=jnp.float32).astype(
        send_ref.dtype
    )
    picked_grad = jnp.dot(pick, grad_ref[...], preferred_element_type=jnp.float32)
    slot_weight = jnp.sum(weight, axis=1, keepdims=True)
    grad_send_ref[...] = (slot_weight * picked_grad).astype(grad_send_ref.dtype)


def dispatch(route_slots, route_weights, rows, grad, slots, tile=256):
    top, tokens = route_slots.shape
    width = rows.shape[1]
    out = jax.ShapeDtypeStruct((slots, width), jnp.bfloat16)
    return pl.pallas_call(
        _dispatch_kernel,
        out_shape=(out, out),
        grid=(slots // tile,),
        in_specs=[
            pl.BlockSpec((top, tokens), lambda i: (0, 0)),
            pl.BlockSpec((top, tokens), lambda i: (0, 0)),
            pl.BlockSpec((tokens, width), lambda i: (0, 0)),
            pl.BlockSpec((tokens, width), lambda i: (0, 0)),
        ],
        out_specs=(
            pl.BlockSpec((tile, width), lambda i: (i, 0)),
            pl.BlockSpec((tile, width), lambda i: (i, 0)),
        ),
        cost_estimate=pl.CostEstimate(
            flops=4 * slots * tokens * width,
            transcendentals=0,
            bytes_accessed=4 * slots * width + 4 * tokens * width + 8 * top * tokens,
        ),
    )(route_slots, route_weights, rows, grad)


def _combine_kernel(with_dots, slot_ref, weight_ref, table_ref, base_ref, other_ref, out_ref, dots_ref):
    tokens, top = slot_ref.shape
    count = table_ref.shape[0]
    total = base_ref[...]
    for k in range(top):
        pick = (
            slot_ref[:, k : k + 1] == lax.broadcasted_iota(jnp.int32, (tokens, count), 1)
        ).astype(jnp.bfloat16)
        row = jnp.dot(pick, table_ref[...], preferred_element_type=jnp.float32)
        total = total + weight_ref[:, k : k + 1] * row
        if with_dots:
            dots_ref[:, k : k + 1] = jnp.sum(
                other_ref[...].astype(jnp.float32) * row, axis=1, keepdims=True
            )
    out_ref[...] = total
    if not with_dots:
        dots_ref[...] = jnp.zeros_like(dots_ref)


def combine(slots, weights, table, base, other, with_dots):
    tokens, top = slots.shape
    count, width = table.shape
    return pl.pallas_call(
        functools.partial(_combine_kernel, with_dots),
        out_shape=(
            jax.ShapeDtypeStruct((tokens, width), jnp.float32),
            jax.ShapeDtypeStruct((tokens, top), jnp.float32),
        ),
        in_specs=[pl.BlockSpec(memory_space=pltpu.VMEM)] * 5,
        out_specs=(pl.BlockSpec(memory_space=pltpu.VMEM), pl.BlockSpec(memory_space=pltpu.VMEM)),
        cost_estimate=pl.CostEstimate(
            flops=2 * tokens * count * width * top,
            transcendentals=0,
            bytes_accessed=2 * count * width + 10 * tokens * width,
        ),
    )(slots, weights, table, base, other)


def sum_halves(values, axis, dim):
    half = values.shape[dim] // 2
    index = lax.axis_index(axis)
    own = lax.dynamic_slice_in_dim(values, index * half, half, axis=dim)
    given = lax.dynamic_slice_in_dim(values, (1 - index) * half, half, axis=dim)
    received = lax.ppermute(given.astype(jnp.bfloat16), axis, [(0, 1), (1, 0)])
    return own + received.astype(own.dtype)


def swap_context(values):
    return lax.ppermute(values, "context", [(0, 1), (1, 0)])


def gather_context(values):
    other = swap_context(values)
    first = lax.axis_index("context") == 0
    return jnp.concatenate(
        [jnp.where(first, values, other), jnp.where(first, other, values)], axis=0
    )


def sum_context_halves(values):
    half = values.shape[0] // 2
    first = lax.axis_index("context") == 0
    own = jnp.where(first, values[:half], values[half:])
    given = jnp.where(first, values[half:], values[:half]).astype(jnp.bfloat16)
    return own + swap_context(given).astype(own.dtype)


def butterfly_sum(values, axes):
    index = lax.axis_index(axes)
    count = 1
    for name in axes:
        count *= lax.axis_size(name)
    step = 1
    while step < count:
        partner = [(i, i ^ step) for i in range(count)]
        received = lax.ppermute(values, axes, partner)
        mine_first = (index & step) == 0
        values = jnp.where(mine_first, values + received, received + values)
        step *= 2
    return values


def body(
    tokens,
    grad_output,
    routes,
    positions,
    attn_gain,
    q_gain,
    k_gain,
    ffn_gain,
    qkv_weight,
    out_weight,
    router_weight,
    expert_in,
    expert_out,
):
    single_precision = jnp.float32
    bf16 = jnp.bfloat16
    seq_tok = tokens.shape[1]
    width = tokens.shape[2]
    top = routes.shape[2]
    heads_width = out_weight.shape[1]
    head_dim = HDIM
    heads = heads_width // head_dim
    local_experts = expert_in.shape[0]
    experts = router_weight.shape[1]
    sources = lax.axis_size("expert")
    capacity = min(seq_tok, seq_tok * top * 5 // (4 * experts))
    scale = head_dim ** (-0.5)
    x = tokens[0].astype(single_precision)
    normed1, factor1 = rms_forward(x)
    attention_input = (normed1 * attn_gain).astype(bf16)
    all_axes = ("dp", "context", "expert")
    weights_full = lax.all_gather(
        jnp.concatenate([qkv_weight.transpose(1, 0, 2), out_weight[:, None, :]], axis=1),
        all_axes,
        axis=0,
        tiled=True,
    )
    out_full = weights_full[:, 3, :]
    both_inputs = gather_context(attention_input)
    projected_both = project(both_inputs, weights_full.transpose(1, 0, 2), 3)
    own_start = lax.axis_index("context") * seq_tok
    projected_output = lax.dynamic_slice_in_dim(projected_both, own_start, seq_tok, axis=1)
    q_normed, q_factor = rms_forward(projected_output[0])
    k_normed, k_factor = rms_forward(projected_output[1])
    all_places = positions[0]
    own_places = lax.dynamic_slice_in_dim(all_places, own_start, seq_tok)
    cosine, sine = rope_tables(own_places, head_dim)
    all_cosine, all_sine = rope_tables(all_places, head_dim)
    queries = rotate(
        (q_normed * q_gain).reshape(seq_tok, heads, head_dim), cosine, sine, 1.0
    ).astype(bf16)
    seq_len = both_inputs.shape[0]
    keys_normed, _ = rms_forward(projected_both[1])
    keys = rotate(
        (keys_normed * k_gain).reshape(seq_len, heads, head_dim), all_cosine, all_sine, 1.0
    ).astype(bf16)
    vals = projected_both[2].astype(bf16)
    keys3 = keys.reshape(seq_len, heads, head_dim)
    vals3 = vals.reshape(seq_len, heads, head_dim)
    allowed = (all_places[None, :] <= own_places[:, None])[None]

    def masked_scores():
        scores = (
            jnp.einsum("qhd,khd->hqk", queries, keys3, preferred_element_type=single_precision)
            * scale
        )
        return jnp.where(allowed, scores, -jnp.inf)

    scores = masked_scores()
    lse = jnp.log(jnp.sum(jnp.exp(scores), axis=-1, keepdims=True))
    probs_b = jnp.exp(scores - lse).astype(bf16)
    attended = (
        jnp.einsum("hqk,khd->qhd", probs_b, vals3, preferred_element_type=single_precision)
        .astype(bf16)
        .reshape(seq_tok, heads_width)
    )
    mid = x + jnp.einsum("tq,dq->td", attended, out_full, preferred_element_type=single_precision)
    normed2, factor2 = rms_forward(mid)
    ffn_in = (normed2 * ffn_gain).astype(bf16)
    router_exp = jnp.exp(jnp.dot(ffn_in, router_weight, preferred_element_type=single_precision))
    router_probs = router_exp / jnp.sum(router_exp, axis=-1, keepdims=True)
    own_routes = routes[0]
    slots = slot_index(own_routes.reshape(-1), experts, capacity)
    expert_ids = jnp.arange(experts, dtype=jnp.int32)
    route_weight = jnp.sum(
        jnp.where(own_routes[:, :, None] == expert_ids, router_probs[:, None, :], 0.0), axis=2
    )
    route_slots = slots.reshape(seq_tok, top)
    send, grad_send = dispatch(
        route_slots.T, route_weight.T, ffn_in, grad_output[0], experts * capacity
    )
    received = lax.all_to_all(
        send.reshape(sources, local_experts * capacity, width),
        "expert",
        split_axis=0,
        concat_axis=0,
        tiled=True,
    )
    rows = expert_major(received, local_experts, capacity)
    gate_up = jnp.einsum("lrd,lkdh->lkrh", rows, expert_in, preferred_element_type=single_precision)
    gate = gate_up[:, 0]
    up = gate_up[:, 1]
    sig = jax.nn.sigmoid(gate)
    hidden = (gate * sig * up).astype(bf16)
    results = jnp.einsum(
        "lrh,lhd->lrd", hidden, expert_out, preferred_element_type=single_precision
    ).astype(bf16)
    back = lax.all_to_all(
        source_major(results, sources, capacity), "expert", split_axis=0, concat_axis=0, tiled=True
    )
    output, route_grad_weight = combine(
        route_slots,
        route_weight,
        back.reshape(experts * capacity, width),
        mid,
        grad_output[0],
        True,
    )
    grad = grad_output[0].astype(single_precision)
    grad_received = lax.all_to_all(
        grad_send.reshape(sources, local_experts * capacity, width),
        "expert",
        split_axis=0,
        concat_axis=0,
        tiled=True,
    )
    grad_rows = expert_major(grad_received, local_experts, capacity)
    grad_hidden = jnp.einsum(
        "lrd,lhd->lrh", grad_rows, expert_out, preferred_element_type=single_precision
    )
    grad_down = jnp.einsum(
        "lrh,lrd->lhd", hidden, grad_rows, preferred_element_type=single_precision
    )
    grad_gate = (grad_hidden * up * sig * (1.0 + gate * (1.0 - sig))).astype(bf16)
    grad_up = (grad_hidden * gate * sig).astype(bf16)
    grad_gate_up = jnp.stack([grad_gate, grad_up], axis=1)
    grad_gate_up_w = jnp.einsum(
        "lrd,lkrh->lkdh", rows, grad_gate_up, preferred_element_type=single_precision
    )
    grad_rows_in = jnp.einsum(
        "lkrh,lkdh->lrd", grad_gate_up, expert_in, preferred_element_type=single_precision
    ).astype(bf16)
    grad_back = lax.all_to_all(
        source_major(grad_rows_in, sources, capacity),
        "expert",
        split_axis=0,
        concat_axis=0,
        tiled=True,
    )
    chosen = (own_routes[:, :, None] == jnp.arange(experts, dtype=jnp.int32)[None, None, :]).astype(
        single_precision
    )
    grad_probs = jnp.sum(route_grad_weight[:, :, None] * chosen, axis=1)
    grad_logits = (
        router_probs * (grad_probs - jnp.sum(router_probs * grad_probs, axis=-1, keepdims=True))
    ).astype(bf16)
    grad_router = jnp.einsum(
        "td,te->de", ffn_in, grad_logits, preferred_element_type=single_precision
    )
    grad_ffn_in, _ = combine(
        route_slots,
        jnp.ones((seq_tok, top), single_precision),
        grad_back.reshape(experts * capacity, width),
        jnp.einsum("te,de->td", grad_logits, router_weight, preferred_element_type=single_precision),
        grad_output[0],
        False,
    )
    grad_mid_norm, grad_ffn_gain = rms_backward(grad_ffn_in, normed2, factor2, ffn_gain)
    grad_mid = grad + grad_mid_norm
    grad_mid_b = grad_mid.astype(bf16)
    grad_att = (
        jnp.einsum("td,dq->tq", grad_mid_b, out_full, preferred_element_type=single_precision)
        .astype(bf16)
        .reshape(seq_tok, heads, head_dim)
    )
    delta = jnp.sum(
        grad_att.astype(single_precision)
        * attended.reshape(seq_tok, heads, head_dim).astype(single_precision),
        axis=-1,
    )
    probs = jnp.exp(masked_scores() - lse)
    grad_vals = jnp.einsum(
        "hqk,qhd->khd", probs.astype(bf16), grad_att, preferred_element_type=single_precision
    )
    grad_p = jnp.einsum("qhd,khd->hqk", grad_att, vals3, preferred_element_type=single_precision)
    grad_scores = (probs * (grad_p - delta.T[:, :, None])).astype(bf16)
    grad_queries = (
        jnp.einsum("hqk,khd->qhd", grad_scores, keys3, preferred_element_type=single_precision)
        * scale
    )
    grad_keys_all = (
        jnp.einsum("hqk,qhd->khd", grad_scores, queries, preferred_element_type=single_precision)
        * scale
    )
    grad_values = sum_context_halves(grad_vals.reshape(seq_len, heads_width))
    grad_keys = sum_context_halves(grad_keys_all.reshape(seq_len, heads_width))
    grad_qn = rotate(grad_queries, cosine, sine, -1.0).reshape(seq_tok, heads_width)
    grad_kn = rotate(grad_keys.reshape(seq_tok, heads, head_dim), cosine, sine, -1.0).reshape(
        seq_tok, heads_width
    )
    grad_q_raw, grad_q_gain = rms_backward(grad_qn, q_normed, q_factor, q_gain)
    grad_k_raw, grad_k_gain = rms_backward(grad_kn, k_normed, k_factor, k_gain)
    projected_gradient = jnp.stack(
        [grad_q_raw, grad_k_raw, grad_values, jnp.zeros_like(grad_values)], axis=1
    ).astype(bf16)
    attention_input_gradient = jnp.dot(
        projected_gradient.reshape(seq_tok, 4 * heads_width),
        weights_full.reshape(width, 4 * heads_width).T,
        preferred_element_type=single_precision,
    )
    grad_x_norm, grad_attn_gain = rms_backward(
        attention_input_gradient, normed1, factor1, attn_gain
    )
    grad_tokens = grad_mid + grad_x_norm
    def scatter_over_copies(values):
        return sum_halves(sum_halves(values, "dp", 1), "context", 1)

    grad_in_shard = scatter_over_copies(grad_gate_up_w[0])[None]
    grad_down_shard = scatter_over_copies(grad_down[0])[None]
    left = jnp.stack([attention_input] * 3 + [grad_mid_b])
    right = jnp.concatenate(
        [projected_gradient[:, :3].transpose(1, 0, 2), attended[None]], axis=0
    )
    stacked = jnp.einsum("sta,stb->sab", left, right, preferred_element_type=single_precision)
    summed = lax.psum(stacked.astype(bf16), all_axes)
    shard_rows = width // lax.axis_size(all_axes)
    start = lax.axis_index(all_axes) * shard_rows
    weight_shard = lax.dynamic_slice_in_dim(summed, start, shard_rows, axis=1).astype(
        single_precision
    )
    grad_qkv_shard = weight_shard[:3]
    grad_out_shard = weight_shard[3]
    small_sum = butterfly_sum(
        jnp.concatenate(
            [grad_attn_gain, grad_q_gain, grad_k_gain, grad_ffn_gain, grad_router.reshape(-1)]
        ),
        all_axes,
    )
    sizes = [width, heads_width, heads_width, width, width * experts]
    offsets = [sum(sizes[:n]) for n in range(len(sizes))]
    totals = [small_sum[o : o + n] for o, n in zip(offsets, sizes)]
    totals[4] = totals[4].reshape(width, experts)
    return (
        output[None],
        grad_tokens[None],
        totals[0],
        totals[1],
        totals[2],
        totals[3],
        totals[4],
        grad_qkv_shard,
        grad_out_shard,
        grad_in_shard,
        grad_down_shard,
    )


def solution(mesh):
    return jax.shard_map(
        body,
        mesh=mesh,
        in_specs=(
            P(("dp", "expert"), "context", None),
            P(("dp", "expert"), "context", None),
            P(("dp", "expert"), "context", None),
            P(("dp", "expert"), None),
            P(),
            P(),
            P(),
            P(),
            P(None, ("dp", "context", "expert"), None),
            P(("dp", "context", "expert"), None),
            P(),
            P("expert", None, None, None),
            P("expert", None, None),
        ),
        out_specs=(
            P(("dp", "expert"), "context", None),
            P(("dp", "expert"), "context", None),
            P(),
            P(),
            P(),
            P(),
            P(),
            P(None, ("dp", "context", "expert"), None),
            P(("dp", "context", "expert"), None),
            P("expert", None, ("dp", "context"), None),
            P("expert", None, ("dp", "context")),
        ),
        check_vma=False,
    )
```

```python
import functools

import jax
import jax.numpy as jnp
from jax import lax
from jax.experimental import pallas as pl
from jax.experimental.pallas import tpu as pltpu
from jax.sharding import PartitionSpec as P

HDIM = 128


EPS = 1e-05
THETA = 10000.0


def rope_tables(places, head_dim):
    half = head_dim // 2
    freq = THETA ** (-jnp.arange(half, dtype=jnp.float32) * 2.0 / head_dim)
    angle = places.astype(jnp.float32)[:, None] * freq[None, :]
    return (jnp.cos(angle), jnp.sin(angle))


def rotate(values, cosine, sine, sign):
    half = values.shape[-1] // 2
    first = values[..., :half]
    second = values[..., half:]
    cosine = cosine[:, None, :]
    sine = sign * sine[:, None, :]
    return jnp.concatenate(
        [first * cosine - second * sine, second * cosine + first * sine], axis=-1
    )


def rms_forward(values):
    factor = lax.rsqrt(jnp.mean(values * values, axis=-1, keepdims=True) + EPS)
    return (values * factor, factor)


def rms_backward(grad_out, normed, factor, gain):
    scaled = grad_out * gain
    grad_in = factor * (scaled - normed * jnp.mean(scaled * normed, axis=-1, keepdims=True))
    return (grad_in, jnp.sum(grad_out * normed, axis=0))


def slot_index(route_rows, experts, capacity):
    onehot = (route_rows[:, None] == jnp.arange(experts, dtype=jnp.int32)[None, :]).astype(
        jnp.int32
    )
    count = route_rows.shape[0]
    earlier = (
        jnp.arange(count, dtype=jnp.int32)[None, :] < jnp.arange(count, dtype=jnp.int32)[:, None]
    ).astype(jnp.bfloat16)
    before = jnp.dot(earlier, onehot.astype(jnp.bfloat16), preferred_element_type=jnp.float32)
    return route_rows * capacity + jnp.sum(before.astype(jnp.int32) * onehot, axis=1)


def expert_major(received, local_experts, capacity):
    sources, _, width = received.shape
    return (
        received.reshape(sources, local_experts, capacity, width)
        .transpose(1, 0, 2, 3)
        .reshape(local_experts, sources * capacity, width)
    )


def source_major(results, sources, capacity):
    local_experts, _, width = results.shape
    return (
        results.reshape(local_experts, sources, capacity, width)
        .transpose(1, 0, 2, 3)
        .reshape(sources, local_experts * capacity, width)
    )


def _project_kernel(inputs_ref, weights_ref, out_ref):
    out_ref[0] = jnp.dot(inputs_ref[...], weights_ref[0], preferred_element_type=jnp.float32)


def project(inputs, weights, blocks, tile=1024):
    tokens, depth = inputs.shape
    columns = weights.shape[2]
    return pl.pallas_call(
        _project_kernel,
        out_shape=jax.ShapeDtypeStruct((blocks, tokens, columns), jnp.float32),
        grid=(blocks, columns // tile),
        in_specs=[
            pl.BlockSpec((tokens, depth), lambda s, j: (0, 0)),
            pl.BlockSpec((1, depth, tile), lambda s, j: (s, 0, j)),
        ],
        out_specs=pl.BlockSpec((1, tokens, tile), lambda s, j: (s, 0, j)),
        cost_estimate=pl.CostEstimate(
            flops=2 * tokens * depth * columns * blocks,
            transcendentals=0,
            bytes_accessed=2 * depth * columns * blocks + 2 * tokens * depth
            + 4 * tokens * columns * blocks,
        ),
    )(inputs, weights)


def _dispatch_kernel(slot_ref, weight_ref, rows_ref, grad_ref, send_ref, grad_send_ref):
    tile = send_ref.shape[0]
    top, tokens = slot_ref.shape
    slot = pl.program_id(0) * tile + lax.broadcasted_iota(jnp.int32, (tile, tokens), 0)
    hit = slot == slot_ref[0:1, :]
    weight = jnp.where(hit, weight_ref[0:1, :], 0.0)
    for k in range(1, top):
        match = slot == slot_ref[k : k + 1, :]
        hit = hit | match
        weight = weight + jnp.where(match, weight_ref[k : k + 1, :], 0.0)
    pick = hit.astype(jnp.bfloat16)
    send_ref[...] = jnp.dot(pick, rows_ref[...], preferred_element_type=jnp.float32).astype(
        send_ref.dtype
    )
    picked_grad = jnp.dot(pick, grad_ref[...], preferred_element_type=jnp.float32)
    slot_weight = jnp.sum(weight, axis=1, keepdims=True)
    grad_send_ref[...] = (slot_weight * picked_grad).astype(grad_send_ref.dtype)


def dispatch(route_slots, route_weights, rows, grad, slots, tile=256):
    top, tokens = route_slots.shape
    width = rows.shape[1]
    out = jax.ShapeDtypeStruct((slots, width), jnp.bfloat16)
    return pl.pallas_call(
        _dispatch_kernel,
        out_shape=(out, out),
        grid=(slots // tile,),
        in_specs=[
            pl.BlockSpec((top, tokens), lambda i: (0, 0)),
            pl.BlockSpec((top, tokens), lambda i: (0, 0)),
            pl.BlockSpec((tokens, width), lambda i: (0, 0)),
            pl.BlockSpec((tokens, width), lambda i: (0, 0)),
        ],
        out_specs=(
            pl.BlockSpec((tile, width), lambda i: (i, 0)),
            pl.BlockSpec((tile, width), lambda i: (i, 0)),
        ),
        cost_estimate=pl.CostEstimate(
            flops=4 * slots * tokens * width,
            transcendentals=0,
            bytes_accessed=4 * slots * width + 4 * tokens * width + 8 * top * tokens,
        ),
    )(route_slots, route_weights, rows, grad)


def _combine_kernel(with_dots, slot_ref, weight_ref, table_ref, base_ref, other_ref, out_ref, dots_ref):
    tokens, top = slot_ref.shape
    count = table_ref.shape[0]
    column = lax.broadcasted_iota(jnp.int32, (tokens, count), 1)
    if not with_dots:
        hit = slot_ref[:, 0:1] == column
        for k in range(1, top):
            hit = hit | (slot_ref[:, k : k + 1] == column)
        out_ref[...] = base_ref[...] + jnp.dot(
            hit.astype(jnp.bfloat16), table_ref[...], preferred_element_type=jnp.float32
        )
        dots_ref[...] = jnp.zeros_like(dots_ref)
        return
    total = base_ref[...]
    for k in range(top):
        pick = (slot_ref[:, k : k + 1] == column).astype(jnp.bfloat16)
        row = jnp.dot(pick, table_ref[...], preferred_element_type=jnp.float32)
        total = total + weight_ref[:, k : k + 1] * row
        dots_ref[:, k : k + 1] = jnp.sum(
            other_ref[...].astype(jnp.float32) * row, axis=1, keepdims=True
        )
    out_ref[...] = total


def combine(slots, weights, table, base, other, with_dots):
    tokens, top = slots.shape
    count, width = table.shape
    return pl.pallas_call(
        functools.partial(_combine_kernel, with_dots),
        out_shape=(
            jax.ShapeDtypeStruct((tokens, width), jnp.float32),
            jax.ShapeDtypeStruct((tokens, top), jnp.float32),
        ),
        in_specs=[pl.BlockSpec(memory_space=pltpu.VMEM)] * 5,
        out_specs=(pl.BlockSpec(memory_space=pltpu.VMEM), pl.BlockSpec(memory_space=pltpu.VMEM)),
        cost_estimate=pl.CostEstimate(
            flops=2 * tokens * count * width * top,
            transcendentals=0,
            bytes_accessed=2 * count * width + 10 * tokens * width,
        ),
    )(slots, weights, table, base, other)


def sum_halves(values, axis, dim):
    half = values.shape[dim] // 2
    index = lax.axis_index(axis)
    own = lax.dynamic_slice_in_dim(values, index * half, half, axis=dim)
    given = lax.dynamic_slice_in_dim(values, (1 - index) * half, half, axis=dim)
    received = lax.ppermute(given.astype(jnp.bfloat16), axis, [(0, 1), (1, 0)])
    return own + received.astype(own.dtype)


def swap_context(values):
    return lax.ppermute(values, "context", [(0, 1), (1, 0)])


def gather_context(values):
    other = swap_context(values)
    first = lax.axis_index("context") == 0
    return jnp.concatenate(
        [jnp.where(first, values, other), jnp.where(first, other, values)], axis=0
    )


def sum_context_halves(values):
    half = values.shape[0] // 2
    first = lax.axis_index("context") == 0
    own = jnp.where(first, values[:half], values[half:])
    given = jnp.where(first, values[half:], values[:half]).astype(jnp.bfloat16)
    return own + swap_context(given).astype(own.dtype)


def butterfly_sum(values, axes):
    index = lax.axis_index(axes)
    count = 1
    for name in axes:
        count *= lax.axis_size(name)
    step = 1
    while step < count:
        partner = [(i, i ^ step) for i in range(count)]
        received = lax.ppermute(values, axes, partner)
        mine_first = (index & step) == 0
        values = jnp.where(mine_first, values + received, received + values)
        step *= 2
    return values


def body(
    tokens,
    grad_output,
    routes,
    positions,
    attn_gain,
    q_gain,
    k_gain,
    ffn_gain,
    qkv_weight,
    out_weight,
    router_weight,
    expert_in,
    expert_out,
):
    single_precision = jnp.float32
    bf16 = jnp.bfloat16
    seq_tok = tokens.shape[1]
    width = tokens.shape[2]
    top = routes.shape[2]
    heads_width = out_weight.shape[1]
    head_dim = HDIM
    heads = heads_width // head_dim
    local_experts = expert_in.shape[0]
    experts = router_weight.shape[1]
    sources = lax.axis_size("expert")
    capacity = min(seq_tok, seq_tok * top * 5 // (4 * experts))
    scale = head_dim ** (-0.5)
    x = tokens[0].astype(single_precision)
    normed1, factor1 = rms_forward(x)
    attention_input = (normed1 * attn_gain).astype(bf16)
    all_axes = ("dp", "context", "expert")
    weights_full = lax.all_gather(
        jnp.concatenate([qkv_weight.transpose(1, 0, 2), out_weight[:, None, :]], axis=1),
        all_axes,
        axis=0,
        tiled=True,
    )
    out_full = weights_full[:, 3, :]
    both_inputs = gather_context(attention_input)
    projected_both = project(both_inputs, weights_full.transpose(1, 0, 2), 3)
    own_start = lax.axis_index("context") * seq_tok
    projected_output = lax.dynamic_slice_in_dim(projected_both, own_start, seq_tok, axis=1)
    q_normed, q_factor = rms_forward(projected_output[0])
    k_normed, k_factor = rms_forward(projected_output[1])
    all_places = positions[0]
    own_places = lax.dynamic_slice_in_dim(all_places, own_start, seq_tok)
    cosine, sine = rope_tables(own_places, head_dim)
    all_cosine, all_sine = rope_tables(all_places, head_dim)
    queries = rotate(
        (q_normed * q_gain).reshape(seq_tok, heads, head_dim), cosine, sine, 1.0
    ).astype(bf16)
    seq_len = both_inputs.shape[0]
    keys_normed, _ = rms_forward(projected_both[1])
    keys = rotate(
        (keys_normed * k_gain).reshape(seq_len, heads, head_dim), all_cosine, all_sine, 1.0
    ).astype(bf16)
    vals = projected_both[2].astype(bf16)
    keys3 = keys.reshape(seq_len, heads, head_dim)
    vals3 = vals.reshape(seq_len, heads, head_dim)
    allowed = (all_places[None, :] <= own_places[:, None])[None]

    def masked_scores():
        scores = (
            jnp.einsum("qhd,khd->hqk", queries, keys3, preferred_element_type=single_precision)
            * scale
        )
        return jnp.where(allowed, scores, -jnp.inf)

    scores = masked_scores()
    lse = jnp.log(jnp.sum(jnp.exp(scores), axis=-1, keepdims=True))
    probs_b = jnp.exp(scores - lse).astype(bf16)
    attended = (
        jnp.einsum("hqk,khd->qhd", probs_b, vals3, preferred_element_type=single_precision)
        .astype(bf16)
        .reshape(seq_tok, heads_width)
    )
    mid = x + jnp.einsum("tq,dq->td", attended, out_full, preferred_element_type=single_precision)
    normed2, factor2 = rms_forward(mid)
    ffn_in = (normed2 * ffn_gain).astype(bf16)
    router_exp = jnp.exp(jnp.dot(ffn_in, router_weight, preferred_element_type=single_precision))
    router_probs = router_exp / jnp.sum(router_exp, axis=-1, keepdims=True)
    own_routes = routes[0]
    slots = slot_index(own_routes.reshape(-1), experts, capacity)
    expert_ids = jnp.arange(experts, dtype=jnp.int32)
    route_weight = jnp.sum(
        jnp.where(own_routes[:, :, None] == expert_ids, router_probs[:, None, :], 0.0), axis=2
    )
    route_slots = slots.reshape(seq_tok, top)
    send, grad_send = dispatch(
        route_slots.T, route_weight.T, ffn_in, grad_output[0], experts * capacity
    )
    received = lax.all_to_all(
        send.reshape(sources, local_experts * capacity, width),
        "expert",
        split_axis=0,
        concat_axis=0,
        tiled=True,
    )
    rows = expert_major(received, local_experts, capacity)
    gate_up = jnp.einsum("lrd,lkdh->lkrh", rows, expert_in, preferred_element_type=single_precision)
    gate = gate_up[:, 0]
    up = gate_up[:, 1]
    sig = jax.nn.sigmoid(gate)
    hidden = (gate * sig * up).astype(bf16)
    results = jnp.einsum(
        "lrh,lhd->lrd", hidden, expert_out, preferred_element_type=single_precision
    ).astype(bf16)
    back = lax.all_to_all(
        source_major(results, sources, capacity), "expert", split_axis=0, concat_axis=0, tiled=True
    )
    output, route_grad_weight = combine(
        route_slots,
        route_weight,
        back.reshape(experts * capacity, width),
        mid,
        grad_output[0],
        True,
    )
    grad = grad_output[0].astype(single_precision)
    grad_received = lax.all_to_all(
        grad_send.reshape(sources, local_experts * capacity, width),
        "expert",
        split_axis=0,
        concat_axis=0,
        tiled=True,
    )
    grad_rows = expert_major(grad_received, local_experts, capacity)
    grad_hidden = jnp.einsum(
        "lrd,lhd->lrh", grad_rows, expert_out, preferred_element_type=single_precision
    )
    grad_down = jnp.einsum(
        "lrh,lrd->lhd", hidden, grad_rows, preferred_element_type=single_precision
    )
    grad_gate = (grad_hidden * up * sig * (1.0 + gate * (1.0 - sig))).astype(bf16)
    grad_up = (grad_hidden * gate * sig).astype(bf16)
    grad_gate_up = jnp.stack([grad_gate, grad_up], axis=1)
    grad_gate_up_w = jnp.einsum(
        "lrd,lkrh->lkdh", rows, grad_gate_up, preferred_element_type=single_precision
    )
    grad_rows_in = jnp.einsum(
        "lkrh,lkdh->lrd", grad_gate_up, expert_in, preferred_element_type=single_precision
    ).astype(bf16)
    grad_back = lax.all_to_all(
        source_major(grad_rows_in, sources, capacity),
        "expert",
        split_axis=0,
        concat_axis=0,
        tiled=True,
    )
    chosen = (own_routes[:, :, None] == jnp.arange(experts, dtype=jnp.int32)[None, None, :]).astype(
        single_precision
    )
    grad_probs = jnp.sum(route_grad_weight[:, :, None] * chosen, axis=1)
    grad_logits = (
        router_probs * (grad_probs - jnp.sum(router_probs * grad_probs, axis=-1, keepdims=True))
    ).astype(bf16)
    grad_router = jnp.einsum(
        "td,te->de", ffn_in, grad_logits, preferred_element_type=single_precision
    )
    grad_ffn_in, _ = combine(
        route_slots,
        jnp.ones((seq_tok, top), single_precision),
        grad_back.reshape(experts * capacity, width),
        jnp.einsum("te,de->td", grad_logits, router_weight, preferred_element_type=single_precision),
        grad_output[0],
        False,
    )
    grad_mid_norm, grad_ffn_gain = rms_backward(grad_ffn_in, normed2, factor2, ffn_gain)
    grad_mid = grad + grad_mid_norm
    grad_mid_b = grad_mid.astype(bf16)
    grad_att = (
        jnp.einsum("td,dq->tq", grad_mid_b, out_full, preferred_element_type=single_precision)
        .astype(bf16)
        .reshape(seq_tok, heads, head_dim)
    )
    delta = jnp.sum(
        grad_att.astype(single_precision)
        * attended.reshape(seq_tok, heads, head_dim).astype(single_precision),
        axis=-1,
    )
    probs = jnp.exp(masked_scores() - lse)
    grad_vals = jnp.einsum(
        "hqk,qhd->khd", probs.astype(bf16), grad_att, preferred_element_type=single_precision
    )
    grad_p = jnp.einsum("qhd,khd->hqk", grad_att, vals3, preferred_element_type=single_precision)
    grad_scores = (probs * (grad_p - delta.T[:, :, None])).astype(bf16)
    grad_queries = (
        jnp.einsum("hqk,khd->qhd", grad_scores, keys3, preferred_element_type=single_precision)
        * scale
    )
    grad_keys_all = (
        jnp.einsum("hqk,qhd->khd", grad_scores, queries, preferred_element_type=single_precision)
        * scale
    )
    grad_values = sum_context_halves(grad_vals.reshape(seq_len, heads_width))
    grad_keys = sum_context_halves(grad_keys_all.reshape(seq_len, heads_width))
    grad_qn = rotate(grad_queries, cosine, sine, -1.0).reshape(seq_tok, heads_width)
    grad_kn = rotate(grad_keys.reshape(seq_tok, heads, head_dim), cosine, sine, -1.0).reshape(
        seq_tok, heads_width
    )
    grad_q_raw, grad_q_gain = rms_backward(grad_qn, q_normed, q_factor, q_gain)
    grad_k_raw, grad_k_gain = rms_backward(grad_kn, k_normed, k_factor, k_gain)
    projected_gradient = jnp.stack(
        [grad_q_raw, grad_k_raw, grad_values, jnp.zeros_like(grad_values)], axis=1
    ).astype(bf16)
    attention_input_gradient = jnp.dot(
        projected_gradient.reshape(seq_tok, 4 * heads_width),
        weights_full.reshape(width, 4 * heads_width).T,
        preferred_element_type=single_precision,
    )
    grad_x_norm, grad_attn_gain = rms_backward(
        attention_input_gradient, normed1, factor1, attn_gain
    )
    grad_tokens = grad_mid + grad_x_norm
    def scatter_over_copies(values):
        return sum_halves(sum_halves(values, "dp", 1), "context", 1)

    grad_in_shard = scatter_over_copies(grad_gate_up_w[0])[None]
    grad_down_shard = scatter_over_copies(grad_down[0])[None]
    left = jnp.stack([attention_input] * 3 + [grad_mid_b])
    right = jnp.concatenate(
        [projected_gradient[:, :3].transpose(1, 0, 2), attended[None]], axis=0
    )
    stacked = jnp.einsum("sta,stb->sab", left, right, preferred_element_type=single_precision)
    summed = lax.psum(stacked.astype(bf16), all_axes)
    shard_rows = width // lax.axis_size(all_axes)
    start = lax.axis_index(all_axes) * shard_rows
    weight_shard = lax.dynamic_slice_in_dim(summed, start, shard_rows, axis=1).astype(
        single_precision
    )
    grad_qkv_shard = weight_shard[:3]
    grad_out_shard = weight_shard[3]
    small_sum = butterfly_sum(
        jnp.concatenate(
            [grad_attn_gain, grad_q_gain, grad_k_gain, grad_ffn_gain, grad_router.reshape(-1)]
        ),
        all_axes,
    )
    sizes = [width, heads_width, heads_width, width, width * experts]
    offsets = [sum(sizes[:n]) for n in range(len(sizes))]
    totals = [small_sum[o : o + n] for o, n in zip(offsets, sizes)]
    totals[4] = totals[4].reshape(width, experts)
    return (
        output[None],
        grad_tokens[None],
        totals[0],
        totals[1],
        totals[2],
        totals[3],
        totals[4],
        grad_qkv_shard,
        grad_out_shard,
        grad_in_shard,
        grad_down_shard,
    )


def solution(mesh):
    return jax.shard_map(
        body,
        mesh=mesh,
        in_specs=(
            P(("dp", "expert"), "context", None),
            P(("dp", "expert"), "context", None),
            P(("dp", "expert"), "context", None),
            P(("dp", "expert"), None),
            P(),
            P(),
            P(),
            P(),
            P(None, ("dp", "context", "expert"), None),
            P(("dp", "context", "expert"), None),
            P(),
            P("expert", None, None, None),
            P("expert", None, None),
        ),
        out_specs=(
            P(("dp", "expert"), "context", None),
            P(("dp", "expert"), "context", None),
            P(),
            P(),
            P(),
            P(),
            P(),
            P(None, ("dp", "context", "expert"), None),
            P(("dp", "context", "expert"), None),
            P("expert", None, ("dp", "context"), None),
            P("expert", None, ("dp", "context")),
        ),
        check_vma=False,
    )
```

```python
import functools

import jax
import jax.numpy as jnp
from jax import lax
from jax.experimental import pallas as pl
from jax.experimental.pallas import tpu as pltpu
from jax.sharding import PartitionSpec as P

HDIM = 128


EPS = 1e-05
THETA = 10000.0


def rope_tables(places, head_dim):
    half = head_dim // 2
    freq = THETA ** (-jnp.arange(half, dtype=jnp.float32) * 2.0 / head_dim)
    angle = places.astype(jnp.float32)[:, None] * freq[None, :]
    return (jnp.cos(angle), jnp.sin(angle))


def rotate(values, cosine, sine, sign):
    half = values.shape[-1] // 2
    first = values[..., :half]
    second = values[..., half:]
    cosine = cosine[:, None, :]
    sine = sign * sine[:, None, :]
    return jnp.concatenate(
        [first * cosine - second * sine, second * cosine + first * sine], axis=-1
    )


def rms_forward(values):
    factor = lax.rsqrt(jnp.mean(values * values, axis=-1, keepdims=True) + EPS)
    return (values * factor, factor)


def rms_backward(grad_out, normed, factor, gain):
    scaled = grad_out * gain
    grad_in = factor * (scaled - normed * jnp.mean(scaled * normed, axis=-1, keepdims=True))
    return (grad_in, jnp.sum(grad_out * normed, axis=0))


def slot_index(route_rows, experts, capacity):
    onehot = (route_rows[:, None] == jnp.arange(experts, dtype=jnp.int32)[None, :]).astype(
        jnp.int32
    )
    count = route_rows.shape[0]
    earlier = (
        jnp.arange(count, dtype=jnp.int32)[None, :] < jnp.arange(count, dtype=jnp.int32)[:, None]
    ).astype(jnp.bfloat16)
    before = jnp.dot(earlier, onehot.astype(jnp.bfloat16), preferred_element_type=jnp.float32)
    return route_rows * capacity + jnp.sum(before.astype(jnp.int32) * onehot, axis=1)


def expert_major(received, local_experts, capacity):
    sources, _, width = received.shape
    return (
        received.reshape(sources, local_experts, capacity, width)
        .transpose(1, 0, 2, 3)
        .reshape(local_experts, sources * capacity, width)
    )


def source_major(results, sources, capacity):
    local_experts, _, width = results.shape
    return (
        results.reshape(local_experts, sources, capacity, width)
        .transpose(1, 0, 2, 3)
        .reshape(sources, local_experts * capacity, width)
    )


def _project_kernel(inputs_ref, weights_ref, out_ref):
    out_ref[0] = jnp.dot(inputs_ref[...], weights_ref[0], preferred_element_type=jnp.float32)


def project(inputs, weights, blocks, tile=1024):
    tokens, depth = inputs.shape
    columns = weights.shape[2]
    return pl.pallas_call(
        _project_kernel,
        out_shape=jax.ShapeDtypeStruct((blocks, tokens, columns), jnp.float32),
        grid=(blocks, columns // tile),
        in_specs=[
            pl.BlockSpec((tokens, depth), lambda s, j: (0, 0)),
            pl.BlockSpec((1, depth, tile), lambda s, j: (s, 0, j)),
        ],
        out_specs=pl.BlockSpec((1, tokens, tile), lambda s, j: (s, 0, j)),
        cost_estimate=pl.CostEstimate(
            flops=2 * tokens * depth * columns * blocks,
            transcendentals=0,
            bytes_accessed=2 * depth * columns * blocks + 2 * tokens * depth
            + 4 * tokens * columns * blocks,
        ),
    )(inputs, weights)


def _dispatch_kernel(slot_ref, weight_ref, rows_ref, grad_ref, send_ref, grad_send_ref):
    tile = send_ref.shape[0]
    top, tokens = slot_ref.shape
    slot = pl.program_id(0) * tile + lax.broadcasted_iota(jnp.int32, (tile, tokens), 0)
    hit = slot == slot_ref[0:1, :]
    weight = jnp.where(hit, weight_ref[0:1, :], 0.0)
    for k in range(1, top):
        match = slot == slot_ref[k : k + 1, :]
        hit = hit | match
        weight = weight + jnp.where(match, weight_ref[k : k + 1, :], 0.0)
    pick = hit.astype(jnp.bfloat16)
    send_ref[...] = jnp.dot(pick, rows_ref[...], preferred_element_type=jnp.float32).astype(
        send_ref.dtype
    )
    picked_grad = jnp.dot(pick, grad_ref[...], preferred_element_type=jnp.float32)
    slot_weight = jnp.sum(weight, axis=1, keepdims=True)
    grad_send_ref[...] = (slot_weight * picked_grad).astype(grad_send_ref.dtype)


def dispatch(route_slots, route_weights, rows, grad, slots, tile=640):
    top, tokens = route_slots.shape
    width = rows.shape[1]
    out = jax.ShapeDtypeStruct((slots, width), jnp.bfloat16)
    return pl.pallas_call(
        _dispatch_kernel,
        out_shape=(out, out),
        grid=(slots // tile,),
        in_specs=[
            pl.BlockSpec((top, tokens), lambda i: (0, 0)),
            pl.BlockSpec((top, tokens), lambda i: (0, 0)),
            pl.BlockSpec((tokens, width), lambda i: (0, 0)),
            pl.BlockSpec((tokens, width), lambda i: (0, 0)),
        ],
        out_specs=(
            pl.BlockSpec((tile, width), lambda i: (i, 0)),
            pl.BlockSpec((tile, width), lambda i: (i, 0)),
        ),
        cost_estimate=pl.CostEstimate(
            flops=4 * slots * tokens * width,
            transcendentals=0,
            bytes_accessed=4 * slots * width + 4 * tokens * width + 8 * top * tokens,
        ),
    )(route_slots, route_weights, rows, grad)


def _combine_kernel(with_dots, slot_ref, weight_ref, table_ref, base_ref, other_ref, out_ref, dots_ref):
    tokens, top = slot_ref.shape
    count = table_ref.shape[0]
    column = lax.broadcasted_iota(jnp.int32, (tokens, count), 1)
    if not with_dots:
        hit = slot_ref[:, 0:1] == column
        for k in range(1, top):
            hit = hit | (slot_ref[:, k : k + 1] == column)
        out_ref[...] = base_ref[...] + jnp.dot(
            hit.astype(jnp.bfloat16), table_ref[...], preferred_element_type=jnp.float32
        )
        dots_ref[...] = jnp.zeros_like(dots_ref)
        return
    total = base_ref[...]
    for k in range(top):
        pick = (slot_ref[:, k : k + 1] == column).astype(jnp.bfloat16)
        row = jnp.dot(pick, table_ref[...], preferred_element_type=jnp.float32)
        total = total + weight_ref[:, k : k + 1] * row
        dots_ref[:, k : k + 1] = jnp.sum(
            other_ref[...].astype(jnp.float32) * row, axis=1, keepdims=True
        )
    out_ref[...] = total


def combine(slots, weights, table, base, other, with_dots):
    tokens, top = slots.shape
    count, width = table.shape
    return pl.pallas_call(
        functools.partial(_combine_kernel, with_dots),
        out_shape=(
            jax.ShapeDtypeStruct((tokens, width), jnp.float32),
            jax.ShapeDtypeStruct((tokens, top), jnp.float32),
        ),
        in_specs=[pl.BlockSpec(memory_space=pltpu.VMEM)] * 5,
        out_specs=(pl.BlockSpec(memory_space=pltpu.VMEM), pl.BlockSpec(memory_space=pltpu.VMEM)),
        cost_estimate=pl.CostEstimate(
            flops=2 * tokens * count * width * top,
            transcendentals=0,
            bytes_accessed=2 * count * width + 10 * tokens * width,
        ),
    )(slots, weights, table, base, other)


def sum_halves(values, axis, dim):
    half = values.shape[dim] // 2
    index = lax.axis_index(axis)
    own = lax.dynamic_slice_in_dim(values, index * half, half, axis=dim)
    given = lax.dynamic_slice_in_dim(values, (1 - index) * half, half, axis=dim)
    received = lax.ppermute(given.astype(jnp.bfloat16), axis, [(0, 1), (1, 0)])
    return own + received.astype(own.dtype)


def swap_context(values):
    return lax.ppermute(values, "context", [(0, 1), (1, 0)])


def gather_context(values):
    other = swap_context(values)
    first = lax.axis_index("context") == 0
    return jnp.concatenate(
        [jnp.where(first, values, other), jnp.where(first, other, values)], axis=0
    )


def sum_context_halves(values):
    half = values.shape[0] // 2
    first = lax.axis_index("context") == 0
    own = jnp.where(first, values[:half], values[half:])
    given = jnp.where(first, values[half:], values[:half]).astype(jnp.bfloat16)
    return own + swap_context(given).astype(own.dtype)


def butterfly_sum(values, axes):
    index = lax.axis_index(axes)
    count = 1
    for name in axes:
        count *= lax.axis_size(name)
    step = 1
    while step < count:
        partner = [(i, i ^ step) for i in range(count)]
        received = lax.ppermute(values, axes, partner)
        mine_first = (index & step) == 0
        values = jnp.where(mine_first, values + received, received + values)
        step *= 2
    return values


def body(
    tokens,
    grad_output,
    routes,
    positions,
    attn_gain,
    q_gain,
    k_gain,
    ffn_gain,
    qkv_weight,
    out_weight,
    router_weight,
    expert_in,
    expert_out,
):
    single_precision = jnp.float32
    bf16 = jnp.bfloat16
    seq_tok = tokens.shape[1]
    width = tokens.shape[2]
    top = routes.shape[2]
    heads_width = out_weight.shape[1]
    head_dim = HDIM
    heads = heads_width // head_dim
    local_experts = expert_in.shape[0]
    experts = router_weight.shape[1]
    sources = lax.axis_size("expert")
    capacity = min(seq_tok, seq_tok * top * 5 // (4 * experts))
    scale = head_dim ** (-0.5)
    x = tokens[0].astype(single_precision)
    normed1, factor1 = rms_forward(x)
    attention_input = (normed1 * attn_gain).astype(bf16)
    all_axes = ("dp", "context", "expert")
    weights_full = lax.all_gather(
        jnp.concatenate([qkv_weight.transpose(1, 0, 2), out_weight[:, None, :]], axis=1),
        all_axes,
        axis=0,
        tiled=True,
    )
    out_full = weights_full[:, 3, :]
    both_inputs = gather_context(attention_input)
    projected_both = project(both_inputs, weights_full.transpose(1, 0, 2), 3)
    own_start = lax.axis_index("context") * seq_tok
    projected_output = lax.dynamic_slice_in_dim(projected_both, own_start, seq_tok, axis=1)
    q_normed, q_factor = rms_forward(projected_output[0])
    k_normed, k_factor = rms_forward(projected_output[1])
    all_places = positions[0]
    own_places = lax.dynamic_slice_in_dim(all_places, own_start, seq_tok)
    cosine, sine = rope_tables(own_places, head_dim)
    all_cosine, all_sine = rope_tables(all_places, head_dim)
    queries = rotate(
        (q_normed * q_gain).reshape(seq_tok, heads, head_dim), cosine, sine, 1.0
    ).astype(bf16)
    seq_len = both_inputs.shape[0]
    keys_normed, _ = rms_forward(projected_both[1])
    keys = rotate(
        (keys_normed * k_gain).reshape(seq_len, heads, head_dim), all_cosine, all_sine, 1.0
    ).astype(bf16)
    vals = projected_both[2].astype(bf16)
    keys3 = keys.reshape(seq_len, heads, head_dim)
    vals3 = vals.reshape(seq_len, heads, head_dim)
    allowed = (all_places[None, :] <= own_places[:, None])[None]

    def masked_scores():
        scores = (
            jnp.einsum("qhd,khd->hqk", queries, keys3, preferred_element_type=single_precision)
            * scale
        )
        return jnp.where(allowed, scores, -jnp.inf)

    scores = masked_scores()
    lse = jnp.log(jnp.sum(jnp.exp(scores), axis=-1, keepdims=True))
    probs_b = jnp.exp(scores - lse).astype(bf16)
    attended = (
        jnp.einsum("hqk,khd->qhd", probs_b, vals3, preferred_element_type=single_precision)
        .astype(bf16)
        .reshape(seq_tok, heads_width)
    )
    mid = x + jnp.einsum("tq,dq->td", attended, out_full, preferred_element_type=single_precision)
    normed2, factor2 = rms_forward(mid)
    ffn_in = (normed2 * ffn_gain).astype(bf16)
    router_exp = jnp.exp(jnp.dot(ffn_in, router_weight, preferred_element_type=single_precision))
    router_probs = router_exp / jnp.sum(router_exp, axis=-1, keepdims=True)
    own_routes = routes[0]
    slots = slot_index(own_routes.reshape(-1), experts, capacity)
    expert_ids = jnp.arange(experts, dtype=jnp.int32)
    route_weight = jnp.sum(
        jnp.where(own_routes[:, :, None] == expert_ids, router_probs[:, None, :], 0.0), axis=2
    )
    route_slots = slots.reshape(seq_tok, top)
    send, grad_send = dispatch(
        route_slots.T, route_weight.T, ffn_in, grad_output[0], experts * capacity
    )
    received = lax.all_to_all(
        send.reshape(sources, local_experts * capacity, width),
        "expert",
        split_axis=0,
        concat_axis=0,
        tiled=True,
    )
    rows = expert_major(received, local_experts, capacity)
    gate_up = jnp.einsum("lrd,lkdh->lkrh", rows, expert_in, preferred_element_type=single_precision)
    gate = gate_up[:, 0]
    up = gate_up[:, 1]
    sig = jax.nn.sigmoid(gate)
    hidden = (gate * sig * up).astype(bf16)
    results = jnp.einsum(
        "lrh,lhd->lrd", hidden, expert_out, preferred_element_type=single_precision
    ).astype(bf16)
    back = lax.all_to_all(
        source_major(results, sources, capacity), "expert", split_axis=0, concat_axis=0, tiled=True
    )
    output, route_grad_weight = combine(
        route_slots,
        route_weight,
        back.reshape(experts * capacity, width),
        mid,
        grad_output[0],
        True,
    )
    grad = grad_output[0].astype(single_precision)
    grad_received = lax.all_to_all(
        grad_send.reshape(sources, local_experts * capacity, width),
        "expert",
        split_axis=0,
        concat_axis=0,
        tiled=True,
    )
    grad_rows = expert_major(grad_received, local_experts, capacity)
    grad_hidden = jnp.einsum(
        "lrd,lhd->lrh", grad_rows, expert_out, preferred_element_type=single_precision
    )
    grad_down = jnp.einsum(
        "lrh,lrd->lhd", hidden, grad_rows, preferred_element_type=single_precision
    )
    grad_gate = (grad_hidden * up * sig * (1.0 + gate * (1.0 - sig))).astype(bf16)
    grad_up = (grad_hidden * gate * sig).astype(bf16)
    grad_gate_up = jnp.stack([grad_gate, grad_up], axis=1)
    grad_gate_up_w = jnp.einsum(
        "lrd,lkrh->lkdh", rows, grad_gate_up, preferred_element_type=single_precision
    )
    grad_rows_in = jnp.einsum(
        "lkrh,lkdh->lrd", grad_gate_up, expert_in, preferred_element_type=single_precision
    ).astype(bf16)
    grad_back = lax.all_to_all(
        source_major(grad_rows_in, sources, capacity),
        "expert",
        split_axis=0,
        concat_axis=0,
        tiled=True,
    )
    chosen = (own_routes[:, :, None] == jnp.arange(experts, dtype=jnp.int32)[None, None, :]).astype(
        single_precision
    )
    grad_probs = jnp.sum(route_grad_weight[:, :, None] * chosen, axis=1)
    grad_logits = (
        router_probs * (grad_probs - jnp.sum(router_probs * grad_probs, axis=-1, keepdims=True))
    ).astype(bf16)
    grad_router = jnp.einsum(
        "td,te->de", ffn_in, grad_logits, preferred_element_type=single_precision
    )
    grad_ffn_in, _ = combine(
        route_slots,
        jnp.ones((seq_tok, top), single_precision),
        grad_back.reshape(experts * capacity, width),
        jnp.einsum("te,de->td", grad_logits, router_weight, preferred_element_type=single_precision),
        grad_output[0],
        False,
    )
    grad_mid_norm, grad_ffn_gain = rms_backward(grad_ffn_in, normed2, factor2, ffn_gain)
    grad_mid = grad + grad_mid_norm
    grad_mid_b = grad_mid.astype(bf16)
    grad_att = (
        jnp.einsum("td,dq->tq", grad_mid_b, out_full, preferred_element_type=single_precision)
        .astype(bf16)
        .reshape(seq_tok, heads, head_dim)
    )
    delta = jnp.sum(
        grad_att.astype(single_precision)
        * attended.reshape(seq_tok, heads, head_dim).astype(single_precision),
        axis=-1,
    )
    probs = jnp.exp(masked_scores() - lse)
    grad_vals = jnp.einsum(
        "hqk,qhd->khd", probs.astype(bf16), grad_att, preferred_element_type=single_precision
    )
    grad_p = jnp.einsum("qhd,khd->hqk", grad_att, vals3, preferred_element_type=single_precision)
    grad_scores = (probs * (grad_p - delta.T[:, :, None])).astype(bf16)
    grad_queries = (
        jnp.einsum("hqk,khd->qhd", grad_scores, keys3, preferred_element_type=single_precision)
        * scale
    )
    grad_keys_all = (
        jnp.einsum("hqk,qhd->khd", grad_scores, queries, preferred_element_type=single_precision)
        * scale
    )
    grad_values = sum_context_halves(grad_vals.reshape(seq_len, heads_width))
    grad_keys = sum_context_halves(grad_keys_all.reshape(seq_len, heads_width))
    grad_qn = rotate(grad_queries, cosine, sine, -1.0).reshape(seq_tok, heads_width)
    grad_kn = rotate(grad_keys.reshape(seq_tok, heads, head_dim), cosine, sine, -1.0).reshape(
        seq_tok, heads_width
    )
    grad_q_raw, grad_q_gain = rms_backward(grad_qn, q_normed, q_factor, q_gain)
    grad_k_raw, grad_k_gain = rms_backward(grad_kn, k_normed, k_factor, k_gain)
    projected_gradient = jnp.stack(
        [grad_q_raw, grad_k_raw, grad_values, jnp.zeros_like(grad_values)], axis=1
    ).astype(bf16)
    attention_input_gradient = jnp.dot(
        projected_gradient.reshape(seq_tok, 4 * heads_width),
        weights_full.reshape(width, 4 * heads_width).T,
        preferred_element_type=single_precision,
    )
    grad_x_norm, grad_attn_gain = rms_backward(
        attention_input_gradient, normed1, factor1, attn_gain
    )
    grad_tokens = grad_mid + grad_x_norm
    def scatter_over_copies(values):
        return sum_halves(sum_halves(values, "dp", 1), "context", 1)

    grad_in_shard = scatter_over_copies(grad_gate_up_w[0])[None]
    grad_down_shard = scatter_over_copies(grad_down[0])[None]
    left = jnp.stack([attention_input] * 3 + [grad_mid_b])
    right = jnp.concatenate(
        [projected_gradient[:, :3].transpose(1, 0, 2), attended[None]], axis=0
    )
    stacked = jnp.einsum("sta,stb->sab", left, right, preferred_element_type=single_precision)
    summed = lax.psum(stacked.astype(bf16), all_axes)
    shard_rows = width // lax.axis_size(all_axes)
    start = lax.axis_index(all_axes) * shard_rows
    weight_shard = lax.dynamic_slice_in_dim(summed, start, shard_rows, axis=1).astype(
        single_precision
    )
    grad_qkv_shard = weight_shard[:3]
    grad_out_shard = weight_shard[3]
    small_sum = butterfly_sum(
        jnp.concatenate(
            [grad_attn_gain, grad_q_gain, grad_k_gain, grad_ffn_gain, grad_router.reshape(-1)]
        ),
        all_axes,
    )
    sizes = [width, heads_width, heads_width, width, width * experts]
    offsets = [sum(sizes[:n]) for n in range(len(sizes))]
    totals = [small_sum[o : o + n] for o, n in zip(offsets, sizes)]
    totals[4] = totals[4].reshape(width, experts)
    return (
        output[None],
        grad_tokens[None],
        totals[0],
        totals[1],
        totals[2],
        totals[3],
        totals[4],
        grad_qkv_shard,
        grad_out_shard,
        grad_in_shard,
        grad_down_shard,
    )


def solution(mesh):
    return jax.shard_map(
        body,
        mesh=mesh,
        in_specs=(
            P(("dp", "expert"), "context", None),
            P(("dp", "expert"), "context", None),
            P(("dp", "expert"), "context", None),
            P(("dp", "expert"), None),
            P(),
            P(),
            P(),
            P(),
            P(None, ("dp", "context", "expert"), None),
            P(("dp", "context", "expert"), None),
            P(),
            P("expert", None, None, None),
            P("expert", None, None),
        ),
        out_specs=(
            P(("dp", "expert"), "context", None),
            P(("dp", "expert"), "context", None),
            P(),
            P(),
            P(),
            P(),
            P(),
            P(None, ("dp", "context", "expert"), None),
            P(("dp", "context", "expert"), None),
            P("expert", None, ("dp", "context"), None),
            P("expert", None, ("dp", "context")),
        ),
        check_vma=False,
    )
```

```python
import functools

import jax
import jax.numpy as jnp
from jax import lax
from jax.experimental import pallas as pl
from jax.experimental.pallas import tpu as pltpu
from jax.sharding import PartitionSpec as P

HDIM = 128


EPS = 1e-05
THETA = 10000.0


def rope_tables(places, head_dim):
    half = head_dim // 2
    freq = THETA ** (-jnp.arange(half, dtype=jnp.float32) * 2.0 / head_dim)
    angle = places.astype(jnp.float32)[:, None] * freq[None, :]
    return (jnp.cos(angle), jnp.sin(angle))


def rotate(values, cosine, sine, sign):
    half = values.shape[-1] // 2
    first = values[..., :half]
    second = values[..., half:]
    cosine = cosine[:, None, :]
    sine = sign * sine[:, None, :]
    return jnp.concatenate(
        [first * cosine - second * sine, second * cosine + first * sine], axis=-1
    )


def rms_forward(values):
    factor = lax.rsqrt(jnp.mean(values * values, axis=-1, keepdims=True) + EPS)
    return (values * factor, factor)


def rms_backward(grad_out, normed, factor, gain):
    scaled = grad_out * gain
    grad_in = factor * (scaled - normed * jnp.mean(scaled * normed, axis=-1, keepdims=True))
    return (grad_in, jnp.sum(grad_out * normed, axis=0))


def slot_index(route_rows, experts, capacity):
    onehot = (route_rows[:, None] == jnp.arange(experts, dtype=jnp.int32)[None, :]).astype(
        jnp.int32
    )
    count = route_rows.shape[0]
    earlier = (
        jnp.arange(count, dtype=jnp.int32)[None, :] < jnp.arange(count, dtype=jnp.int32)[:, None]
    ).astype(jnp.bfloat16)
    before = jnp.dot(earlier, onehot.astype(jnp.bfloat16), preferred_element_type=jnp.float32)
    return route_rows * capacity + jnp.sum(before.astype(jnp.int32) * onehot, axis=1)


def expert_major(received, local_experts, capacity):
    sources, _, width = received.shape
    return (
        received.reshape(sources, local_experts, capacity, width)
        .transpose(1, 0, 2, 3)
        .reshape(local_experts, sources * capacity, width)
    )


def source_major(results, sources, capacity):
    local_experts, _, width = results.shape
    return (
        results.reshape(local_experts, sources, capacity, width)
        .transpose(1, 0, 2, 3)
        .reshape(sources, local_experts * capacity, width)
    )


def _project_kernel(inputs_ref, weights_ref, out_ref):
    out_ref[0] = jnp.dot(inputs_ref[...], weights_ref[0], preferred_element_type=jnp.float32)


def project(inputs, weights, blocks, tile=1024):
    tokens, depth = inputs.shape
    columns = weights.shape[2]
    return pl.pallas_call(
        _project_kernel,
        out_shape=jax.ShapeDtypeStruct((blocks, tokens, columns), jnp.float32),
        grid=(blocks, columns // tile),
        in_specs=[
            pl.BlockSpec((tokens, depth), lambda s, j: (0, 0)),
            pl.BlockSpec((1, depth, tile), lambda s, j: (s, 0, j)),
        ],
        out_specs=pl.BlockSpec((1, tokens, tile), lambda s, j: (s, 0, j)),
        cost_estimate=pl.CostEstimate(
            flops=2 * tokens * depth * columns * blocks,
            transcendentals=0,
            bytes_accessed=2 * depth * columns * blocks + 2 * tokens * depth
            + 4 * tokens * columns * blocks,
        ),
    )(inputs, weights)


def _dispatch_kernel(slot_ref, weight_ref, rows_ref, grad_ref, send_ref, grad_send_ref):
    tile = send_ref.shape[0]
    top, tokens = slot_ref.shape
    slot = pl.program_id(0) * tile + lax.broadcasted_iota(jnp.int32, (tile, tokens), 0)
    hit = slot == slot_ref[0:1, :]
    weight = jnp.where(hit, weight_ref[0:1, :], 0.0)
    for k in range(1, top):
        match = slot == slot_ref[k : k + 1, :]
        hit = hit | match
        weight = weight + jnp.where(match, weight_ref[k : k + 1, :], 0.0)
    pick = hit.astype(jnp.bfloat16)
    send_ref[...] = jnp.dot(pick, rows_ref[...], preferred_element_type=jnp.float32).astype(
        send_ref.dtype
    )
    picked_grad = jnp.dot(pick, grad_ref[...], preferred_element_type=jnp.float32)
    slot_weight = jnp.sum(weight, axis=1, keepdims=True)
    grad_send_ref[...] = (slot_weight * picked_grad).astype(grad_send_ref.dtype)


def dispatch(route_slots, route_weights, rows, grad, slots, tile=640):
    top, tokens = route_slots.shape
    width = rows.shape[1]
    out = jax.ShapeDtypeStruct((slots, width), jnp.bfloat16)
    return pl.pallas_call(
        _dispatch_kernel,
        out_shape=(out, out),
        grid=(slots // tile,),
        in_specs=[
            pl.BlockSpec((top, tokens), lambda i: (0, 0)),
            pl.BlockSpec((top, tokens), lambda i: (0, 0)),
            pl.BlockSpec((tokens, width), lambda i: (0, 0)),
            pl.BlockSpec((tokens, width), lambda i: (0, 0)),
        ],
        out_specs=(
            pl.BlockSpec((tile, width), lambda i: (i, 0)),
            pl.BlockSpec((tile, width), lambda i: (i, 0)),
        ),
        cost_estimate=pl.CostEstimate(
            flops=4 * slots * tokens * width,
            transcendentals=0,
            bytes_accessed=4 * slots * width + 4 * tokens * width + 8 * top * tokens,
        ),
    )(route_slots, route_weights, rows, grad)


def _combine_kernel(with_dots, slot_ref, weight_ref, table_ref, base_ref, other_ref, out_ref, dots_ref):
    tokens, top = slot_ref.shape
    count = table_ref.shape[0]
    column = lax.broadcasted_iota(jnp.int32, (tokens, count), 1)
    if not with_dots:
        hit = slot_ref[:, 0:1] == column
        for k in range(1, top):
            hit = hit | (slot_ref[:, k : k + 1] == column)
        out_ref[...] = base_ref[...] + jnp.dot(
            hit.astype(jnp.bfloat16), table_ref[...], preferred_element_type=jnp.float32
        )
        dots_ref[...] = jnp.zeros_like(dots_ref)
        return
    total = base_ref[...]
    for k in range(top):
        pick = (slot_ref[:, k : k + 1] == column).astype(jnp.bfloat16)
        row = jnp.dot(pick, table_ref[...], preferred_element_type=jnp.float32)
        total = total + weight_ref[:, k : k + 1] * row
        dots_ref[:, k : k + 1] = jnp.sum(
            other_ref[...].astype(jnp.float32) * row, axis=1, keepdims=True
        )
    out_ref[...] = total


def combine(slots, weights, table, base, other, with_dots):
    tokens, top = slots.shape
    count, width = table.shape
    return pl.pallas_call(
        functools.partial(_combine_kernel, with_dots),
        out_shape=(
            jax.ShapeDtypeStruct((tokens, width), jnp.float32),
            jax.ShapeDtypeStruct((tokens, top), jnp.float32),
        ),
        in_specs=[pl.BlockSpec(memory_space=pltpu.VMEM)] * 5,
        out_specs=(pl.BlockSpec(memory_space=pltpu.VMEM), pl.BlockSpec(memory_space=pltpu.VMEM)),
        cost_estimate=pl.CostEstimate(
            flops=2 * tokens * count * width * top,
            transcendentals=0,
            bytes_accessed=2 * count * width + 10 * tokens * width,
        ),
    )(slots, weights, table, base, other)


def sum_halves(values, axis, dim):
    half = values.shape[dim] // 2
    index = lax.axis_index(axis)
    own = lax.dynamic_slice_in_dim(values, index * half, half, axis=dim)
    given = lax.dynamic_slice_in_dim(values, (1 - index) * half, half, axis=dim)
    received = lax.ppermute(given.astype(jnp.bfloat16), axis, [(0, 1), (1, 0)])
    return own + received.astype(own.dtype)


def swap_context(values):
    return lax.ppermute(values, "context", [(0, 1), (1, 0)])


def gather_context(values):
    other = swap_context(values)
    first = lax.axis_index("context") == 0
    return jnp.concatenate(
        [jnp.where(first, values, other), jnp.where(first, other, values)], axis=0
    )


def sum_context_halves(values):
    half = values.shape[0] // 2
    first = lax.axis_index("context") == 0
    own = jnp.where(first, values[:half], values[half:])
    given = jnp.where(first, values[half:], values[:half]).astype(jnp.bfloat16)
    return own + swap_context(given).astype(own.dtype)


def butterfly_sum(values, axes):
    index = lax.axis_index(axes)
    count = 1
    for name in axes:
        count *= lax.axis_size(name)
    step = 1
    while step < count:
        partner = [(i, i ^ step) for i in range(count)]
        received = lax.ppermute(values, axes, partner)
        mine_first = (index & step) == 0
        values = jnp.where(mine_first, values + received, received + values)
        step *= 2
    return values


def body(
    tokens,
    grad_output,
    routes,
    positions,
    attn_gain,
    q_gain,
    k_gain,
    ffn_gain,
    qkv_weight,
    out_weight,
    router_weight,
    expert_in,
    expert_out,
):
    single_precision = jnp.float32
    bf16 = jnp.bfloat16
    seq_tok = tokens.shape[1]
    width = tokens.shape[2]
    top = routes.shape[2]
    heads_width = out_weight.shape[1]
    head_dim = HDIM
    heads = heads_width // head_dim
    local_experts = expert_in.shape[0]
    experts = router_weight.shape[1]
    sources = lax.axis_size("expert")
    capacity = min(seq_tok, seq_tok * top * 5 // (4 * experts))
    scale = head_dim ** (-0.5)
    x = tokens[0].astype(single_precision)
    normed1, factor1 = rms_forward(x)
    attention_input = (normed1 * attn_gain).astype(bf16)
    all_axes = ("dp", "context", "expert")
    weights_full = lax.all_gather(
        jnp.concatenate([qkv_weight.transpose(1, 0, 2), out_weight[:, None, :]], axis=1),
        all_axes,
        axis=0,
        tiled=True,
    )
    out_full = weights_full[:, 3, :]
    both_inputs = gather_context(attention_input)
    projected_both = project(both_inputs, weights_full.transpose(1, 0, 2), 3)
    own_start = lax.axis_index("context") * seq_tok
    projected_output = lax.dynamic_slice_in_dim(projected_both, own_start, seq_tok, axis=1)
    q_normed, q_factor = rms_forward(projected_output[0])
    k_normed, k_factor = rms_forward(projected_output[1])
    all_places = positions[0]
    own_places = lax.dynamic_slice_in_dim(all_places, own_start, seq_tok)
    cosine, sine = rope_tables(own_places, head_dim)
    all_cosine, all_sine = rope_tables(all_places, head_dim)
    queries = rotate(
        (q_normed * q_gain).reshape(seq_tok, heads, head_dim), cosine, sine, 1.0
    ).astype(bf16)
    seq_len = both_inputs.shape[0]
    keys_normed, _ = rms_forward(projected_both[1])
    keys = rotate(
        (keys_normed * k_gain).reshape(seq_len, heads, head_dim), all_cosine, all_sine, 1.0
    ).astype(bf16)
    vals = projected_both[2].astype(bf16)
    keys3 = keys.reshape(seq_len, heads, head_dim)
    vals3 = vals.reshape(seq_len, heads, head_dim)
    allowed = (all_places[None, :] <= own_places[:, None])[None]

    def masked_scores():
        scores = (
            jnp.einsum("qhd,khd->hqk", queries, keys3, preferred_element_type=single_precision)
            * scale
        )
        return jnp.where(allowed, scores, -jnp.inf)

    scores = masked_scores()
    lse = jnp.log(jnp.sum(jnp.exp(scores), axis=-1, keepdims=True))
    probs_b = jnp.exp(scores - lse).astype(bf16)
    attended = (
        jnp.einsum("hqk,khd->qhd", probs_b, vals3, preferred_element_type=single_precision)
        .astype(bf16)
        .reshape(seq_tok, heads_width)
    )
    mid = x + jnp.einsum("tq,dq->td", attended, out_full, preferred_element_type=single_precision)
    normed2, factor2 = rms_forward(mid)
    ffn_in = (normed2 * ffn_gain).astype(bf16)
    router_exp = jnp.exp(jnp.dot(ffn_in, router_weight, preferred_element_type=single_precision))
    router_probs = router_exp / jnp.sum(router_exp, axis=-1, keepdims=True)
    own_routes = routes[0]
    slots = slot_index(own_routes.reshape(-1), experts, capacity)
    expert_ids = jnp.arange(experts, dtype=jnp.int32)
    route_weight = jnp.sum(
        jnp.where(own_routes[:, :, None] == expert_ids, router_probs[:, None, :], 0.0), axis=2
    )
    route_slots = slots.reshape(seq_tok, top)
    send, grad_send = dispatch(
        route_slots.T, route_weight.T, ffn_in, grad_output[0], experts * capacity
    )
    received = lax.all_to_all(
        send.reshape(sources, local_experts * capacity, width),
        "expert",
        split_axis=0,
        concat_axis=0,
        tiled=True,
    )
    rows = expert_major(received, local_experts, capacity)
    gate_up = jnp.einsum("lrd,lkdh->lkrh", rows, expert_in, preferred_element_type=single_precision)
    gate = gate_up[:, 0]
    up = gate_up[:, 1]
    sig = jax.nn.sigmoid(gate)
    hidden = (gate * sig * up).astype(bf16)
    results = jnp.einsum(
        "lrh,lhd->lrd", hidden, expert_out, preferred_element_type=single_precision
    ).astype(bf16)
    back = lax.all_to_all(
        source_major(results, sources, capacity), "expert", split_axis=0, concat_axis=0, tiled=True
    )
    output, route_grad_weight = combine(
        route_slots,
        route_weight,
        back.reshape(experts * capacity, width),
        mid,
        grad_output[0],
        True,
    )
    grad = grad_output[0].astype(single_precision)
    grad_received = lax.all_to_all(
        grad_send.reshape(sources, local_experts * capacity, width),
        "expert",
        split_axis=0,
        concat_axis=0,
        tiled=True,
    )
    grad_rows = expert_major(grad_received, local_experts, capacity)
    grad_hidden = jnp.einsum(
        "lrd,lhd->lrh", grad_rows, expert_out, preferred_element_type=single_precision
    )
    grad_down = jnp.einsum(
        "lrh,lrd->lhd", hidden, grad_rows, preferred_element_type=single_precision
    )
    grad_gate = (grad_hidden * up * sig * (1.0 + gate * (1.0 - sig))).astype(bf16)
    grad_up = (grad_hidden * gate * sig).astype(bf16)
    grad_gate_up = jnp.stack([grad_gate, grad_up], axis=1)
    grad_gate_up_w = jnp.einsum(
        "lrd,lkrh->lkdh", rows, grad_gate_up, preferred_element_type=single_precision
    )
    grad_rows_in = jnp.einsum(
        "lkrh,lkdh->lrd", grad_gate_up, expert_in, preferred_element_type=single_precision
    ).astype(bf16)
    grad_back = lax.all_to_all(
        source_major(grad_rows_in, sources, capacity),
        "expert",
        split_axis=0,
        concat_axis=0,
        tiled=True,
    )
    chosen = (own_routes[:, :, None] == jnp.arange(experts, dtype=jnp.int32)[None, None, :]).astype(
        single_precision
    )
    grad_probs = jnp.sum(route_grad_weight[:, :, None] * chosen, axis=1)
    grad_logits = (
        router_probs * (grad_probs - jnp.sum(router_probs * grad_probs, axis=-1, keepdims=True))
    ).astype(bf16)
    grad_router = jnp.einsum(
        "td,te->de", ffn_in, grad_logits, preferred_element_type=single_precision
    )
    grad_ffn_in, _ = combine(
        route_slots,
        jnp.ones((seq_tok, top), single_precision),
        grad_back.reshape(experts * capacity, width),
        jnp.einsum("te,de->td", grad_logits, router_weight, preferred_element_type=single_precision),
        grad_output[0],
        False,
    )
    grad_mid_norm, grad_ffn_gain = rms_backward(grad_ffn_in, normed2, factor2, ffn_gain)
    grad_mid = grad + grad_mid_norm
    grad_mid_b = grad_mid.astype(bf16)
    out_block = jnp.einsum(
        "td,tq->dq", grad_mid_b, attended, preferred_element_type=single_precision
    ).astype(bf16)
    grad_att = (
        jnp.einsum("td,dq->tq", grad_mid_b, out_full, preferred_element_type=single_precision)
        .astype(bf16)
        .reshape(seq_tok, heads, head_dim)
    )
    delta = jnp.sum(
        grad_att.astype(single_precision)
        * attended.reshape(seq_tok, heads, head_dim).astype(single_precision),
        axis=-1,
    )
    probs = jnp.exp(masked_scores() - lse)
    grad_vals = jnp.einsum(
        "hqk,qhd->khd", probs.astype(bf16), grad_att, preferred_element_type=single_precision
    )
    grad_p = jnp.einsum("qhd,khd->hqk", grad_att, vals3, preferred_element_type=single_precision)
    grad_scores = (probs * (grad_p - delta.T[:, :, None])).astype(bf16)
    grad_queries = (
        jnp.einsum("hqk,khd->qhd", grad_scores, keys3, preferred_element_type=single_precision)
        * scale
    )
    grad_keys_all = (
        jnp.einsum("hqk,qhd->khd", grad_scores, queries, preferred_element_type=single_precision)
        * scale
    )
    grad_values = sum_context_halves(grad_vals.reshape(seq_len, heads_width))
    grad_keys = sum_context_halves(grad_keys_all.reshape(seq_len, heads_width))
    grad_qn = rotate(grad_queries, cosine, sine, -1.0).reshape(seq_tok, heads_width)
    grad_kn = rotate(grad_keys.reshape(seq_tok, heads, head_dim), cosine, sine, -1.0).reshape(
        seq_tok, heads_width
    )
    grad_q_raw, grad_q_gain = rms_backward(grad_qn, q_normed, q_factor, q_gain)
    grad_k_raw, grad_k_gain = rms_backward(grad_kn, k_normed, k_factor, k_gain)
    projected_gradient = jnp.stack(
        [grad_q_raw, grad_k_raw, grad_values, jnp.zeros_like(grad_values)], axis=1
    ).astype(bf16)
    attention_input_gradient = jnp.dot(
        projected_gradient.reshape(seq_tok, 4 * heads_width),
        weights_full.reshape(width, 4 * heads_width).T,
        preferred_element_type=single_precision,
    )
    grad_x_norm, grad_attn_gain = rms_backward(
        attention_input_gradient, normed1, factor1, attn_gain
    )
    grad_tokens = grad_mid + grad_x_norm
    def scatter_over_copies(values):
        return sum_halves(sum_halves(values, "dp", 1), "context", 1)

    grad_in_shard = scatter_over_copies(grad_gate_up_w[0])[None]
    grad_down_shard = scatter_over_copies(grad_down[0])[None]
    qkv_stack = jnp.einsum(
        "ta,stb->sab",
        attention_input,
        projected_gradient[:, :3].transpose(1, 0, 2),
        preferred_element_type=single_precision,
    ).astype(bf16)
    qkv_sum, out_sum = lax.psum((qkv_stack, out_block), all_axes)
    shard_rows = width // lax.axis_size(all_axes)
    start = lax.axis_index(all_axes) * shard_rows
    grad_qkv_shard = lax.dynamic_slice_in_dim(qkv_sum, start, shard_rows, axis=1).astype(
        single_precision
    )
    grad_out_shard = lax.dynamic_slice_in_dim(out_sum, start, shard_rows, axis=0).astype(
        single_precision
    )
    small_sum = butterfly_sum(
        jnp.concatenate(
            [grad_attn_gain, grad_q_gain, grad_k_gain, grad_ffn_gain, grad_router.reshape(-1)]
        ),
        all_axes,
    )
    sizes = [width, heads_width, heads_width, width, width * experts]
    offsets = [sum(sizes[:n]) for n in range(len(sizes))]
    totals = [small_sum[o : o + n] for o, n in zip(offsets, sizes)]
    totals[4] = totals[4].reshape(width, experts)
    return (
        output[None],
        grad_tokens[None],
        totals[0],
        totals[1],
        totals[2],
        totals[3],
        totals[4],
        grad_qkv_shard,
        grad_out_shard,
        grad_in_shard,
        grad_down_shard,
    )


def solution(mesh):
    return jax.shard_map(
        body,
        mesh=mesh,
        in_specs=(
            P(("dp", "expert"), "context", None),
            P(("dp", "expert"), "context", None),
            P(("dp", "expert"), "context", None),
            P(("dp", "expert"), None),
            P(),
            P(),
            P(),
            P(),
            P(None, ("dp", "context", "expert"), None),
            P(("dp", "context", "expert"), None),
            P(),
            P("expert", None, None, None),
            P("expert", None, None),
        ),
        out_specs=(
            P(("dp", "expert"), "context", None),
            P(("dp", "expert"), "context", None),
            P(),
            P(),
            P(),
            P(),
            P(),
            P(None, ("dp", "context", "expert"), None),
            P(("dp", "context", "expert"), None),
            P("expert", None, ("dp", "context"), None),
            P("expert", None, ("dp", "context")),
        ),
        check_vma=False,
    )
```

```python
import functools

import jax
import jax.numpy as jnp
from jax import lax
from jax.experimental import pallas as pl
from jax.experimental.pallas import tpu as pltpu
from jax.sharding import PartitionSpec as P

HDIM = 128


EPS = 1e-05
THETA = 10000.0


def rope_tables(places, head_dim):
    half = head_dim // 2
    freq = THETA ** (-jnp.arange(half, dtype=jnp.float32) * 2.0 / head_dim)
    angle = places.astype(jnp.float32)[:, None] * freq[None, :]
    return (jnp.cos(angle), jnp.sin(angle))


def rotate(values, cosine, sine, sign):
    half = values.shape[-1] // 2
    first = values[..., :half]
    second = values[..., half:]
    cosine = cosine[:, None, :]
    sine = sign * sine[:, None, :]
    return jnp.concatenate(
        [first * cosine - second * sine, second * cosine + first * sine], axis=-1
    )


def rms_forward(values):
    factor = lax.rsqrt(jnp.mean(values * values, axis=-1, keepdims=True) + EPS)
    return (values * factor, factor)


def rms_backward(grad_out, normed, factor, gain):
    scaled = grad_out * gain
    grad_in = factor * (scaled - normed * jnp.mean(scaled * normed, axis=-1, keepdims=True))
    return (grad_in, jnp.sum(grad_out * normed, axis=0))


def slot_index(route_rows, experts, capacity):
    onehot = (route_rows[:, None] == jnp.arange(experts, dtype=jnp.int32)[None, :]).astype(
        jnp.int32
    )
    count = route_rows.shape[0]
    earlier = (
        jnp.arange(count, dtype=jnp.int32)[None, :] < jnp.arange(count, dtype=jnp.int32)[:, None]
    ).astype(jnp.bfloat16)
    before = jnp.dot(earlier, onehot.astype(jnp.bfloat16), preferred_element_type=jnp.float32)
    return route_rows * capacity + jnp.sum(before.astype(jnp.int32) * onehot, axis=1)


def expert_major(received, local_experts, capacity):
    sources, _, width = received.shape
    return (
        received.reshape(sources, local_experts, capacity, width)
        .transpose(1, 0, 2, 3)
        .reshape(local_experts, sources * capacity, width)
    )


def source_major(results, sources, capacity):
    local_experts, _, width = results.shape
    return (
        results.reshape(local_experts, sources, capacity, width)
        .transpose(1, 0, 2, 3)
        .reshape(sources, local_experts * capacity, width)
    )


def _project_kernel(inputs_ref, weights_ref, out_ref):
    out_ref[0] = jnp.dot(inputs_ref[...], weights_ref[0], preferred_element_type=jnp.float32)


def project(inputs, weights, blocks, tile=1024):
    tokens, depth = inputs.shape
    columns = weights.shape[2]
    return pl.pallas_call(
        _project_kernel,
        out_shape=jax.ShapeDtypeStruct((blocks, tokens, columns), jnp.float32),
        grid=(blocks, columns // tile),
        in_specs=[
            pl.BlockSpec((tokens, depth), lambda s, j: (0, 0)),
            pl.BlockSpec((1, depth, tile), lambda s, j: (s, 0, j)),
        ],
        out_specs=pl.BlockSpec((1, tokens, tile), lambda s, j: (s, 0, j)),
        cost_estimate=pl.CostEstimate(
            flops=2 * tokens * depth * columns * blocks,
            transcendentals=0,
            bytes_accessed=2 * depth * columns * blocks + 2 * tokens * depth
            + 4 * tokens * columns * blocks,
        ),
    )(inputs, weights)


def _dispatch_kernel(slot_ref, weight_ref, rows_ref, grad_ref, send_ref, grad_send_ref):
    tile = send_ref.shape[0]
    top, tokens = slot_ref.shape
    slot = pl.program_id(0) * tile + lax.broadcasted_iota(jnp.int32, (tile, tokens), 0)
    hit = slot == slot_ref[0:1, :]
    weight = jnp.where(hit, weight_ref[0:1, :], 0.0)
    for k in range(1, top):
        match = slot == slot_ref[k : k + 1, :]
        hit = hit | match
        weight = weight + jnp.where(match, weight_ref[k : k + 1, :], 0.0)
    pick = hit.astype(jnp.bfloat16)
    send_ref[...] = jnp.dot(pick, rows_ref[...], preferred_element_type=jnp.float32).astype(
        send_ref.dtype
    )
    picked_grad = jnp.dot(pick, grad_ref[...], preferred_element_type=jnp.float32)
    slot_weight = jnp.sum(weight, axis=1, keepdims=True)
    grad_send_ref[...] = (slot_weight * picked_grad).astype(grad_send_ref.dtype)


def dispatch(route_slots, route_weights, rows, grad, slots, tile=640):
    top, tokens = route_slots.shape
    width = rows.shape[1]
    out = jax.ShapeDtypeStruct((slots, width), jnp.bfloat16)
    return pl.pallas_call(
        _dispatch_kernel,
        out_shape=(out, out),
        grid=(slots // tile,),
        in_specs=[
            pl.BlockSpec((top, tokens), lambda i: (0, 0)),
            pl.BlockSpec((top, tokens), lambda i: (0, 0)),
            pl.BlockSpec((tokens, width), lambda i: (0, 0)),
            pl.BlockSpec((tokens, width), lambda i: (0, 0)),
        ],
        out_specs=(
            pl.BlockSpec((tile, width), lambda i: (i, 0)),
            pl.BlockSpec((tile, width), lambda i: (i, 0)),
        ),
        cost_estimate=pl.CostEstimate(
            flops=4 * slots * tokens * width,
            transcendentals=0,
            bytes_accessed=4 * slots * width + 4 * tokens * width + 8 * top * tokens,
        ),
    )(route_slots, route_weights, rows, grad)


def _combine_kernel(with_dots, slot_ref, weight_ref, table_ref, base_ref, other_ref, out_ref, dots_ref):
    tokens, top = slot_ref.shape
    count = table_ref.shape[0]
    column = lax.broadcasted_iota(jnp.int32, (tokens, count), 1)
    if not with_dots:
        hit = slot_ref[:, 0:1] == column
        for k in range(1, top):
            hit = hit | (slot_ref[:, k : k + 1] == column)
        out_ref[...] = base_ref[...] + jnp.dot(
            hit.astype(jnp.bfloat16), table_ref[...], preferred_element_type=jnp.float32
        )
        dots_ref[...] = jnp.zeros_like(dots_ref)
        return
    total = base_ref[...]
    for k in range(top):
        pick = (slot_ref[:, k : k + 1] == column).astype(jnp.bfloat16)
        row = jnp.dot(pick, table_ref[...], preferred_element_type=jnp.float32)
        total = total + weight_ref[:, k : k + 1] * row
        dots_ref[:, k : k + 1] = jnp.sum(
            other_ref[...].astype(jnp.float32) * row, axis=1, keepdims=True
        )
    out_ref[...] = total


def combine(slots, weights, table, base, other, with_dots):
    tokens, top = slots.shape
    count, width = table.shape
    return pl.pallas_call(
        functools.partial(_combine_kernel, with_dots),
        out_shape=(
            jax.ShapeDtypeStruct((tokens, width), jnp.float32),
            jax.ShapeDtypeStruct((tokens, top), jnp.float32),
        ),
        in_specs=[pl.BlockSpec(memory_space=pltpu.VMEM)] * 5,
        out_specs=(pl.BlockSpec(memory_space=pltpu.VMEM), pl.BlockSpec(memory_space=pltpu.VMEM)),
        cost_estimate=pl.CostEstimate(
            flops=2 * tokens * count * width * top,
            transcendentals=0,
            bytes_accessed=2 * count * width + 10 * tokens * width,
        ),
    )(slots, weights, table, base, other)


def _sum_rows_kernel(slot_ref, table_ref, base_ref, out_ref):
    tokens, top = slot_ref.shape
    chunk = table_ref.shape[0]
    column = pl.program_id(0) * chunk + lax.broadcasted_iota(jnp.int32, (tokens, chunk), 1)
    hit = slot_ref[:, 0:1] == column
    for k in range(1, top):
        hit = hit | (slot_ref[:, k : k + 1] == column)
    part = jnp.dot(hit.astype(jnp.bfloat16), table_ref[...], preferred_element_type=jnp.float32)

    @pl.when(pl.program_id(0) == 0)
    def _():
        out_ref[...] = base_ref[...]

    out_ref[...] += part


def sum_rows(slots, table, base, chunk=256):
    tokens, top = slots.shape
    count, width = table.shape
    return pl.pallas_call(
        _sum_rows_kernel,
        out_shape=jax.ShapeDtypeStruct((tokens, width), jnp.float32),
        grid=(count // chunk,),
        in_specs=[
            pl.BlockSpec((tokens, top), lambda i: (0, 0)),
            pl.BlockSpec((chunk, width), lambda i: (i, 0)),
            pl.BlockSpec((tokens, width), lambda i: (0, 0)),
        ],
        out_specs=pl.BlockSpec((tokens, width), lambda i: (0, 0)),
        cost_estimate=pl.CostEstimate(
            flops=2 * tokens * count * width,
            transcendentals=0,
            bytes_accessed=2 * count * width + 8 * tokens * width,
        ),
    )(slots, table, base)


def sum_halves(values, axis, dim):
    half = values.shape[dim] // 2
    index = lax.axis_index(axis)
    own = lax.dynamic_slice_in_dim(values, index * half, half, axis=dim)
    given = lax.dynamic_slice_in_dim(values, (1 - index) * half, half, axis=dim)
    received = lax.ppermute(given.astype(jnp.bfloat16), axis, [(0, 1), (1, 0)])
    return own + received.astype(own.dtype)


def swap_context(values):
    return lax.ppermute(values, "context", [(0, 1), (1, 0)])


def gather_context(values):
    other = swap_context(values)
    first = lax.axis_index("context") == 0
    return jnp.concatenate(
        [jnp.where(first, values, other), jnp.where(first, other, values)], axis=0
    )


def sum_context_halves(values):
    half = values.shape[0] // 2
    first = lax.axis_index("context") == 0
    own = jnp.where(first, values[:half], values[half:])
    given = jnp.where(first, values[half:], values[:half]).astype(jnp.bfloat16)
    return own + swap_context(given).astype(own.dtype)


def butterfly_sum(values, axes):
    index = lax.axis_index(axes)
    count = 1
    for name in axes:
        count *= lax.axis_size(name)
    step = 1
    while step < count:
        partner = [(i, i ^ step) for i in range(count)]
        received = lax.ppermute(values, axes, partner)
        mine_first = (index & step) == 0
        values = jnp.where(mine_first, values + received, received + values)
        step *= 2
    return values


def body(
    tokens,
    grad_output,
    routes,
    positions,
    attn_gain,
    q_gain,
    k_gain,
    ffn_gain,
    qkv_weight,
    out_weight,
    router_weight,
    expert_in,
    expert_out,
):
    single_precision = jnp.float32
    bf16 = jnp.bfloat16
    seq_tok = tokens.shape[1]
    width = tokens.shape[2]
    top = routes.shape[2]
    heads_width = out_weight.shape[1]
    head_dim = HDIM
    heads = heads_width // head_dim
    local_experts = expert_in.shape[0]
    experts = router_weight.shape[1]
    sources = lax.axis_size("expert")
    capacity = min(seq_tok, seq_tok * top * 5 // (4 * experts))
    scale = head_dim ** (-0.5)
    x = tokens[0].astype(single_precision)
    normed1, factor1 = rms_forward(x)
    attention_input = (normed1 * attn_gain).astype(bf16)
    all_axes = ("dp", "context", "expert")
    weights_full = lax.all_gather(
        jnp.concatenate([qkv_weight.transpose(1, 0, 2), out_weight[:, None, :]], axis=1),
        all_axes,
        axis=0,
        tiled=True,
    )
    out_full = weights_full[:, 3, :]
    both_inputs = gather_context(attention_input)
    projected_both = project(both_inputs, weights_full.transpose(1, 0, 2), 3)
    own_start = lax.axis_index("context") * seq_tok
    projected_output = lax.dynamic_slice_in_dim(projected_both, own_start, seq_tok, axis=1)
    q_normed, q_factor = rms_forward(projected_output[0])
    k_normed, k_factor = rms_forward(projected_output[1])
    all_places = positions[0]
    own_places = lax.dynamic_slice_in_dim(all_places, own_start, seq_tok)
    cosine, sine = rope_tables(own_places, head_dim)
    all_cosine, all_sine = rope_tables(all_places, head_dim)
    queries = rotate(
        (q_normed * q_gain).reshape(seq_tok, heads, head_dim), cosine, sine, 1.0
    ).astype(bf16)
    seq_len = both_inputs.shape[0]
    keys_normed, _ = rms_forward(projected_both[1])
    keys = rotate(
        (keys_normed * k_gain).reshape(seq_len, heads, head_dim), all_cosine, all_sine, 1.0
    ).astype(bf16)
    vals = projected_both[2].astype(bf16)
    keys3 = keys.reshape(seq_len, heads, head_dim)
    vals3 = vals.reshape(seq_len, heads, head_dim)
    allowed = (all_places[None, :] <= own_places[:, None])[None]

    def masked_scores():
        scores = (
            jnp.einsum("qhd,khd->hqk", queries, keys3, preferred_element_type=single_precision)
            * scale
        )
        return jnp.where(allowed, scores, -jnp.inf)

    scores = masked_scores()
    lse = jnp.log(jnp.sum(jnp.exp(scores), axis=-1, keepdims=True))
    probs_b = jnp.exp(scores - lse).astype(bf16)
    attended = (
        jnp.einsum("hqk,khd->qhd", probs_b, vals3, preferred_element_type=single_precision)
        .astype(bf16)
        .reshape(seq_tok, heads_width)
    )
    mid = x + jnp.einsum("tq,dq->td", attended, out_full, preferred_element_type=single_precision)
    normed2, factor2 = rms_forward(mid)
    ffn_in = (normed2 * ffn_gain).astype(bf16)
    router_exp = jnp.exp(jnp.dot(ffn_in, router_weight, preferred_element_type=single_precision))
    router_probs = router_exp / jnp.sum(router_exp, axis=-1, keepdims=True)
    own_routes = routes[0]
    slots = slot_index(own_routes.reshape(-1), experts, capacity)
    expert_ids = jnp.arange(experts, dtype=jnp.int32)
    route_weight = jnp.sum(
        jnp.where(own_routes[:, :, None] == expert_ids, router_probs[:, None, :], 0.0), axis=2
    )
    route_slots = slots.reshape(seq_tok, top)
    send, grad_send = dispatch(
        route_slots.T, route_weight.T, ffn_in, grad_output[0], experts * capacity
    )
    received = lax.all_to_all(
        send.reshape(sources, local_experts * capacity, width),
        "expert",
        split_axis=0,
        concat_axis=0,
        tiled=True,
    )
    rows = expert_major(received, local_experts, capacity)
    gate_up = jnp.einsum("lrd,lkdh->lkrh", rows, expert_in, preferred_element_type=single_precision)
    gate = gate_up[:, 0]
    up = gate_up[:, 1]
    sig = jax.nn.sigmoid(gate)
    hidden = (gate * sig * up).astype(bf16)
    results = jnp.einsum(
        "lrh,lhd->lrd", hidden, expert_out, preferred_element_type=single_precision
    ).astype(bf16)
    back = lax.all_to_all(
        source_major(results, sources, capacity), "expert", split_axis=0, concat_axis=0, tiled=True
    )
    output, route_grad_weight = combine(
        route_slots,
        route_weight,
        back.reshape(experts * capacity, width),
        mid,
        grad_output[0],
        True,
    )
    grad = grad_output[0].astype(single_precision)
    grad_received = lax.all_to_all(
        grad_send.reshape(sources, local_experts * capacity, width),
        "expert",
        split_axis=0,
        concat_axis=0,
        tiled=True,
    )
    grad_rows = expert_major(grad_received, local_experts, capacity)
    grad_hidden = jnp.einsum(
        "lrd,lhd->lrh", grad_rows, expert_out, preferred_element_type=single_precision
    )
    grad_down = jnp.einsum(
        "lrh,lrd->lhd", hidden, grad_rows, preferred_element_type=single_precision
    )
    grad_gate = (grad_hidden * up * sig * (1.0 + gate * (1.0 - sig))).astype(bf16)
    grad_up = (grad_hidden * gate * sig).astype(bf16)
    grad_gate_up = jnp.stack([grad_gate, grad_up], axis=1)
    grad_gate_up_w = jnp.einsum(
        "lrd,lkrh->lkdh", rows, grad_gate_up, preferred_element_type=single_precision
    )
    grad_rows_in = jnp.einsum(
        "lkrh,lkdh->lrd", grad_gate_up, expert_in, preferred_element_type=single_precision
    ).astype(bf16)
    grad_back = lax.all_to_all(
        source_major(grad_rows_in, sources, capacity),
        "expert",
        split_axis=0,
        concat_axis=0,
        tiled=True,
    )
    chosen = (own_routes[:, :, None] == jnp.arange(experts, dtype=jnp.int32)[None, None, :]).astype(
        single_precision
    )
    grad_probs = jnp.sum(route_grad_weight[:, :, None] * chosen, axis=1)
    grad_logits = (
        router_probs * (grad_probs - jnp.sum(router_probs * grad_probs, axis=-1, keepdims=True))
    ).astype(bf16)
    grad_router = jnp.einsum(
        "td,te->de", ffn_in, grad_logits, preferred_element_type=single_precision
    )
    grad_ffn_in = sum_rows(
        route_slots,
        grad_back.reshape(experts * capacity, width),
        jnp.einsum("te,de->td", grad_logits, router_weight, preferred_element_type=single_precision),
    )
    grad_mid_norm, grad_ffn_gain = rms_backward(grad_ffn_in, normed2, factor2, ffn_gain)
    grad_mid = grad + grad_mid_norm
    grad_mid_b = grad_mid.astype(bf16)
    grad_att = (
        jnp.einsum("td,dq->tq", grad_mid_b, out_full, preferred_element_type=single_precision)
        .astype(bf16)
        .reshape(seq_tok, heads, head_dim)
    )
    delta = jnp.sum(
        grad_att.astype(single_precision)
        * attended.reshape(seq_tok, heads, head_dim).astype(single_precision),
        axis=-1,
    )
    probs = jnp.exp(masked_scores() - lse)
    grad_vals = jnp.einsum(
        "hqk,qhd->khd", probs.astype(bf16), grad_att, preferred_element_type=single_precision
    )
    grad_p = jnp.einsum("qhd,khd->hqk", grad_att, vals3, preferred_element_type=single_precision)
    grad_scores = (probs * (grad_p - delta.T[:, :, None])).astype(bf16)
    grad_queries = (
        jnp.einsum("hqk,khd->qhd", grad_scores, keys3, preferred_element_type=single_precision)
        * scale
    )
    grad_keys_all = (
        jnp.einsum("hqk,qhd->khd", grad_scores, queries, preferred_element_type=single_precision)
        * scale
    )
    grad_values = sum_context_halves(grad_vals.reshape(seq_len, heads_width))
    grad_keys = sum_context_halves(grad_keys_all.reshape(seq_len, heads_width))
    grad_qn = rotate(grad_queries, cosine, sine, -1.0).reshape(seq_tok, heads_width)
    grad_kn = rotate(grad_keys.reshape(seq_tok, heads, head_dim), cosine, sine, -1.0).reshape(
        seq_tok, heads_width
    )
    grad_q_raw, grad_q_gain = rms_backward(grad_qn, q_normed, q_factor, q_gain)
    grad_k_raw, grad_k_gain = rms_backward(grad_kn, k_normed, k_factor, k_gain)
    projected_gradient = jnp.stack(
        [grad_q_raw, grad_k_raw, grad_values, jnp.zeros_like(grad_values)], axis=1
    ).astype(bf16)
    attention_input_gradient = jnp.dot(
        projected_gradient.reshape(seq_tok, 4 * heads_width),
        weights_full.reshape(width, 4 * heads_width).T,
        preferred_element_type=single_precision,
    )
    grad_x_norm, grad_attn_gain = rms_backward(
        attention_input_gradient, normed1, factor1, attn_gain
    )
    grad_tokens = grad_mid + grad_x_norm
    def scatter_over_copies(values):
        return sum_halves(sum_halves(values, "dp", 1), "context", 1)

    grad_in_shard = scatter_over_copies(grad_gate_up_w[0])[None]
    grad_down_shard = scatter_over_copies(grad_down[0])[None]
    left = jnp.stack([attention_input] * 3 + [grad_mid_b])
    right = jnp.concatenate(
        [projected_gradient[:, :3].transpose(1, 0, 2), attended[None]], axis=0
    )
    stacked = jnp.einsum("sta,stb->sab", left, right, preferred_element_type=single_precision)
    summed = lax.psum(stacked.astype(bf16), all_axes)
    shard_rows = width // lax.axis_size(all_axes)
    start = lax.axis_index(all_axes) * shard_rows
    weight_shard = lax.dynamic_slice_in_dim(summed, start, shard_rows, axis=1).astype(
        single_precision
    )
    grad_qkv_shard = weight_shard[:3]
    grad_out_shard = weight_shard[3]
    small_sum = butterfly_sum(
        jnp.concatenate(
            [grad_attn_gain, grad_q_gain, grad_k_gain, grad_ffn_gain, grad_router.reshape(-1)]
        ),
        all_axes,
    )
    sizes = [width, heads_width, heads_width, width, width * experts]
    offsets = [sum(sizes[:n]) for n in range(len(sizes))]
    totals = [small_sum[o : o + n] for o, n in zip(offsets, sizes)]
    totals[4] = totals[4].reshape(width, experts)
    return (
        output[None],
        grad_tokens[None],
        totals[0],
        totals[1],
        totals[2],
        totals[3],
        totals[4],
        grad_qkv_shard,
        grad_out_shard,
        grad_in_shard,
        grad_down_shard,
    )


def solution(mesh):
    return jax.shard_map(
        body,
        mesh=mesh,
        in_specs=(
            P(("dp", "expert"), "context", None),
            P(("dp", "expert"), "context", None),
            P(("dp", "expert"), "context", None),
            P(("dp", "expert"), None),
            P(),
            P(),
            P(),
            P(),
            P(None, ("dp", "context", "expert"), None),
            P(("dp", "context", "expert"), None),
            P(),
            P("expert", None, None, None),
            P("expert", None, None),
        ),
        out_specs=(
            P(("dp", "expert"), "context", None),
            P(("dp", "expert"), "context", None),
            P(),
            P(),
            P(),
            P(),
            P(),
            P(None, ("dp", "context", "expert"), None),
            P(("dp", "context", "expert"), None),
            P("expert", None, ("dp", "context"), None),
            P("expert", None, ("dp", "context")),
        ),
        check_vma=False,
    )
```
